32 devices in a mesh: rows: 8 (over z, y), heads: 4 (over x, core).
Axes of the slice: x: 2, y: 2, z: 4, core: 2. Of those that a mesh axis runs over, the one named last changes fastest.
Arguments:
- inputs: bfloat16 [8, 1024, 768], P('rows', 'heads'), may hold values from -6 to 6
- encoded: bfloat16 [8, 1024, 768], P('rows', 'heads'), may hold values from -6 to 6
- cotangent: bfloat16 [8, 1024, 768], P('rows', 'heads'), may hold values from -6 to 6
- dec_lengths: int32 [8, 8], P('rows'), may hold values from 96 to 128, as said below
- enc_lengths: int32 [8, 8], P('rows'), may hold values from 96 to 128, as said below
- self_query: bfloat16 [768, 768], P('rows', 'heads'), may hold values from -0.0546875 to 0.0546875
- self_key: bfloat16 [768, 768], P('rows', 'heads'), may hold values from -0.21875 to 0.21875
- self_value: bfloat16 [768, 768], P('rows', 'heads'), may hold values from -0.21875 to 0.21875
- self_output: bfloat16 [768, 768], P('heads', 'rows'), may hold values from -0.875 to 0.875
- cross_query: bfloat16 [768, 768], P('rows', 'heads'), may hold values from -0.0546875 to 0.0546875
- cross_key: bfloat16 [768, 768], P('rows', 'heads'), may hold values from -0.21875 to 0.21875
- cross_value: bfloat16 [768, 768], P('rows', 'heads'), may hold values from -0.21875 to 0.21875
- cross_output: bfloat16 [768, 768], P('heads', 'rows'), may hold values from -0.875 to 0.875
- inner_weight: bfloat16 [768, 3072], P('rows', 'heads'), may hold values from -0.21875 to 0.21875
- outer_weight: bfloat16 [3072, 768], P('heads', 'rows'), may hold values from -0.15625 to 0.15625
- bias_table: bfloat16 [32, 12], P(None, 'heads'), may hold values from -4 to 4
- gain_first: bfloat16 [768], P(('rows', 'heads')), may hold values from 0.25 to 1.75
- gain_second: bfloat16 [768], P(('rows', 'heads')), may hold values from 0.25 to 1.75
- gain_third: bfloat16 [768], P(('rows', 'heads')), may hold values from 0.25 to 1.75
Outputs:
- layer_out: bfloat16 [8, 1024, 768], P('rows', 'heads')
- input_grad: float32 [8, 1024, 768], P('rows', 'heads')
- encoded_grad: float32 [8, 1024, 768], P('rows', 'heads')
- self_query_grad: float32 [768, 768], P('rows', 'heads')
- self_key_grad: float32 [768, 768], P('rows', 'heads')
- self_value_grad: float32 [768, 768], P('rows', 'heads')
- self_output_grad: float32 [768, 768], P('heads', 'rows')
- cross_query_grad: float32 [768, 768], P('rows', 'heads')
- cross_key_grad: float32 [768, 768], P('rows', 'heads')
- cross_value_grad: float32 [768, 768], P('rows', 'heads')
- cross_output_grad: float32 [768, 768], P('heads', 'rows')
- inner_grad: float32 [768, 3072], P('rows', 'heads')
- outer_grad: float32 [3072, 768], P('heads', 'rows')
- bias_table_grad: float32 [32, 12], P(None, 'heads')
- gain_first_grad: float32 [768], P(('rows', 'heads'))
- gain_second_grad: float32 [768], P(('rows', 'heads'))
- gain_third_grad: float32 [768], P(('rows', 'heads'))
The draws below stay inside these ranges and needn't reach their ends.
Inputs may be any that keep to these rules, and one draw needn't show every extreme that they name: `dec_lengths`: A row's comments occupy its first tokens in order and the rest is padding; some comment has exactly 128 tokens. `enc_lengths`: entry c is the encoder token count of the code input of comment c; these occupy a row's first encoder tokens in order and the rest is padding; some entry is exactly 128.
All inputs are finite; a program needn't handle non-finite values.
Results may differ from the reference program's by a relative error of at most 0.028.
The reference program's roundings to bfloat16 on the way count: a program that leaves them out, or rounds other values in their place, can miss the bound.
Values may be sent and summed in bfloat16 or wider, within the bound.
No kernel may reach another device: no remote copies, remote signals or barrier semaphores. Data moves between devices by JAX's collectives and lax.ppermute only.
A program may use at most 256 MiB of HBM per device.

```python
import math
import jax
import jax.numpy as jnp
import numpy as np
from jax import lax

D = 768
HEADS = 12
HEAD_DIM = 64
FF = 3072
BUCKETS = 32
MAX_DISTANCE = 128
LEN = 1024
ENC_LEN = 1024
COMMENTS = 8
DEC_MOST = 128
ENC_MOST = 128
INNER = 768
ROWS = 8


def comment_lengths(key, salt_value, longest):
    base_key = jax.random.fold_in(key, salt_value)
    lengths = jax.random.randint(base_key, (ROWS, COMMENTS), longest - longest // 4, longest + 1, dtype=jnp.int32)
    chosen_slot = jax.random.randint(jax.random.fold_in(base_key, 11), (), 0, ROWS * COMMENTS, dtype=jnp.int32)
    flat_lengths = jnp.where(jnp.arange(ROWS * COMMENTS, dtype=jnp.int32) == chosen_slot, longest, lengths.reshape(-1))
    return flat_lengths.reshape(ROWS, COMMENTS).astype(jnp.int32)


def draw_dec_lengths(key, part):
    return comment_lengths(key, 1, DEC_MOST)


def draw_enc_lengths(key, part):
    return comment_lengths(key, 2, ENC_MOST)


def level_of(stream_key, dims, shards, smallest, top_value):
    level = 1.0
    for dim, shards_of in shards:
        steps = jax.random.uniform(jax.random.fold_in(jax.random.fold_in(stream_key, 6), dim), (shards_of,), jnp.float32, smallest / len(shards), top_value / len(shards))
        level = level * jnp.repeat(jnp.exp(steps), dims[dim] // shards_of).reshape((-1,) + (1,) * (len(dims) - 1 - dim))
    return level


def centred(stream_key, shape, width, reach, split=(), held_as=jnp.bfloat16):
    entries = width * jax.random.normal(stream_key, shape, jnp.float32)
    if split:
        entries = entries * level_of(stream_key, shape, split, -0.22, 0.18)
    return jnp.clip(entries, -reach, reach).astype(held_as)


def setup_inputs(seed: int = 0) -> dict:
    seeds = jax.random.split(jax.random.key(seed), 20)
    inputs = centred(seeds[0], (ROWS, LEN, D), 1.0, 6.0, ((0, 8), (1, 4)))
    encoded = centred(seeds[1], (ROWS, ENC_LEN, D), 1.0, 6.0, ((0, 8), (1, 4)))
    cotangent = centred(seeds[2], (ROWS, LEN, D), 1.0, 6.0, ((0, 8), (1, 4)))
    dec_lengths = draw_dec_lengths(jax.random.fold_in(seeds[19], 71), 0)
    enc_lengths = draw_enc_lengths(jax.random.fold_in(seeds[19], 71), 0)
    self_query = centred(seeds[5], (D, INNER), (D * 16) ** -0.5, 0.0546875, ((0, 8), (1, 4)))
    self_key = centred(seeds[6], (D, INNER), D ** -0.5, 0.21875, ((0, 8), (1, 4)))
    self_value = centred(seeds[7], (D, INNER), D ** -0.5, 0.21875, ((0, 8), (1, 4)))
    self_output = centred(seeds[8], (INNER, D), (D // 16) ** -0.5, 0.875, ((0, 4), (1, 8)))
    cross_query = centred(seeds[9], (D, INNER), (D * 16) ** -0.5, 0.0546875, ((0, 8), (1, 4)))
    cross_key = centred(seeds[10], (D, INNER), D ** -0.5, 0.21875, ((0, 8), (1, 4)))
    cross_value = centred(seeds[11], (D, INNER), D ** -0.5, 0.21875, ((0, 8), (1, 4)))
    cross_output = centred(seeds[12], (INNER, D), (D // 16) ** -0.5, 0.875, ((0, 4), (1, 8)))
    inner_weight = centred(seeds[13], (D, FF), D ** -0.5, 0.21875, ((0, 8), (1, 4)))
    outer_weight = centred(seeds[14], (FF, D), (FF // 2) ** -0.5, 0.15625, ((0, 4), (1, 8)))
    bias_table = centred(seeds[15], (BUCKETS, HEADS), 1.0, 4.0, ((1, 4),))
    gain_first = jnp.clip(1.0 + 0.15 * jax.random.normal(seeds[16], (D,), jnp.float32), 0.25, 1.75).astype(jnp.bfloat16)
    gain_second = jnp.clip(1.0 + 0.15 * jax.random.normal(seeds[17], (D,), jnp.float32), 0.25, 1.75).astype(jnp.bfloat16)
    gain_third = jnp.clip(1.0 + 0.15 * jax.random.normal(seeds[18], (D,), jnp.float32), 0.25, 1.75).astype(jnp.bfloat16)
    return {"inputs": inputs, "encoded": encoded, "cotangent": cotangent, "dec_lengths": dec_lengths, "enc_lengths": enc_lengths, "self_query": self_query, "self_key": self_key, "self_value": self_value, "self_output": self_output, "cross_query": cross_query, "cross_key": cross_key, "cross_value": cross_value, "cross_output": cross_output, "inner_weight": inner_weight, "outer_weight": outer_weight, "bias_table": bias_table, "gain_first": gain_first, "gain_second": gain_second, "gain_third": gain_third}


EPS = 1e-06
NEG = -1000000000.0
HIGHEST = lax.Precision.HIGHEST

@jax.custom_vjp
def low(v):
    return lax.optimization_barrier(v.astype(jnp.bfloat16)).astype(jnp.float32)

@jax.custom_vjp
def low_back(v):
    return v

def low_keep(v):
    return (low(v), None)

def low_pass(kept, grad):
    return (grad,)

def back_keep(v):
    return (v, None)

def back_low(kept, grad):
    return (low(grad),)
low.defvjp(low_keep, low_pass)
low_back.defvjp(back_keep, back_low)

def rounded_both(value):
    return low(low_back(value))

def smooth_unit(values):
    return jax.nn.gelu(values, approximate=False)

def bucket_edges(bucket_count, max_reach):
    exact_span = bucket_count // 2
    boundaries = []
    for target in range(exact_span + 1, bucket_count):
        distance = exact_span
        while distance < max_reach and exact_span + int(np.log(distance / exact_span) / np.log(max_reach / exact_span) * (bucket_count - exact_span)) < target:
            distance += 1
        boundaries.append(distance)
    return boundaries

def bucket_of(distance):
    distance = jnp.maximum(distance.astype(jnp.int32), jnp.zeros((), jnp.int32)).astype(jnp.int32)
    result = jnp.minimum(distance, jnp.full((), BUCKETS // 2, jnp.int32)).astype(jnp.int32)
    for boundary in bucket_edges(BUCKETS, MAX_DISTANCE):
        result = (result + (distance >= jnp.full((), boundary, jnp.int32)).astype(jnp.int32)).astype(jnp.int32)
    return result.astype(jnp.int32)

def segment_ids(lengths, total):
    segment_ends = jnp.cumsum(lengths.astype(jnp.int32), axis=-1).astype(jnp.int32)
    positions = jnp.arange(total, dtype=jnp.int32)
    above = (positions[None, :, None] >= segment_ends[:, None, :]).astype(jnp.int32)
    return lax.optimization_barrier(jnp.sum(above, axis=-1)).astype(jnp.int32)

def rms_norm(values, norm_gain):
    factor = lax.rsqrt(lax.optimization_barrier(jnp.mean(values * values, axis=-1, keepdims=True)) + EPS)
    return values * factor * norm_gain

def attend(queries, key_rows, values, position_bias, allowed):
    scores = jnp.einsum('gqhd,gkhd->ghqk', queries, key_rows, precision=HIGHEST) + position_bias
    scores = jnp.where(allowed[:, None], low_back(scores), NEG)
    largest = lax.optimization_barrier(jnp.max(scores, axis=-1, keepdims=True))
    totals = largest + jnp.log(lax.optimization_barrier(jnp.sum(jnp.exp(scores - largest), axis=-1, keepdims=True)))
    attention = low(jnp.exp(scores - totals))
    return jnp.einsum('ghqk,gkhd->gqhd', attention, values, precision=HIGHEST)

def layer(inputs, encoded, dec_lengths, enc_lengths, weights):
    self_query, self_key, self_value, self_output, cross_query, cross_key, cross_value, cross_output, inner_weight, outer_weight, bias_table, gain_first, gain_second, gain_third = weights
    groups = inputs.shape[0]
    length = inputs.shape[1]
    dec_seg = segment_ids(dec_lengths, length)
    enc_seg = segment_ids(enc_lengths, encoded.shape[1])
    positions = jnp.arange(length, dtype=jnp.int32)
    causal = positions[None, :] <= positions[:, None]
    comment_mark = jnp.full((), COMMENTS, jnp.int32)
    self_allowed = (dec_seg[:, :, None] == dec_seg[:, None, :]) & causal[None]
    cross_allowed = (dec_seg[:, :, None] == enc_seg[:, None, :]) | (dec_seg[:, :, None] == comment_mark)
    buckets = bucket_of((positions[:, None] - positions[None, :]).astype(jnp.int32))
    one_hot = (buckets[:, :, None] == jnp.arange(BUCKETS, dtype=jnp.int32)[None, None, :]).astype(jnp.float32).astype(bias_table.dtype)
    position_bias = jnp.einsum('qkb,bh->hqk', one_hot, bias_table, precision=HIGHEST)[None]

    def project(values, matrix):
        product = jnp.einsum('gtd,de->gte', values, matrix, precision=HIGHEST)
        return rounded_both(product).reshape(values.shape[0], values.shape[1], HEADS, HEAD_DIM)
    norm_one = low(rms_norm(inputs, gain_first))
    context_one = attend(project(norm_one, self_query), project(norm_one, self_key), project(norm_one, self_value), position_bias, self_allowed)
    context_one = rounded_both(context_one.reshape(groups, length, INNER))
    after_self = inputs + low_back(jnp.einsum('gte,ed->gtd', context_one, self_output, precision=HIGHEST))
    norm_two = low(rms_norm(after_self, gain_second))
    context_two = attend(project(norm_two, cross_query), project(encoded, cross_key), project(encoded, cross_value), 0.0, cross_allowed)
    context_two = rounded_both(context_two.reshape(groups, length, INNER))
    second = after_self + low_back(jnp.einsum('gte,ed->gtd', context_two, cross_output, precision=HIGHEST))
    norm_three = low(rms_norm(second, gain_third))
    active = low_back(jnp.einsum('gtd,df->gtf', norm_three, inner_weight, precision=HIGHEST))
    hidden = low(smooth_unit(active))
    return second + jnp.einsum('gtf,fd->gtd', hidden, outer_weight, precision=HIGHEST)

def reference(inputs, encoded, cotangent, dec_lengths, enc_lengths, self_query, self_key, self_value, self_output, cross_query, cross_key, cross_value, cross_output, inner_weight, outer_weight, bias_table, gain_first, gain_second, gain_third):
    weights = tuple((argument.astype(jnp.float32) for argument in (self_query, self_key, self_value, self_output, cross_query, cross_key, cross_value, cross_output, inner_weight, outer_weight, bias_table, gain_first, gain_second, gain_third)))
    group_rows = math.gcd(ROWS, max(1, 4096 // LEN))
    blocks = ROWS // group_rows
    dec_blocks = dec_lengths.astype(jnp.int32).reshape(blocks, group_rows, COMMENTS)
    enc_blocks = enc_lengths.astype(jnp.int32).reshape(blocks, group_rows, COMMENTS)

    def forward(inputs_value, encoded_value, weights_value):

        def one_group(pieces):
            return layer(pieces[0], pieces[1], pieces[2], pieces[3], weights_value)
        stacked = (inputs_value.reshape(blocks, group_rows, LEN, D), encoded_value.reshape(blocks, group_rows, ENC_LEN, D), dec_blocks, enc_blocks)
        return lax.map(jax.checkpoint(one_group), stacked).reshape(ROWS, LEN, D)
    outputs, pullback = jax.vjp(forward, inputs.astype(jnp.float32), encoded.astype(jnp.float32), weights)
    grad_inputs, grad_encoded, gradients = pullback(cotangent.astype(jnp.float32))
    return (outputs.astype(jnp.bfloat16), grad_inputs, grad_encoded, gradients[0], gradients[1], gradients[2], gradients[3], gradients[4], gradients[5], gradients[6], gradients[7], gradients[8], gradients[9], gradients[10], gradients[11], gradients[12], gradients[13])
```

```python
import functools

import jax
import jax.numpy as jnp
import numpy as np
from jax import lax
from jax.experimental import pallas as pl
from jax.experimental.pallas import tpu as pltpu
from jax.sharding import PartitionSpec as P

MAX_DISTANCE = 128
EPS = 1e-06
NEG = -1000000000.0
LEAST = 96
MOST = 128
BLOCK = 128
BF = jnp.bfloat16
F32 = jnp.float32
VMEM = pl.BlockSpec(memory_space=pltpu.VMEM)
SMEM = pl.BlockSpec(memory_space=pltpu.SMEM)
PARAMS = pltpu.CompilerParams(vmem_limit_bytes=48 << 20)


def bucket_starts(bucket_count, max_reach):
    exact_span = bucket_count // 2
    starts = list(range(exact_span + 1))
    for target in range(exact_span + 1, bucket_count):
        distance = exact_span
        while (
            distance < max_reach
            and exact_span
            + int(
                np.log(distance / exact_span)
                / np.log(max_reach / exact_span)
                * (bucket_count - exact_span)
            )
            < target
        ):
            distance += 1
        starts.append(distance)
    return starts


def send(part, axis, bits):
    count = lax.axis_size(axis)
    return lax.ppermute(part, axis, [(i, i ^ bits) for i in range(count)])


def gather_heads(part):
    across = send(part, "heads", 2)
    return [part, send(part, "heads", 1), across, send(across, "heads", 1)]


def scatter_heads(parts):
    far = send(parts[3].astype(BF), "heads", 1)
    near = send(parts[1].astype(BF), "heads", 1)
    across = send((parts[2] + far.astype(F32)).astype(BF), "heads", 2)
    return parts[0].astype(F32) + near.astype(F32) + across.astype(F32)


def place_kernel(count, axis, *refs):
    out = refs[count]
    me = lax.axis_index(axis)
    for t in range(count):
        out[me ^ t] = refs[t][...]


def place(pieces, axis):
    count = len(pieces)
    shape = (count,) + pieces[0].shape
    return pl.pallas_call(
        functools.partial(place_kernel, count, axis),
        out_shape=jax.ShapeDtypeStruct(shape, pieces[0].dtype),
        in_specs=[VMEM] * count,
        out_specs=VMEM,
        compiler_params=PARAMS,
        name="place",
    )(*pieces)


def gather_rows(part):
    pieces = []
    for upper in range(lax.axis_size("rows") // 2):
        near = part if upper == 0 else send(part, "rows", 2 * upper)
        pieces += [near, send(near, "rows", 1)]
    placed = place(pieces, "rows")
    return placed.reshape(-1, part.shape[1])


def scatter_rows(partial):
    count = lax.axis_size("rows")
    me = lax.axis_index("rows")
    upper, lower = me // 2, me % 2
    rows_each = partial.shape[0] // count
    view = partial.reshape(count // 2, 2, rows_each, partial.shape[1])
    pick = functools.partial(lax.dynamic_index_in_dim, keepdims=False)
    got = send(pick(view, 1 - lower, 1), "rows", 1)
    half = pick(view, lower, 1).astype(F32) + got.astype(F32)
    total = pick(half, upper, 0)
    sent = half.astype(BF)
    for k in range(1, count // 2):
        total = total + send(pick(sent, upper ^ k, 0), "rows", 2 * k).astype(F32)
    return total


def dot(a, b, dims):
    return lax.dot_general(a, b, (dims, ((), ())), preferred_element_type=F32)


NT = ((1,), (1,))
NN = ((1,), (0,))
TN = ((0,), (0,))


def distances(first, rows):
    query = lax.broadcasted_iota(jnp.int32, (rows, 2 * BLOCK), 0) + (first + BLOCK)
    return query - lax.broadcasted_iota(jnp.int32, (rows, 2 * BLOCK), 1)


def bias_kernel(starts, table_ref, out_ref):
    heads = out_ref.shape[0]
    step = 32

    def rows(t, carry):
        first = pl.multiple_of(t * step, step)
        reach = distances(first, step)
        values = [jnp.full((step, 2 * BLOCK), table_ref[0, h], F32) for h in range(heads)]
        for b in range(1, len(starts)):
            beyond = reach >= starts[b]
            values = [jnp.where(beyond, table_ref[b, h], values[h]) for h in range(heads)]
        for h in range(heads):
            out_ref[h, pl.ds(first, step), :] = values[h]
        return carry

    lax.fori_loop(0, BLOCK // step, rows, 0)


def bias_grad_kernel(starts, acc_ref, out_ref):
    heads = acc_ref.shape[0]
    reach = distances(0, BLOCK)
    ends = list(starts[1:]) + [1 << 20]
    for b in range(len(starts)):
        low = reach >= starts[b] if b else reach < starts[1]
        inside = low & (reach < ends[b]) if b else low
        for h in range(heads):
            out_ref[h, b : b + 1, :] = jnp.sum(
                jnp.where(inside, acc_ref[h], 0.0), axis=0, keepdims=True
            )


def running(lengths_ref, count):
    total = lengths_ref[0, 0]
    ends = [total]
    for c in range(1, count):
        total = total + lengths_ref[0, c]
        ends.append(total)
    return ends


def place_of(block, me, quarter):
    each = quarter // BLOCK
    return pl.multiple_of((((block // each) ^ me) * each + block % each) * BLOCK, BLOCK)


def self_forward_kernel(quarter, size, lengths_ref, qkv_ref, bias_ref, context_ref, probs_ref):
    heads = bias_ref.shape[0]
    width = heads * size
    me = lax.axis_index("heads")
    ends = running(lengths_ref, lengths_ref.shape[1])

    def block(b, carry):
        own = place_of(b, me, quarter)
        before = place_of(jnp.maximum(b - 1, 0), me, quarter)
        query = b * BLOCK + lax.broadcasted_iota(jnp.int32, (BLOCK, 1), 0)
        start = jnp.zeros((BLOCK, 1), jnp.int32)
        for end in ends:
            start = jnp.where(query >= end, end, start)
        key = (b - 1) * BLOCK + lax.broadcasted_iota(jnp.int32, (BLOCK, 2 * BLOCK), 1)
        allowed = (key >= start) & (key <= query)
        outs = []
        for h in range(heads):
            q = qkv_ref[pl.ds(own, BLOCK), h * size : (h + 1) * size]
            at = width + h * size
            k = jnp.concatenate(
                [qkv_ref[pl.ds(o, BLOCK), at : at + size] for o in (before, own)], 0
            )
            v = jnp.concatenate(
                [qkv_ref[pl.ds(o, BLOCK), at + width : at + width + size] for o in (before, own)],
                0,
            )
            scores = jnp.where(allowed, dot(q, k, NT) + bias_ref[h], NEG)
            top = jnp.max(scores, axis=-1, keepdims=True)
            e = jnp.exp(scores - top)
            probs = (e * (1.0 / jnp.sum(e, axis=-1, keepdims=True))).astype(BF)
            probs_ref[b, h] = probs
            outs.append(dot(probs, v, NN).astype(BF))
        context_ref[pl.ds(own, BLOCK), :] = jnp.concatenate(outs, 1)
        return carry

    lax.fori_loop(0, qkv_ref.shape[0] // BLOCK, block, 0)


def self_backward_kernel(
    quarter, size, qkv_ref, probs_ref, grad_ref, out_ref, bias_acc_ref, key_acc
):
    heads = bias_acc_ref.shape[0]
    width = heads * size
    me = lax.axis_index("heads")
    key_acc[...] = jnp.zeros_like(key_acc)
    bias_acc_ref[...] = jnp.zeros_like(bias_acc_ref)

    def block(b, carry):
        own = place_of(b, me, quarter)
        before = place_of(jnp.maximum(b - 1, 0), me, quarter)
        grads_q, grads_kv = [], []
        for h in range(heads):
            q = qkv_ref[pl.ds(own, BLOCK), h * size : (h + 1) * size]
            at = width + h * size
            k = jnp.concatenate(
                [qkv_ref[pl.ds(o, BLOCK), at : at + size] for o in (before, own)], 0
            )
            v = jnp.concatenate(
                [qkv_ref[pl.ds(o, BLOCK), at + width : at + width + size] for o in (before, own)],
                0,
            )
            c = grad_ref[pl.ds(own, BLOCK), h * size : (h + 1) * size]
            probs = probs_ref[b, h]
            wide = probs.astype(F32)
            grad_probs = dot(c, v, NT)
            inner = jnp.sum(grad_probs * wide, axis=-1, keepdims=True)
            grad_scores = wide * (grad_probs - inner)
            bias_acc_ref[h] += grad_scores
            short = grad_scores.astype(BF)
            grads_q.append(dot(short, k, NN).astype(BF))
            grads_kv.append((dot(short, q, TN), dot(probs, c, TN)))
        out_ref[pl.ds(own, BLOCK), :width] = jnp.concatenate(grads_q, 1)
        both = jnp.concatenate([g[0] for g in grads_kv] + [g[1] for g in grads_kv], 1)
        key_acc[pl.ds(before, BLOCK), :] += both[:BLOCK]
        key_acc[pl.ds(own, BLOCK), :] += both[BLOCK:]
        return carry

    lax.fori_loop(0, qkv_ref.shape[0] // BLOCK, block, 0)
    out_ref[:, width:] = key_acc[...].astype(BF)


def cross_window(b, dec_ends, enc_ends, enc_length, window):
    first = jnp.int32(0)
    for c in range(len(dec_ends) - 1):
        first = jnp.where(b * BLOCK >= dec_ends[c], enc_ends[c], first)
    return pl.multiple_of(
        jnp.minimum(first // BLOCK * BLOCK, enc_length - window), BLOCK
    )


def cross_forward_kernel(
    quarter, size, dec_ref, enc_ref, q_ref, kv_ref, context_ref, narrow_ref, broad_ref
):
    heads = narrow_ref.shape[1]
    width = heads * size
    me = lax.axis_index("heads")
    enc_length = kv_ref.shape[0]
    comments = dec_ref.shape[1]
    dec_ends = running(dec_ref, comments)
    enc_ends = running(enc_ref, comments)
    plain = narrow_ref.shape[0]

    def block(b, window, first, store):
        own = place_of(b, me, quarter)
        query = b * BLOCK + lax.broadcasted_iota(jnp.int32, (BLOCK, 1), 0)
        low = jnp.zeros((BLOCK, 1), jnp.int32)
        high = jnp.full((BLOCK, 1), enc_ends[0], jnp.int32)
        for c in range(comments):
            later = query >= dec_ends[c]
            last = c == comments - 1
            low = jnp.where(later, 0 if last else enc_ends[c], low)
            high = jnp.where(later, enc_length if last else enc_ends[c + 1], high)
        key = first + lax.broadcasted_iota(jnp.int32, (BLOCK, window), 1)
        allowed = (key >= low) & (key < high)
        outs = []
        for h in range(heads):
            q = q_ref[pl.ds(own, BLOCK), h * size : (h + 1) * size]
            k = kv_ref[pl.ds(first, window), h * size : (h + 1) * size]
            v = kv_ref[pl.ds(first, window), width + h * size : width + (h + 1) * size]
            scores = jnp.where(allowed, dot(q, k, NT), NEG)
            top = jnp.max(scores, axis=-1, keepdims=True)
            e = jnp.exp(scores - top)
            probs = (e * (1.0 / jnp.sum(e, axis=-1, keepdims=True))).astype(BF)
            store(h, probs)
            outs.append(dot(probs, v, NN).astype(BF))
        context_ref[pl.ds(own, BLOCK), :] = jnp.concatenate(outs, 1)

    def narrow(b, carry):
        def store(h, probs):
            narrow_ref[b, h] = probs

        window = narrow_ref.shape[3]
        block(b, window, cross_window(b, dec_ends, enc_ends, enc_length, window), store)
        return carry

    def broad(b, carry):
        def store(h, probs):
            broad_ref[b - plain, h] = probs

        block(b, enc_length, 0, store)
        return carry

    lax.fori_loop(0, plain, narrow, 0)
    lax.fori_loop(plain, q_ref.shape[0] // BLOCK, broad, 0)


def cross_backward_kernel(
    quarter,
    size,
    dec_ref,
    enc_ref,
    q_ref,
    kv_ref,
    narrow_ref,
    broad_ref,
    grad_ref,
    grad_q_ref,
    grad_kv_ref,
    key_acc,
):
    heads = narrow_ref.shape[1]
    width = heads * size
    me = lax.axis_index("heads")
    enc_length = kv_ref.shape[0]
    comments = dec_ref.shape[1]
    dec_ends = running(dec_ref, comments)
    enc_ends = running(enc_ref, comments)
    plain = narrow_ref.shape[0]
    key_acc[...] = jnp.zeros_like(key_acc)

    def block(b, window, first, load):
        own = place_of(b, me, quarter)
        grads_q, grads_kv = [], []
        for h in range(heads):
            q = q_ref[pl.ds(own, BLOCK), h * size : (h + 1) * size]
            k = kv_ref[pl.ds(first, window), h * size : (h + 1) * size]
            v = kv_ref[pl.ds(first, window), width + h * size : width + (h + 1) * size]
            c = grad_ref[pl.ds(own, BLOCK), h * size : (h + 1) * size]
            probs = load(h)
            wide = probs.astype(F32)
            grad_probs = dot(c, v, NT)
            inner = jnp.sum(grad_probs * wide, axis=-1, keepdims=True)
            short = (wide * (grad_probs - inner)).astype(BF)
            grads_q.append(dot(short, k, NN).astype(BF))
            grads_kv.append((dot(short, q, TN), dot(probs, c, TN)))
        grad_q_ref[pl.ds(own, BLOCK), :] = jnp.concatenate(grads_q, 1)
        key_acc[pl.ds(first, window), :] += jnp.concatenate(
            [g[0] for g in grads_kv] + [g[1] for g in grads_kv], 1
        )

    def narrow(b, carry):
        window = narrow_ref.shape[3]
        first = cross_window(b, dec_ends, enc_ends, enc_length, window)
        block(b, window, first, lambda h: narrow_ref[b, h])
        return carry

    def broad(b, carry):
        block(b, enc_length, 0, lambda h: broad_ref[b - plain, h])
        return carry

    lax.fori_loop(0, plain, narrow, 0)
    lax.fori_loop(plain, q_ref.shape[0] // BLOCK, broad, 0)
    grad_kv_ref[...] = key_acc[...].astype(BF)


def kernel_call(body, outs, in_specs, name, flops, scratch=()):
    return pl.pallas_call(
        body,
        out_shape=[jax.ShapeDtypeStruct(s, d) for s, d in outs],
        in_specs=in_specs,
        out_specs=[VMEM] * len(outs),
        scratch_shapes=list(scratch),
        compiler_params=PARAMS,
        name=name,
        cost_estimate=pl.CostEstimate(flops=flops, bytes_accessed=4 << 20, transcendentals=0),
    )


def mm(a, b, spec, dtype=F32):
    return jnp.einsum(spec, a, b, preferred_element_type=F32).astype(dtype)


def factor_of(values):
    return lax.rsqrt(jnp.mean(values * values, axis=-1, keepdims=True) + EPS)


def rms(values, gain):
    return (values * factor_of(values) * gain).astype(BF)


def rms_backward(values, gain, grad):
    factor = factor_of(values)
    scaled = gain * grad
    mean = jnp.mean(scaled * values, axis=-1, keepdims=True)
    grad_gain = jnp.sum(grad * values * factor, axis=0)
    return factor * scaled - values * (factor * factor * factor * mean), grad_gain


def shards(
    inputs,
    encoded,
    cotangent,
    dec_lengths,
    enc_lengths,
    self_query,
    self_key,
    self_value,
    self_output,
    cross_query,
    cross_key,
    cross_value,
    cross_output,
    inner_weight,
    outer_weight,
    bias_table,
    gain_first,
    gain_second,
    gain_third,
):
    groups = lax.axis_size("heads")
    devices = groups * lax.axis_size("rows")
    me = lax.axis_index("heads")
    heads = bias_table.shape[1]
    buckets = bias_table.shape[0]
    width = self_query.shape[1]
    size = width // heads
    quarter = inputs.shape[1]
    length = quarter * groups
    enc_quarter = encoded.shape[1]
    enc_length = enc_quarter * groups
    features = inputs.shape[2]
    hidden_width = inner_weight.shape[1]
    comments = dec_lengths.shape[1]
    starts = bucket_starts(buckets, MAX_DISTANCE)
    blocks = length // BLOCK
    plain = LEAST * comments // BLOCK
    window = 4 * MOST

    inputs, encoded, cotangent = inputs[0], encoded[0], cotangent[0]

    gains = jnp.concatenate([gain_first, gain_second, gain_third])
    each = gain_first.shape[0]
    spread = jnp.broadcast_to(gains[None], (devices, 3 * each))
    spread = lax.all_to_all(spread, ("rows", "heads"), 0, 0, tiled=True).astype(F32)
    gain_one, gain_two, gain_three = (
        spread[:, i * each : (i + 1) * each].reshape(1, features) for i in range(3)
    )

    weights_one = gather_rows(jnp.concatenate([self_query, self_key, self_value], 1))
    inputs_pieces = gather_heads(inputs)
    weights_two = gather_rows(
        jnp.concatenate(
            [self_output.T, cross_query, cross_key, cross_value, cross_output.T], 1
        )
    )
    enc_pieces = gather_heads(encoded)
    weights_three = gather_rows(jnp.concatenate([inner_weight, outer_weight.T], 1))
    cot_pieces = gather_heads(cotangent)

    out_self = weights_two[:, :width]
    query_cross = weights_two[:, width : 2 * width]
    kv_cross = weights_two[:, 2 * width : 4 * width]
    out_cross = weights_two[:, 4 * width :]
    inner = weights_three[:, :hidden_width]
    outer = weights_three[:, hidden_width:]

    table = bias_table.astype(F32)
    bias = kernel_call(
        functools.partial(bias_kernel, starts),
        [((heads, BLOCK, 2 * BLOCK), F32)],
        [SMEM],
        "bias",
        1 << 20,
    )(table)[0]

    inputs_full = jnp.concatenate(inputs_pieces, 0).astype(F32)
    norm_one = rms(inputs_full, gain_one)
    qkv_one = mm(norm_one, weights_one, "td,de->te", BF)
    context_one, probs_one = kernel_call(
        functools.partial(self_forward_kernel, quarter, size),
        [((length, width), BF), ((blocks, heads, BLOCK, 2 * BLOCK), BF)],
        [SMEM, VMEM, VMEM],
        "self_forward",
        1 << 30,
    )(dec_lengths, qkv_one, bias)

    def quarters(array):
        return [array[k * quarter : (k + 1) * quarter] for k in range(groups)]

    inputs_float = inputs.astype(F32)
    after_self = inputs_float + scatter_heads(
        [mm(c, out_self, "te,de->td") for c in quarters(context_one)]
    )

    enc_full = place(enc_pieces, "heads").reshape(enc_length, features)
    kv_two = mm(enc_full, kv_cross, "td,de->te", BF)
    norm_two = jnp.concatenate(gather_heads(rms(after_self, gain_two)), 0)
    query_two = mm(norm_two, query_cross, "td,de->te", BF)
    context_two, narrow, broad = kernel_call(
        functools.partial(cross_forward_kernel, quarter, size),
        [
            ((length, width), BF),
            ((plain, heads, BLOCK, window), BF),
            ((blocks - plain, heads, BLOCK, enc_length), BF),
        ],
        [SMEM, SMEM, VMEM, VMEM],
        "cross_forward",
        1 << 30,
    )(dec_lengths, enc_lengths, query_two, kv_two)
    second = after_self + scatter_heads(
        [mm(c, out_cross, "te,de->td") for c in quarters(context_two)]
    )

    cot_full = jnp.concatenate(cot_pieces, 0)
    grad_hidden = mm(cot_full, outer, "td,df->tf")
    norm_three = jnp.concatenate(gather_heads(rms(second, gain_three)), 0)
    active = mm(norm_three, inner, "td,df->tf")
    share = 0.5 * (1.0 + lax.erf(active * np.float32(np.sqrt(0.5))))
    slope = share + active * (
        jnp.exp(-0.5 * active * active) * np.float32(1.0 / np.sqrt(2.0 * np.pi))
    )
    hidden = (active * share).astype(BF)
    grad_active = (grad_hidden * slope).astype(BF)
    grad_norm_three = scatter_heads(
        [mm(g, inner, "tf,df->td") for g in quarters(grad_active)]
    )
    layer_out = second + scatter_heads([mm(x, outer, "tf,df->td") for x in quarters(hidden)])
    inner_grad = mm(norm_three, grad_active, "td,tf->df", BF)
    outer_grad = mm(cot_full, hidden, "td,tf->df", BF)
    ffn_grad = scatter_rows(jnp.concatenate([inner_grad, outer_grad], 1))

    grad_second, gain_three_grad = rms_backward(second, gain_three, grad_norm_three)
    grad_second = cotangent.astype(F32) + grad_second
    branch_two = jnp.concatenate(gather_heads(grad_second.astype(BF)), 0)
    grad_context_two = mm(branch_two, out_cross, "td,de->te", BF)
    grad_query_two, grad_kv_two = kernel_call(
        functools.partial(cross_backward_kernel, quarter, size),
        [((length, width), BF), ((enc_length, 2 * width), BF)],
        [SMEM, SMEM] + [VMEM] * 5,
        "cross_backward",
        2 << 30,
        [pltpu.VMEM((enc_length, 2 * width), F32)],
    )(dec_lengths, enc_lengths, query_two, kv_two, narrow, broad, grad_context_two)
    grad_norm_two = scatter_heads(
        [mm(g, query_cross, "te,de->td") for g in quarters(grad_query_two)]
    )
    first_part, gain_two_grad = rms_backward(after_self, gain_two, grad_norm_two)
    grad_after_self = grad_second + first_part
    branch_one = jnp.concatenate(gather_heads(grad_after_self.astype(BF)), 0)

    cross_output_grad = mm(branch_two, context_two, "td,te->de", BF)
    cross_query_grad = mm(norm_two, grad_query_two, "td,te->de", BF)
    cross_kv_grad = mm(enc_full, grad_kv_two, "td,te->de", BF)
    cross_grad = scatter_rows(
        jnp.concatenate([cross_query_grad, cross_kv_grad, cross_output_grad], 1)
    )
    encoded_grad = scatter_heads(
        [
            mm(
                lax.dynamic_slice_in_dim(
                    grad_kv_two, (me ^ k) * enc_quarter, enc_quarter, 0
                ),
                kv_cross,
                "te,de->td",
            )
            for k in range(groups)
        ]
    )

    grad_context_one = mm(branch_one, out_self, "td,de->te", BF)
    grad_qkv_one, bias_acc = kernel_call(
        functools.partial(self_backward_kernel, quarter, size),
        [((length, 3 * width), BF), ((heads, BLOCK, 2 * BLOCK), F32)],
        [VMEM] * 3,
        "self_backward",
        2 << 30,
        [pltpu.VMEM((length, 2 * width), F32)],
    )(qkv_one, probs_one, grad_context_one)
    qkv_grad = mm(norm_one, grad_qkv_one, "td,te->de", BF)
    self_output_grad = mm(branch_one, context_one, "td,te->de", BF)
    self_grad = scatter_rows(jnp.concatenate([qkv_grad, self_output_grad], 1))
    grad_norm_one = scatter_heads(
        [mm(g, weights_one, "te,de->td") for g in quarters(grad_qkv_one)]
    )
    input_part, gain_one_grad = rms_backward(inputs_float, gain_one, grad_norm_one)
    input_grad = grad_after_self + input_part

    bias_sums = kernel_call(
        functools.partial(bias_grad_kernel, starts),
        [((heads, buckets, 2 * BLOCK), F32)],
        [VMEM],
        "bias_grad",
        1 << 20,
    )(bias_acc)[0]
    bias_grad = jnp.sum(bias_sums, axis=-1).T.reshape(1, -1)
    gain_grads = jnp.stack([gain_one_grad, gain_two_grad, gain_three_grad])
    gain_grads = gain_grads.reshape(3, devices, each).transpose(1, 0, 2).reshape(devices, 3 * each)
    same = (jnp.arange(devices, dtype=jnp.int32)[:, None] % groups == me).astype(F32)
    small = jnp.concatenate([gain_grads, same * bias_grad], 1)
    small = jnp.sum(lax.all_to_all(small, ("rows", "heads"), 0, 0, tiled=True), axis=0)

    return (
        layer_out.astype(BF)[None],
        input_grad[None],
        encoded_grad[None],
        self_grad[:, :width],
        self_grad[:, width : 2 * width],
        self_grad[:, 2 * width : 3 * width],
        self_grad[:, 3 * width :].T,
        cross_grad[:, :width],
        cross_grad[:, width : 2 * width],
        cross_grad[:, 2 * width : 3 * width],
        cross_grad[:, 3 * width :].T,
        ffn_grad[:, :hidden_width],
        ffn_grad[:, hidden_width:].T,
        small[3 * each :].reshape(buckets, heads),
        small[:each],
        small[each : 2 * each],
        small[2 * each : 3 * each],
    )


def solution(mesh):
    positions = P("rows", "heads", None)
    columns = P("rows", "heads")
    lines = P("heads", "rows")
    gains = P(("rows", "heads"))
    return jax.shard_map(
        shards,
        mesh=mesh,
        in_specs=(
            positions,
            positions,
            positions,
            P("rows", None),
            P("rows", None),
            columns,
            columns,
            columns,
            lines,
            columns,
            columns,
            columns,
            lines,
            columns,
            lines,
            P(None, "heads"),
            gains,
            gains,
            gains,
        ),
        out_specs=(
            positions,
            positions,
            positions,
            columns,
            columns,
            columns,
            lines,
            columns,
            columns,
            columns,
            lines,
            columns,
            lines,
            P(None, "heads"),
            gains,
            gains,
            gains,
        ),
        check_vma=False,
    )
```

```python
import functools

import jax
import jax.numpy as jnp
import numpy as np
from jax import lax
from jax.experimental import pallas as pl
from jax.experimental.pallas import tpu as pltpu
from jax.sharding import PartitionSpec as P

MAX_DISTANCE = 128
EPS = 1e-06
NEG = -1000000000.0
LEAST = 96
MOST = 128
BLOCK = 128
BF = jnp.bfloat16
F32 = jnp.float32
VMEM = pl.BlockSpec(memory_space=pltpu.VMEM)
SMEM = pl.BlockSpec(memory_space=pltpu.SMEM)


def bucket_starts(bucket_count, max_reach):
    exact_span = bucket_count // 2
    starts = list(range(exact_span + 1))
    for target in range(exact_span + 1, bucket_count):
        distance = exact_span
        while (
            distance < max_reach
            and exact_span
            + int(
                np.log(distance / exact_span)
                / np.log(max_reach / exact_span)
                * (bucket_count - exact_span)
            )
            < target
        ):
            distance += 1
        starts.append(distance)
    return starts


class Far:
    def __init__(self, array):
        self.array = array


class Moves:
    def __init__(self, sems):
        self.sems, self.used = sems, 0
        self.coming, self.going, self.started = [], [], []

    def copy(self, source, target):
        made = pltpu.make_async_copy(source, target, self.sems.at[self.used])
        self.used += 1
        made.start()
        return made

    def need(self, *refs):
        for ref in refs:
            for k, (held, made) in enumerate(self.coming):
                if held is ref:
                    made.wait()
                    del self.coming[k]
                    break

    def need_all(self):
        self.need(*[held for held, made in self.coming])

    def send(self, source, target):
        self.started.append(self.copy(source, target))

    def ready(self, *refs):
        for ref in refs:
            for k, (held, target) in enumerate(self.going):
                if held is ref:
                    self.send(held, target)
                    del self.going[k]
                    break

    def finish(self):
        self.need_all()
        self.ready(*[held for held, target in self.going])
        for made in self.started:
            made.wait()


HBM = pl.BlockSpec(memory_space=pltpu.HBM)


def call(body, name, args, outs, scratch=(), us=2.0, smem=0, raw=0, lazy=False):
    far_in = [isinstance(x, Far) for x in args]
    arrays = [
        pltpu.with_memory_space_constraint(x.array, pltpu.HBM) if isinstance(x, Far) else x
        for x in args
    ]
    far_out = [len(o) > 2 for o in outs]
    last = len(outs) - (raw > 0)
    held = [pltpu.VMEM(x.shape, x.dtype) for x, f in zip(arrays, far_in) if f]
    held += [pltpu.VMEM(o[0], o[1]) for o, f in zip(outs[:last], far_out) if f]
    copies = len(held) + raw
    if copies:
        held.append(pltpu.SemaphoreType.DMA((copies,)))

    def kernel(*refs):
        ins, results = refs[: len(args)], refs[len(args) : len(args) + len(outs)]
        own = refs[len(args) + len(outs) : len(args) + len(outs) + len(scratch)]
        spare = list(refs[len(args) + len(outs) + len(scratch) :])
        moves = Moves(spare.pop() if copies else None)
        given = []
        for ref, f in zip(ins, far_in):
            if f:
                here = spare.pop(0)
                moves.coming.append((here, moves.copy(ref, here)))
                ref = here
            given.append(ref)
        for k, ref in enumerate(results):
            if far_out[k] and k < last:
                here = spare.pop(0)
                moves.going.append((here, ref))
                ref = here
            given.append(ref)
        if not lazy:
            moves.need_all()
        body(moves, *given, *own)
        moves.finish()

    return pl.pallas_call(
        kernel,
        out_shape=[
            (pltpu.HBM if f else jax.ShapeDtypeStruct)(o[0], o[1])
            for o, f in zip(outs, far_out)
        ],
        in_specs=[SMEM] * smem + [HBM if f else VMEM for f in far_in[smem:]],
        out_specs=[HBM if f else VMEM for f in far_out],
        scratch_shapes=list(scratch) + held,
        compiler_params=pltpu.CompilerParams(vmem_limit_bytes=40 << 20),
        name=name,
        cost_estimate=pl.CostEstimate(
            flops=int(us * 1e9), bytes_accessed=int(us * 3e6), transcendentals=0
        ),
    )(*arrays)


def send(part, axis, bits):
    count = lax.axis_size(axis)
    return lax.ppermute(part, axis, [(i, i ^ bits) for i in range(count)])


def after(value, *others):
    return lax.optimization_barrier((value,) + others)[0]


def gather_heads(part):
    across = send(part, "heads", 2)
    return [part, send(part, "heads", 1), across, send(across, "heads", 1)]


def place_kernel(count, moves, *refs):
    me = lax.axis_index("rows")
    for t in range(count):
        moves.send(refs[t], refs[count].at[me ^ t])


def gather_rows_first(part):
    return [part] + [
        send(part, "rows", 2 * upper) for upper in range(1, lax.axis_size("rows") // 2)
    ]


def gather_rows_second(firsts, *others):
    pieces = []
    for near in firsts:
        pieces += [near, send(near, "rows", 1)]
    count = len(pieces)
    shape = (count,) + pieces[0].shape
    pieces[0] = after(pieces[0], *others)
    placed = call(
        functools.partial(place_kernel, count), "place", pieces, [(shape, BF, "far")], us=1.5, raw=count
    )[0]
    return placed.reshape(-1, shape[2])


def gather_rows(part):
    count = lax.axis_size("rows")
    spread = jnp.broadcast_to(part[None], (count,) + part.shape)
    return lax.all_to_all(spread, "rows", 0, 0, tiled=True).reshape(-1, part.shape[1])


def exchange_rows(blocks):
    return lax.all_to_all(blocks, "rows", 0, 0, tiled=True)


def sum_rows(got):
    return jnp.sum(got.astype(F32), axis=0)


def dot(a, b, dims):
    return lax.dot_general(a, b, (dims, ((), ())), preferred_element_type=F32)


NT = ((1,), (1,))
NN = ((1,), (0,))
TN = ((0,), (0,))


def core_and_chip():
    me = lax.axis_index("heads")
    return me % 2, me // 2


def rms_rows(values, gain):
    factor = lax.rsqrt(jnp.mean(values * values, axis=-1, keepdims=True) + EPS)
    return (values * factor * gain).astype(BF)


def pick_half(half, pieces, out):
    unused, chip = core_and_chip()
    quarter = pieces[0].shape[0]
    for near in (True, False):

        @pl.when((chip == half) == near)
        def _(near=near):
            for s in range(2):
                out[s * quarter : (s + 1) * quarter, :] = pieces[s + (0 if near else 2)][...]


def distances(first, rows):
    query = lax.broadcasted_iota(jnp.int32, (rows, 2 * BLOCK), 0) + (first + BLOCK)
    return query - lax.broadcasted_iota(jnp.int32, (rows, 2 * BLOCK), 1)


def bias_kernel(starts, moves, table_ref, out_ref):
    heads = out_ref.shape[0]
    step = 32

    def rows(t, carry):
        first = pl.multiple_of(t * step, step)
        reach = distances(first, step)
        values = [jnp.full((step, 2 * BLOCK), table_ref[0, h], F32) for h in range(heads)]
        for b in range(1, len(starts)):
            beyond = reach >= starts[b]
            values = [jnp.where(beyond, table_ref[b, h], values[h]) for h in range(heads)]
        for h in range(heads):
            out_ref[h, pl.ds(first, step), :] = values[h]
        return carry

    lax.fori_loop(0, BLOCK // step, rows, 0)


def bias_grad_kernel(starts, moves, one_ref, two_ref, out_ref):
    heads = one_ref.shape[0]
    reach = distances(0, BLOCK)
    for h in range(heads):
        acc = one_ref[h] + two_ref[h]
        for b in range(len(starts)):
            inside = reach < starts[1] if b == 0 else reach >= starts[b]
            if 0 < b < len(starts) - 1:
                inside = inside & (reach < starts[b + 1])
            out_ref[h, b : b + 1, :] = jnp.sum(jnp.where(inside, acc, 0.0), axis=0, keepdims=True)


def running(lengths_ref, count):
    total = lengths_ref[0, 0]
    ends = [total]
    for c in range(1, count):
        total = total + lengths_ref[0, c]
        ends.append(total)
    return ends


def slot_of(block, core, quarter):
    each = quarter // BLOCK
    return pl.multiple_of((((block // each) ^ core) * each + block % each) * BLOCK, BLOCK)


def softmax(scores):
    e = jnp.exp(scores - jnp.max(scores, axis=-1, keepdims=True))
    return (e * (1.0 / jnp.sum(e, axis=-1, keepdims=True))).astype(BF)


def self_forward_kernel(size, half, moves, lengths_ref, *refs):
    pieces = refs[:4]
    gain_ref, w_ref, bias_ref = refs[4:7]
    norm_ref, qkv_ref, context_ref, probs_ref, own_ref, near_ref, far_ref = refs[7:14]
    x, kv = refs[14:]
    heads = bias_ref.shape[0]
    width = heads * size
    quarter = own_ref.shape[0]
    core, chip = core_and_chip()
    ends = running(lengths_ref, lengths_ref.shape[1])
    blocks = 2 * quarter // BLOCK
    gain = gain_ref[...]
    pick_half(half, pieces, x)
    own_ref[...] = x[:quarter, :]
    moves.need(w_ref)

    if half:
        for k in range(4):

            @pl.when((core == 1 - k % 2) & ((chip == 0) == (k < 2)))
            def _(k=k):
                before = pieces[k][quarter - BLOCK :, :].astype(F32)
                kv[:BLOCK, :] = dot(rms_rows(before, gain), w_ref[:, width : 3 * width], NN).astype(
                    BF
                )
    else:
        kv[:BLOCK, :] = jnp.zeros((BLOCK, 2 * width), BF)

    def project(b, carry):
        at = pl.multiple_of(slot_of(b, core, quarter), BLOCK)
        norm = rms_rows(x[pl.ds(at, BLOCK), :].astype(F32), gain)
        norm_ref[pl.ds(at, BLOCK), :] = norm
        qkv = dot(norm, w_ref[:, : 3 * width], NN).astype(BF)
        qkv_ref[pl.ds(at, BLOCK), :] = qkv
        kv[pl.ds(pl.multiple_of((b + 1) * BLOCK, BLOCK), BLOCK), :] = qkv[:, width:]
        return carry

    lax.fori_loop(0, blocks, project, 0)
    moves.ready(norm_ref, qkv_ref)
    moves.need(bias_ref)

    def block(b, carry):
        own = slot_of(b, core, quarter)
        at = pl.multiple_of(b * BLOCK, BLOCK)
        base = (half * blocks + b) * BLOCK
        query = base + lax.broadcasted_iota(jnp.int32, (BLOCK, 1), 0)
        start = jnp.zeros((BLOCK, 1), jnp.int32)
        for end in ends:
            start = jnp.where(query >= end, end, start)
        key = base - BLOCK + lax.broadcasted_iota(jnp.int32, (BLOCK, 2 * BLOCK), 1)
        allowed = (key >= start) & (key <= query)
        outs = []
        for h in range(heads):
            q = qkv_ref[pl.ds(own, BLOCK), h * size : (h + 1) * size]
            k = kv[pl.ds(at, 2 * BLOCK), h * size : (h + 1) * size]
            v = kv[pl.ds(at, 2 * BLOCK), width + h * size : width + (h + 1) * size]
            probs = softmax(jnp.where(allowed, dot(q, k, NT) + bias_ref[h], NEG))
            probs_ref[b, h] = probs
            outs.append(dot(probs, v, NN).astype(BF))
        context_ref[pl.ds(own, BLOCK), :] = jnp.concatenate(outs, 1)
        return carry

    lax.fori_loop(0, blocks, block, 0)
    moves.ready(context_ref, probs_ref)
    out_weight = w_ref[:, 3 * width :]
    far_ref[...] = dot(context_ref[quarter:, :], out_weight, NT).astype(BF)
    near_ref[...] = dot(context_ref[:quarter, :], out_weight, NT)


def self_backward_kernel(size, half, moves, *refs):
    own_ref, other_ref, w_ref, qkv_ref, probs_ref, edge_in = refs[:6]
    out_ref, acc_ref = refs[6:8]
    branch_ref = refs[-4]
    kv, key_acc, grad = refs[-3:]
    heads = acc_ref.shape[0]
    width = heads * size
    quarter = own_ref.shape[0]
    core, chip = core_and_chip()
    blocks = 2 * quarter // BLOCK
    moves.send(own_ref, branch_ref.at[:quarter])
    moves.send(other_ref, branch_ref.at[quarter:])
    key_acc[...] = jnp.zeros_like(key_acc)
    acc_ref[...] = jnp.zeros_like(acc_ref)
    moves.need(w_ref)
    out_weight = w_ref[:, 3 * width :]
    grad[:quarter, :] = dot(own_ref[...], out_weight, NN).astype(BF)
    grad[quarter:, :] = dot(other_ref[...], out_weight, NN).astype(BF)
    moves.need(edge_in, qkv_ref)
    if half:
        kv[:BLOCK, :] = edge_in[pl.ds(slot_of(blocks - 1, core, quarter), BLOCK), width:]
    else:
        kv[:BLOCK, :] = jnp.zeros((BLOCK, 2 * width), BF)
        key_acc[blocks * BLOCK :, :] = edge_in[...]
    for b in range(blocks):
        kv[(b + 1) * BLOCK : (b + 2) * BLOCK, :] = qkv_ref[
            pl.ds(slot_of(b, core, quarter), BLOCK), width:
        ]
    moves.need(probs_ref)

    def block(b, carry):
        own = slot_of(b, core, quarter)
        at = pl.multiple_of(b * BLOCK, BLOCK)
        grads_q, grads_k, grads_v = [], [], []
        for h in range(heads):
            q = qkv_ref[pl.ds(own, BLOCK), h * size : (h + 1) * size]
            k = kv[pl.ds(at, 2 * BLOCK), h * size : (h + 1) * size]
            v = kv[pl.ds(at, 2 * BLOCK), width + h * size : width + (h + 1) * size]
            c = grad[pl.ds(own, BLOCK), h * size : (h + 1) * size]
            probs = probs_ref[b, h]
            wide = probs.astype(F32)
            grad_probs = dot(c, v, NT)
            inner = jnp.sum(grad_probs * wide, axis=-1, keepdims=True)
            grad_scores = wide * (grad_probs - inner)
            acc_ref[h] += grad_scores
            short = grad_scores.astype(BF)
            grads_q.append(dot(short, k, NN).astype(BF))
            grads_k.append(dot(short, q, TN))
            grads_v.append(dot(probs, c, TN))
        out_ref[pl.ds(own, BLOCK), :width] = jnp.concatenate(grads_q, 1)
        key_acc[pl.ds(at, 2 * BLOCK), :] += jnp.concatenate(grads_k + grads_v, 1)
        return carry

    lax.fori_loop(0, blocks, block, 0)
    for b in range(blocks):
        out_ref[pl.ds(slot_of(b, core, quarter), BLOCK), width:] = key_acc[
            (b + 1) * BLOCK : (b + 2) * BLOCK, :
        ].astype(BF)
    if half:
        refs[8][...] = key_acc[:BLOCK, :]


def cross_keys_kernel(width, moves, *refs):
    pieces, w_ref = refs[:4], refs[4]
    kv_ref, enc_ref = refs[5:]
    quarter = pieces[0].shape[1]
    me = lax.axis_index("heads")
    weight = w_ref[:, width : 3 * width]
    for k in range(4):
        at = pl.ds(pl.multiple_of((me ^ k) * quarter, quarter), quarter)
        moves.send(pieces[k].at[0], enc_ref.at[at])
        kv_ref[at, :] = dot(pieces[k][0], weight, NN).astype(BF)


def cross_window(block, dec_ends, enc_ends, enc_length, window):
    first = jnp.int32(0)
    for c in range(len(dec_ends) - 1):
        first = jnp.where(block * BLOCK >= dec_ends[c], enc_ends[c], first)
    return pl.multiple_of(
        jnp.minimum(first // BLOCK * BLOCK, enc_length - window), BLOCK
    )


def cross_forward_kernel(size, half, moves, dec_ref, enc_ref, own_ref, other_ref, w_ref, kv_ref, *refs):
    query_ref, context_ref, near_ref, far_ref = refs[:4]
    all_probs, norm_ref = refs[4:-1], refs[-1]
    heads = refs[4].shape[1]
    width = heads * size
    quarter = own_ref.shape[0]
    core, chip = core_and_chip()
    first = half * (2 * quarter // BLOCK)
    enc_length = kv_ref.shape[0]
    comments = dec_ref.shape[1]
    dec_ends = running(dec_ref, comments)
    enc_ends = running(enc_ref, comments)
    moves.send(own_ref, norm_ref.at[:quarter])
    moves.send(other_ref, norm_ref.at[quarter:])
    moves.need(w_ref)
    query_ref[:quarter, :] = dot(own_ref[...], w_ref[:, :width], NN).astype(BF)
    query_ref[quarter:, :] = dot(other_ref[...], w_ref[:, :width], NN).astype(BF)
    moves.ready(query_ref)
    moves.need(kv_ref)
    done = 0
    for probs_ref in all_probs:
        window = probs_ref.shape[3]

        def block(b, carry, window=window, probs_ref=probs_ref, done=done):
            own = slot_of(b, core, quarter)
            base = (first + b) * BLOCK
            start = (
                cross_window(first + b, dec_ends, enc_ends, enc_length, window)
                if window < enc_length
                else 0
            )
            query = base + lax.broadcasted_iota(jnp.int32, (BLOCK, 1), 0)
            low = jnp.zeros((BLOCK, 1), jnp.int32)
            high = jnp.full((BLOCK, 1), enc_ends[0], jnp.int32)
            for c in range(comments):
                later = query >= dec_ends[c]
                last = c == comments - 1
                low = jnp.where(later, 0 if last else enc_ends[c], low)
                high = jnp.where(later, enc_length if last else enc_ends[c + 1], high)
            key = start + lax.broadcasted_iota(jnp.int32, (BLOCK, window), 1)
            allowed = (key >= low) & (key < high)
            contexts = []
            for h in range(heads):
                q = query_ref[pl.ds(own, BLOCK), h * size : (h + 1) * size]
                k = kv_ref[pl.ds(start, window), h * size : (h + 1) * size]
                v = kv_ref[pl.ds(start, window), width + h * size : width + (h + 1) * size]
                probs = softmax(jnp.where(allowed, dot(q, k, NT), NEG))
                probs_ref[b - done, h] = probs
                contexts.append(dot(probs, v, NN).astype(BF))
            context_ref[pl.ds(own, BLOCK), :] = jnp.concatenate(contexts, 1)
            return carry

        lax.fori_loop(done, done + probs_ref.shape[0], block, 0)
        done += probs_ref.shape[0]
        moves.ready(probs_ref)
    moves.ready(context_ref)
    out_weight = w_ref[:, 3 * width :]
    far_ref[...] = dot(context_ref[quarter:, :], out_weight, NT).astype(BF)
    near_ref[...] = dot(context_ref[:quarter, :], out_weight, NT)


def cross_backward_kernel(size, half, kinds, more, moves, dec_ref, enc_ref, *refs):
    own_ref, other_ref, w_ref, query_ref, kv_ref = refs[:5]
    probs_refs = refs[5 : 5 + kinds]
    so_far = refs[5 + kinds : 5 + kinds + more]
    grad_q_ref, grad_kv_ref, near_ref, far_ref, branch_ref, key_acc, grad = refs[5 + kinds + more :]
    heads = probs_refs[0].shape[1]
    width = heads * size
    quarter = own_ref.shape[0]
    core, chip = core_and_chip()
    first = half * (2 * quarter // BLOCK)
    enc_length = kv_ref.shape[0]
    comments = dec_ref.shape[1]
    dec_ends = running(dec_ref, comments)
    enc_ends = running(enc_ref, comments)
    moves.send(own_ref, branch_ref.at[:quarter])
    moves.send(other_ref, branch_ref.at[quarter:])
    key_acc[...] = so_far[0][...] if more else jnp.zeros_like(key_acc)
    moves.need(w_ref)
    out_weight = w_ref[:, 3 * width :]
    grad[:quarter, :] = dot(own_ref[...], out_weight, NN).astype(BF)
    grad[quarter:, :] = dot(other_ref[...], out_weight, NN).astype(BF)
    moves.need(query_ref, kv_ref)
    done = 0
    for probs_ref in probs_refs:
        moves.need(probs_ref)
        window = probs_ref.shape[3]

        def block(b, carry, window=window, probs_ref=probs_ref, done=done):
            own = slot_of(b, core, quarter)
            start = (
                cross_window(first + b, dec_ends, enc_ends, enc_length, window)
                if window < enc_length
                else 0
            )
            grads_q, grads_k, grads_v = [], [], []
            for h in range(heads):
                q = query_ref[pl.ds(own, BLOCK), h * size : (h + 1) * size]
                k = kv_ref[pl.ds(start, window), h * size : (h + 1) * size]
                v = kv_ref[pl.ds(start, window), width + h * size : width + (h + 1) * size]
                c = grad[pl.ds(own, BLOCK), h * size : (h + 1) * size]
                probs = probs_ref[b - done, h]
                wide = probs.astype(F32)
                grad_probs = dot(c, v, NT)
                inner = jnp.sum(grad_probs * wide, axis=-1, keepdims=True)
                short = (wide * (grad_probs - inner)).astype(BF)
                grads_q.append(dot(short, k, NN).astype(BF))
                grads_k.append(dot(short, q, TN))
                grads_v.append(dot(probs, c, TN))
            grad_q_ref[pl.ds(own, BLOCK), :] = jnp.concatenate(grads_q, 1)
            key_acc[pl.ds(start, window), :] += jnp.concatenate(grads_k + grads_v, 1)
            return carry

        lax.fori_loop(done, done + probs_ref.shape[0], block, 0)
        done += probs_ref.shape[0]
    grad_kv_ref[...] = key_acc[...].astype(grad_kv_ref.dtype)
    weight = w_ref[:, :width]
    far_ref[...] = dot(grad_q_ref[quarter:, :], weight, NT).astype(BF)
    near_ref[...] = dot(grad_q_ref[:quarter, :], weight, NT)


def ffn_kernel(half, moves, own_ref, other_ref, *refs):
    pieces, w_ref = refs[:4], refs[4]
    cot_ref, hidden_ref, active_ref, own_cot_ref, near_ref, far_ref, norms_ref = refs[5:]
    quarter = own_ref.shape[0]
    units = hidden_ref.shape[1]
    part = 256 if units % 256 == 0 else units
    moves.send(own_ref, norms_ref.at[:quarter])
    moves.send(other_ref, norms_ref.at[quarter:])
    pick_half(half, [part.at[1] for part in pieces], cot_ref)
    own_cot_ref[...] = cot_ref[:quarter, :]
    moves.ready(cot_ref)
    moves.need(w_ref)
    for s, norm_ref in ((0, own_ref), (1, other_ref)):

        def rows(t, carry, s=s, norm_ref=norm_ref):
            at = pl.multiple_of(t * BLOCK, BLOCK)
            to = pl.ds(pl.multiple_of(s * quarter + t * BLOCK, BLOCK), BLOCK)
            norm = norm_ref[pl.ds(at, BLOCK), :]
            cot = cot_ref[to, :]
            for f in range(0, units, part):
                active = dot(norm, w_ref[:, f : f + part], NN)
                grad = dot(cot, w_ref[:, units + f : units + f + part], NN)
                share = 0.5 + 0.5 * lax.erf(active * np.float32(np.sqrt(0.5)))
                slope = share + active * (
                    jnp.exp(-0.5 * active * active) * np.float32(1.0 / np.sqrt(2.0 * np.pi))
                )
                hidden_ref[to, f : f + part] = (active * share).astype(BF)
                active_ref[to, f : f + part] = (grad * slope).astype(BF)
            return carry

        lax.fori_loop(0, quarter // BLOCK, rows, 0)
    moves.ready(hidden_ref, active_ref)
    weight = w_ref[:, :units]
    far_ref[...] = dot(active_ref[quarter:, :], weight, NT).astype(BF)
    near_ref[...] = dot(active_ref[:quarter, :], weight, NT)


def scatter_kernel(first, moves, one_ref, two_ref, w_ref, far_far, far_near, near_far, near_near):
    unused, chip = core_and_chip()
    quarter = far_far.shape[0]
    weight = w_ref[:, first : first + one_ref.shape[1]]
    for index in range(2):

        @pl.when(chip == index)
        def _(index=index):
            near, far = (one_ref, two_ref) if index == 0 else (two_ref, one_ref)
            far_far[...] = dot(far[quarter:, :], weight, NT).astype(BF)
            near_far[...] = dot(near[quarter:, :], weight, NT).astype(BF)
            far_near[...] = dot(far[:quarter, :], weight, NT)
            near_near[...] = dot(near[:quarter, :], weight, NT)


def scatter_keys_kernel(width, moves, grad_ref, w_ref, *outs):
    quarter = outs[0].shape[0]
    me = lax.axis_index("heads")
    weight = w_ref[:, width : 3 * width]
    for k in range(4):
        at = pl.ds(pl.multiple_of((me ^ k) * quarter, quarter), quarter)
        outs[k][...] = dot(grad_ref[at, :], weight, NT).astype(outs[k].dtype)


def norm_forward_kernel(moves, one_ref, two_ref, base_ref, gain_ref, sum_ref, norm_ref):
    rows = base_ref.shape[0]
    step = min(64, rows)

    def some(t, carry):
        at = pl.ds(pl.multiple_of(t * step, step), step)
        total = base_ref[at, :].astype(F32) + one_ref[at, :].astype(F32) + two_ref[at, :].astype(F32)
        sum_ref[at, :] = total
        norm_ref[at, :] = rms_rows(total, gain_ref[...])
        return carry

    lax.fori_loop(0, rows // step, some, 0)


def norm_backward_kernel(parts, moves, *refs):
    values_ref, base_ref, gain_ref = refs[parts : parts + 3]
    grad_ref, *branch_ref = refs[parts + 3 :]
    rows = values_ref.shape[0]
    step = min(64, rows)

    def some(t, carry):
        at = pl.ds(pl.multiple_of(t * step, step), step)
        grad = refs[0][at, :].astype(F32)
        for part in refs[1:parts]:
            grad = grad + part[at, :].astype(F32)
        values = values_ref[at, :].astype(F32)
        factor = lax.rsqrt(jnp.mean(values * values, axis=-1, keepdims=True) + EPS)
        scaled = gain_ref[...] * grad
        mean = jnp.mean(scaled * values, axis=-1, keepdims=True)
        total = (
            base_ref[at, :].astype(F32)
            + factor * scaled
            - values * (factor * factor * factor * mean)
        )
        grad_ref[at, :] = total
        if branch_ref:
            branch_ref[0][at, :] = total.astype(BF)
        return carry

    lax.fori_loop(0, rows // step, some, 0)


def weights_kernel(segments, moves, *refs):
    out_ref, whole = refs[-2:]
    features = whole.shape[0]
    group = out_ref.shape[1]
    to = 0
    for pairs in segments:
        for left, right in pairs:
            moves.need(refs[left], refs[right])
        lanes = refs[pairs[0][1]].shape[1]

        def rows(j, carry, pairs=pairs, to=to, lanes=lanes):
            at = pl.ds(pl.multiple_of(j * BLOCK, BLOCK), BLOCK)
            total = sum(dot(refs[left][:, at], refs[right][...], TN) for left, right in pairs)
            whole[at, to : to + lanes] = total.astype(BF)
            return carry

        lax.fori_loop(0, features // BLOCK, rows, 0)
        to += lanes
    for r in range(features // group):
        block = whole.at[r * group : (r + 1) * group, :]
        if group % 16 == 0:
            moves.send(block, out_ref.at[r])
        else:
            out_ref[r] = block[...]


def weight_blocks(segments, lanes, features, us):
    operands, index = [], {}

    def number(operand):
        key = id(operand.array if isinstance(operand, Far) else operand)
        if key not in index:
            index[key] = len(operands)
            operands.append(operand)
        return index[key]

    numbered = [[(number(l), number(r)) for l, r in pairs] for pairs in segments]
    count = lax.axis_size("rows")
    whole = (features // count) % 16 == 0
    return call(
        functools.partial(weights_kernel, numbered),
        "weights",
        operands,
        [((count, features // count, lanes), BF) + (("far",) if whole else ())],
        [pltpu.VMEM((features, lanes), BF)],
        us=us,
        raw=count if whole else 0,
        lazy=True,
    )[0]


def shards(
    inputs,
    encoded,
    cotangent,
    dec_lengths,
    enc_lengths,
    self_query,
    self_key,
    self_value,
    self_output,
    cross_query,
    cross_key,
    cross_value,
    cross_output,
    inner_weight,
    outer_weight,
    bias_table,
    gain_first,
    gain_second,
    gain_third,
):
    groups = lax.axis_size("heads")
    devices = groups * lax.axis_size("rows")
    me = lax.axis_index("heads")
    chip = me // 2
    heads = bias_table.shape[1]
    buckets = bias_table.shape[0]
    width = self_query.shape[1]
    size = width // heads
    quarter = inputs.shape[1]
    half = 2 * quarter
    enc_quarter = encoded.shape[1]
    enc_length = enc_quarter * groups
    features = inputs.shape[2]
    units = inner_weight.shape[1]
    comments = dec_lengths.shape[1]
    starts = bucket_starts(buckets, MAX_DISTANCE)
    blocks = half // BLOCK
    window = 4 * MOST
    order = (1, 0)
    plain = [min(max(LEAST * comments // BLOCK - i * blocks, 0), blocks) for i in range(2)]
    piece = (quarter, features)

    inputs, encoded, cotangent = inputs[0], encoded[0], cotangent[0]

    gains = jnp.concatenate([gain_first, gain_second, gain_third])
    each = gain_first.shape[0]
    spread = jnp.broadcast_to(gains[None], (devices, 3 * each))
    spread = lax.all_to_all(spread, ("rows", "heads"), 0, 0, tiled=True).astype(F32)
    gain_one, gain_two, gain_three = (
        spread[:, i * each : (i + 1) * each].reshape(1, features) for i in range(3)
    )

    far = lambda shape: (shape, BF, "far")
    bias = call(
        functools.partial(bias_kernel, starts),
        "bias",
        [bias_table.astype(F32)],
        [((heads, BLOCK, 2 * BLOCK), F32, "far")],
        us=2.0,
        smem=1,
    )[0]

    weights_one = gather_rows_first(
        jnp.concatenate([self_query, self_key, self_value, self_output.T], 1)
    )
    inputs_pieces = gather_heads(inputs)
    weights_one = gather_rows_second(
        weights_one[:1] + [after(part, inputs_pieces[2]) for part in weights_one[1:]],
        spread,
        bias,
    )
    parts_two = [
        after(part, weights_one) for part in (cross_query, cross_key, cross_value, cross_output)
    ]
    weights_two = gather_rows(jnp.concatenate(parts_two[:3] + [parts_two[3].T], 1))
    both_pieces = gather_heads(after(jnp.stack([encoded, cotangent]), inputs_pieces[2]))

    def chip_sum(near, far):
        return (near + send(far, "heads", 1).astype(F32)).astype(BF)

    def forward_norm(one, base, gain, gate):
        total, norm = call(
            norm_forward_kernel,
            "norm_forward",
            [one, send(one, "heads", 2), base, after(gain, *gate)],
            [(piece, F32, "far"), (piece, BF)],
            us=1.0,
        )
        return Far(total), (norm, send(norm, "heads", 1))

    def backward_norm(parts, values, base, gain, branch=True):
        return call(
            functools.partial(norm_backward_kernel, len(parts)),
            "norm_backward",
            [*parts, values, base, gain],
            [(piece, F32)] + [(piece, BF)] * branch,
            us=1.5,
        )

    def backward_pair(one, values, base, gain, gate):
        grad, branch = backward_norm(
            [one, send(one, "heads", 2)], values, base, after(gain, *gate)
        )
        return grad, (branch, send(branch, "heads", 1))

    def own_of(pair):
        return jnp.where(chip == 0, *(x.array if isinstance(x, Far) else x for x in pair))

    def scatter_halves(pair, weight, first):
        far_far, far_near, near_far, near_near = call(
            functools.partial(scatter_kernel, first),
            "scatter",
            [pair[0], pair[1], Far(weight)],
            [(piece, BF), (piece, F32), (piece, BF), (piece, F32)],
            us=2.0,
        )
        across = send(chip_sum(far_near, far_far), "heads", 2)
        return [near_near, send(near_far, "heads", 1), across]

    parts = ((piece, F32), (piece, BF))
    none = [None, None]
    norms_two, norms_three, branches_two, branches_one = (list(none) for unused in range(4))
    norm_one, qkv_one, context_one, probs_one = list(none), list(none), list(none), list(none)
    after_self, norm_two = list(none), list(none)
    query_two, context_two, probs_two = list(none), list(none), list(none)
    second, norm_three = list(none), list(none)
    cot_half, hidden, active = list(none), list(none), list(none)
    grad_second, branch_two = list(none), list(none)
    grad_query_two, grad_after_self, branch_one = list(none), list(none), list(none)
    grad_qkv_one, bias_acc = list(none), list(none)

    def self_forward(i, gate):
        *saved, own, near, away = call(
            functools.partial(self_forward_kernel, size, i),
            "self_forward",
            [dec_lengths, *inputs_pieces, after(gain_one, *gate), Far(weights_one), Far(bias)],
            [
                far((half, features)),
                far((half, 3 * width)),
                far((half, width)),
                far((blocks, heads, BLOCK, 2 * BLOCK)),
                (piece, BF),
                *parts,
            ],
            [
                pltpu.VMEM((half, features), BF),
                pltpu.VMEM((half + BLOCK, 2 * width), BF),
            ],
            us=2.0,
            smem=1,
            lazy=True,
        )
        norm_one[i], qkv_one[i], context_one[i], probs_one[i] = map(Far, saved)

        def finish(one, gate):
            after_self[i], norm_two[i] = forward_norm(one, own, gain_two, gate)
            return norm_two[i][0]

        return near, away, finish

    def cross_forward(i, gate):
        kinds = []
        if plain[i]:
            kinds.append(far((plain[i], heads, BLOCK, window)))
        if plain[i] < blocks:
            kinds.append(far((blocks - plain[i], heads, BLOCK, enc_length)))
        query, context, near, away, *saved = call(
            functools.partial(cross_forward_kernel, size, i),
            "cross_forward",
            [
                dec_lengths,
                enc_lengths,
                *norm_two[i],
                Far(weights_two),
                Far(after(keys["kv"], *gate)),
            ],
            [far((half, width)), far((half, width)), *parts, *kinds, far((half, features))],
            us=7.0,
            smem=2,
            raw=2,
            lazy=True,
        )
        query_two[i], context_two[i] = Far(query), Far(context)
        *probs_two[i], norms_two[i] = map(Far, saved)

        def finish(one, gate):
            second[i], norm_three[i] = forward_norm(one, after_self[i], gain_three, gate)
            return norm_three[i][0]

        return near, away, finish

    def gather_units(gate):
        parts = [after(part, *gate) for part in (inner_weight, outer_weight)]
        keys["units"] = gather_rows(jnp.concatenate([parts[0], parts[1].T], 1))

    def feed_forward(i, gate):
        *saved, own, near, away, norms = call(
            functools.partial(ffn_kernel, i),
            "ffn",
            [*norm_three[i], *both_pieces, Far(after(keys["units"], *gate))],
            [
                far((half, features)),
                far((half, units)),
                far((half, units)),
                (piece, BF),
                *parts,
                far((half, features)),
            ],
            us=5.0,
            raw=2,
            lazy=True,
        )
        cot_half[i], hidden[i], active[i] = map(Far, saved)
        norms_three[i] = Far(norms)

        def finish(one, gate):
            grad_second[i], branch_two[i] = backward_pair(
                one, second[i], own, gain_three, gate
            )
            return branch_two[i][0]

        return near, away, finish

    def cross_backward(i, gate):
        last = i == order[-1]
        so_far = keys["grad"]
        grad_query_two[i], grad_kv, near, away, branch = call(
            functools.partial(
                cross_backward_kernel, size, i, len(probs_two[i]), len(so_far)
            ),
            "cross_backward",
            [
                dec_lengths,
                enc_lengths,
                *branch_two[i],
                Far(weights_two),
                query_two[i],
                Far(after(keys["kv"], *gate)),
                *probs_two[i],
                *so_far,
            ],
            [
                ((half, width), BF),
                ((enc_length, 2 * width), BF if last else F32),
                *parts,
                far((half, features)),
            ],
            [
                pltpu.VMEM((enc_length, 2 * width), F32),
                pltpu.VMEM((half, width), BF),
            ],
            us=8.0,
            smem=2,
            raw=2,
            lazy=True,
        )
        keys["grad"] = [grad_kv]
        branches_two[i] = Far(branch)

        def finish(one, gate):
            grad_after_self[i], branch_one[i] = backward_pair(
                one, after_self[i], grad_second[i], gain_two, gate
            )
            return branch_one[i][0]

        return near, away, finish

    def self_backward(i, gate):
        first = Far(after(qkv_one[i].array, *gate))
        grad_qkv_one[i], acc, *edge, branch = call(
            functools.partial(self_backward_kernel, size, i),
            "self_backward",
            [
                *branch_one[i],
                Far(weights_one),
                first,
                probs_one[i],
                qkv_one[0] if i else keys["edge"],
            ],
            [
                ((half, 3 * width), BF),
                ((heads, BLOCK, 2 * BLOCK), F32, "far"),
                *[((BLOCK, 2 * width), F32)] * i,
                far((half, features)),
            ],
            [
                pltpu.VMEM((half + BLOCK, 2 * width), BF),
                pltpu.VMEM((half + BLOCK, 2 * width), F32),
                pltpu.VMEM((half, width), BF),
            ],
            us=2.0,
            raw=2,
            lazy=True,
        )
        bias_acc[i], branches_one[i] = Far(acc), Far(branch)
        if edge:
            keys["edge"] = edge[0]
        return [grad_qkv_one[i]]

    def halves(left, right):
        return [(left[i], right[i]) for i in order]

    def make_keys(gate):
        keys["kv"], enc = call(
            functools.partial(cross_keys_kernel, width),
            "cross_keys",
            [*both_pieces, Far(after(weights_two, *gate))],
            [far((enc_length, 2 * width)), far((enc_length, features))],
            us=2.5,
            raw=4,
        )
        keys["enc"] = Far(enc)
        gather_units([keys["kv"]])
        return keys["kv"]

    def ffn_weights(gate):
        held = {i: Far(after(hidden[i].array, *gate)) for i in order}
        blocks = weight_blocks(
            [halves(norms_three, active), halves(cot_half, held)], 2 * units, features, 5.0
        )
        grads["ffn"] = exchange_rows(blocks)
        return blocks

    def layer_parts(gate):
        held = [hidden[0], Far(after(hidden[1].array, *gate))]
        layer = scatter_halves(held, keys["units"], units)
        grads["layer"] = own_of(second) + sum(part.astype(F32) for part in layer)
        grads["ffn"] = sum_rows(grads["ffn"])
        return key_parts([layer[0]])

    def cross_weights(gate):
        blocks = weight_blocks(
            [
                halves(norms_two, grad_query_two),
                [(keys["enc"], after(keys["grad"][0], *gate))],
                halves(branches_two, context_two),
            ],
            4 * width,
            features,
            4.0,
        )
        grads["cross"] = exchange_rows(after(blocks, grads["ffn"]))
        return blocks

    def key_parts(gate):
        key_parts = call(
            functools.partial(scatter_keys_kernel, width),
            "scatter_keys",
            [after(keys["grad"][0], *gate), Far(weights_two)],
            [(piece, F32), (piece, BF), (piece, F32), (piece, BF)],
            us=2.0,
        )
        across = send(chip_sum(key_parts[2], key_parts[3]), "heads", 2)
        grads["encoded"] = (
            key_parts[0] + send(key_parts[1], "heads", 1).astype(F32) + across.astype(F32)
        )
        return key_parts[0]

    keys = {"grad": [], "edge": []}
    grads = {}
    filler = {2: make_keys, 6: ffn_weights, 8: cross_weights, 9: layer_parts}
    stages = [self_forward, cross_forward, feed_forward, cross_backward, self_backward]
    gate, pending, step = [], None, 0
    for stage in stages:
        for i in order:
            result = stage(i, gate)
            gate = [result[0]]
            step += 1
            if step in filler:
                gate = [filler[step](gate)]
            if pending:
                gate = [pending[0](pending[1], gate)]
                pending = None
            if stage is self_backward:
                continue
            near, away, finish = result
            one = chip_sum(after(near, *gate), away)
            gate = [one]
            pending = (finish, one)
    self_blocks = weight_blocks(
        [halves(norm_one, grad_qkv_one), halves(branches_one, context_one)],
        4 * width,
        features,
        4.0,
    )
    self_got = exchange_rows(
        after(self_blocks, grads["cross"], grads["encoded"], grads["layer"], grads["ffn"])
    )
    input_parts = scatter_halves(
        [after(grad_qkv_one[0], self_blocks), grad_qkv_one[1]], weights_one, 0
    )
    (input_grad,) = backward_norm(
        input_parts,
        inputs,
        own_of(grad_after_self),
        gain_one,
        branch=False,
    )
    cross_grad, self_grad = sum_rows(grads["cross"]), sum_rows(self_got)
    ffn_grad = grads["ffn"]

    bias_sums = call(
        functools.partial(bias_grad_kernel, starts),
        "bias_grad",
        [Far(after(bias_acc[0].array, input_parts[2])), bias_acc[1]],
        [((heads, buckets, 2 * BLOCK), F32)],
        us=2.0,
    )[0]
    bias_grad = jnp.sum(bias_sums, axis=-1)
    bits = 1
    while bits < lax.axis_size("rows"):
        bias_grad = bias_grad + send(bias_grad, "rows", bits)
        bits *= 2

    def along(weights, gradient):
        return jnp.sum(
            jnp.concatenate([w.astype(F32) for w in weights], 1) * gradient, axis=1
        )

    gain_grads = jnp.stack(
        [
            along([self_query, self_key, self_value], self_grad[:, : 3 * width]),
            along([cross_query], cross_grad[:, :width]),
            along([inner_weight], ffn_grad[:, :units]),
        ]
    )
    for bits in (1, 2):
        gain_grads = gain_grads + send(gain_grads, "heads", bits)
    gain_grads = lax.dynamic_slice_in_dim(gain_grads, me * each, each, 1) / jnp.stack(
        [gain_first, gain_second, gain_third]
    ).astype(F32)

    return (
        grads["layer"].astype(BF)[None],
        input_grad[None],
        grads["encoded"][None],
        self_grad[:, :width],
        self_grad[:, width : 2 * width],
        self_grad[:, 2 * width : 3 * width],
        self_grad[:, 3 * width :].T,
        cross_grad[:, :width],
        cross_grad[:, width : 2 * width],
        cross_grad[:, 2 * width : 3 * width],
        cross_grad[:, 3 * width :].T,
        ffn_grad[:, :units],
        ffn_grad[:, units:].T,
        bias_grad.T,
        gain_grads[0],
        gain_grads[1],
        gain_grads[2],
    )


def solution(mesh):
    positions = P("rows", "heads", None)
    columns = P("rows", "heads")
    lines = P("heads", "rows")
    gains = P(("rows", "heads"))
    return jax.shard_map(
        shards,
        mesh=mesh,
        in_specs=(
            positions,
            positions,
            positions,
            P("rows", None),
            P("rows", None),
            columns,
            columns,
            columns,
            lines,
            columns,
            columns,
            columns,
            lines,
            columns,
            lines,
            P(None, "heads"),
            gains,
            gains,
            gains,
        ),
        out_specs=(
            positions,
            positions,
            positions,
            columns,
            columns,
            columns,
            lines,
            columns,
            columns,
            columns,
            lines,
            columns,
            lines,
            P(None, "heads"),
            gains,
            gains,
            gains,
        ),
        check_vma=False,
    )
```

```python
import functools

import jax
import jax.numpy as jnp
import numpy as np
from jax import lax
from jax.experimental import pallas as pl
from jax.experimental.pallas import tpu as pltpu
from jax.sharding import PartitionSpec as P

MAX_DISTANCE = 128
EPS = 1e-06
NEG = -1000000000.0
LEAST = 96
MOST = 128
BLOCK = 128
BF = jnp.bfloat16
F32 = jnp.float32
VMEM = pl.BlockSpec(memory_space=pltpu.VMEM)
SMEM = pl.BlockSpec(memory_space=pltpu.SMEM)


def bucket_starts(bucket_count, max_reach):
    exact_span = bucket_count // 2
    starts = list(range(exact_span + 1))
    for target in range(exact_span + 1, bucket_count):
        distance = exact_span
        while (
            distance < max_reach
            and exact_span
            + int(
                np.log(distance / exact_span)
                / np.log(max_reach / exact_span)
                * (bucket_count - exact_span)
            )
            < target
        ):
            distance += 1
        starts.append(distance)
    return starts


COST = {}


class Far:
    def __init__(self, array):
        self.array = array


class Moves:
    def __init__(self, sems):
        self.sems, self.used = sems, 0
        self.coming, self.going, self.started = [], [], []

    def copy(self, source, target):
        made = pltpu.make_async_copy(source, target, self.sems.at[self.used])
        self.used += 1
        made.start()
        return made

    def need(self, *refs):
        for ref in refs:
            for k, (held, made) in enumerate(self.coming):
                if held is ref:
                    made.wait()
                    del self.coming[k]
                    break

    def need_all(self):
        self.need(*[held for held, made in self.coming])

    def send(self, source, target):
        self.started.append(self.copy(source, target))

    def ready(self, *refs):
        for ref in refs:
            for k, (held, target) in enumerate(self.going):
                if held is ref:
                    self.send(held, target)
                    del self.going[k]
                    break

    def finish(self):
        self.need_all()
        self.ready(*[held for held, target in self.going])
        for made in self.started:
            made.wait()


HBM = pl.BlockSpec(memory_space=pltpu.HBM)


def call(body, name, args, outs, scratch=(), us=2.0, smem=0, raw=0, moved=0, lazy=False, fetch=False, key=None):
    far_in = [fetch and isinstance(x, Far) for x in args]
    arrays = [
        pltpu.with_memory_space_constraint(x.array, pltpu.HBM)
        if f
        else x.array
        if isinstance(x, Far)
        else x
        for x, f in zip(args, far_in)
    ]
    far_out = [len(o) > 2 for o in outs]
    last = len(outs) - (raw > 0)
    held = [pltpu.VMEM(x.shape, x.dtype) for x, f in zip(arrays, far_in) if f]
    held += [pltpu.VMEM(o[0], o[1]) for o, f in zip(outs[:last], far_out) if f]
    copies = len(held) + raw + moved
    if copies:
        held.append(pltpu.SemaphoreType.DMA((copies,)))

    def kernel(*refs):
        ins, results = refs[: len(args)], refs[len(args) : len(args) + len(outs)]
        own = refs[len(args) + len(outs) : len(args) + len(outs) + len(scratch)]
        spare = list(refs[len(args) + len(outs) + len(scratch) :])
        moves = Moves(spare.pop() if copies else None)
        given = []
        for ref, f in zip(ins, far_in):
            if f:
                here = spare.pop(0)
                moves.coming.append((here, moves.copy(ref, here)))
                ref = here
            given.append(ref)
        for k, ref in enumerate(results):
            if far_out[k] and k < last:
                here = spare.pop(0)
                moves.going.append((here, ref))
                ref = here
            given.append(ref)
        if not lazy:
            moves.need_all()
        body(moves, *given, *own)
        moves.finish()

    return pl.pallas_call(
        kernel,
        out_shape=[
            (pltpu.HBM if f else jax.ShapeDtypeStruct)(o[0], o[1])
            for o, f in zip(outs, far_out)
        ],
        in_specs=[SMEM] * smem + [HBM if f else VMEM for f in far_in[smem:]],
        out_specs=[HBM if f else VMEM for f in far_out],
        scratch_shapes=list(scratch) + held,
        compiler_params=pltpu.CompilerParams(vmem_limit_bytes=16 << 20),
        name=name,
        cost_estimate=pl.CostEstimate(
            flops=int(COST.get(key or name, us) * 1e9),
            bytes_accessed=int(COST.get(key or name, us) * 3e6),
            transcendentals=0,
        ),
    )(*arrays)


def send(part, axis, bits):
    count = lax.axis_size(axis)
    return lax.ppermute(part, axis, [(i, i ^ bits) for i in range(count)])


def after(value, *others):
    return lax.optimization_barrier((value,) + others)[0]


def gather_heads(part):
    across = send(part, "heads", 2)
    return [part, send(part, "heads", 1), across, send(across, "heads", 1)]


def place_kernel(count, moves, *refs):
    me = lax.axis_index("rows")
    for t in range(count):
        moves.send(refs[t], refs[count].at[me ^ t])


def pair_kernel(moves, near, other, out):
    lower = lax.axis_index("rows") % 2
    moves.send(near, out.at[:, lower])
    moves.send(other, out.at[:, 1 - lower])


def gather_rows_first(part):
    return [part] + [
        send(part, "rows", 2 * upper) for upper in range(1, lax.axis_size("rows") // 2)
    ]


def gather_rows_second(firsts):
    pieces = []
    for near in firsts:
        pieces += [near, send(near, "rows", 1)]
    return pieces


def lay_rows(pieces, *others):
    count = len(pieces)
    shape = (count,) + pieces[0].shape
    pieces = [after(pieces[0], *others)] + pieces[1:]
    placed = call(
        functools.partial(place_kernel, count), "place", pieces, [(shape, BF)], us=1.5, moved=count
    )[0]
    return placed.reshape(-1, shape[2])


def upper_groups():
    count = lax.axis_size("rows")
    return [list(range(lower, count, 2)) for lower in range(2)]


def gather_rows_upper(part):
    count = lax.axis_size("rows") // 2
    spread = jnp.broadcast_to(part[None], (count,) + part.shape)
    return lax.all_to_all(
        spread, "rows", 0, 0, tiled=True, axis_index_groups=upper_groups()
    )


def gather_rows_lower(near):
    count, rows, lanes = near.shape
    placed = call(
        pair_kernel,
        "pair",
        [near, send(near, "rows", 1)],
        [((count, 2, rows, lanes), BF)],
        us=1.5,
        moved=2,
    )[0]
    return placed.reshape(-1, lanes)


def scatter_rows_lower(keep, away):
    return (keep.astype(F32) + send(away, "rows", 1).astype(F32)).astype(BF)


def scatter_rows_upper(blocks):
    return lax.all_to_all(blocks, "rows", 0, 0, tiled=True, axis_index_groups=upper_groups())


def sum_rows(got):
    return jnp.sum(got.astype(F32), axis=0)


def dot(a, b, dims):
    return lax.dot_general(a, b, (dims, ((), ())), preferred_element_type=F32)


NT = ((1,), (1,))
NN = ((1,), (0,))
TN = ((0,), (0,))


def core_and_chip():
    me = lax.axis_index("heads")
    return me % 2, me // 2


def rms_rows(values, gain):
    factor = lax.rsqrt(jnp.mean(values * values, axis=-1, keepdims=True) + EPS)
    return (values * factor * gain).astype(BF)


def pick_half(half, pieces, out):
    unused, chip = core_and_chip()
    quarter = pieces[0].shape[0]
    for near in (True, False):

        @pl.when((chip == half) == near)
        def _(near=near):
            for s in range(2):
                out[s * quarter : (s + 1) * quarter, :] = pieces[s + (0 if near else 2)][...]


def distances(first, rows):
    query = lax.broadcasted_iota(jnp.int32, (rows, 2 * BLOCK), 0) + (first + BLOCK)
    return query - lax.broadcasted_iota(jnp.int32, (rows, 2 * BLOCK), 1)


def bias_kernel(starts, moves, table_ref, out_ref):
    heads = out_ref.shape[0]
    step = 32

    def rows(t, carry):
        first = pl.multiple_of(t * step, step)
        reach = distances(first, step)
        values = [jnp.full((step, 2 * BLOCK), table_ref[0, h], F32) for h in range(heads)]
        for b in range(1, len(starts)):
            beyond = reach >= starts[b]
            values = [jnp.where(beyond, table_ref[b, h], values[h]) for h in range(heads)]
        for h in range(heads):
            out_ref[h, pl.ds(first, step), :] = values[h]
        return carry

    lax.fori_loop(0, BLOCK // step, rows, 0)


def bias_grad_kernel(moves, edges_ref, one_ref, two_ref, out_ref):
    reach = distances(0, BLOCK)
    reach = jnp.maximum(reach, 0)
    for h in range(one_ref.shape[0]):
        one_ref[h] += two_ref[h]

    def bucket(b, carry):
        inside = (reach >= edges_ref[b]) & (reach < edges_ref[b + 1])
        for h in range(one_ref.shape[0]):
            out_ref[h, pl.ds(b, 1), :] = jnp.sum(
                jnp.where(inside, one_ref[h], 0.0), axis=0, keepdims=True
            )
        return carry

    lax.fori_loop(0, out_ref.shape[1], bucket, 0)


def running(lengths_ref, count):
    total = lengths_ref[0, 0]
    ends = [total]
    for c in range(1, count):
        total = total + lengths_ref[0, c]
        ends.append(total)
    return ends


def slot_of(block, core, quarter):
    each = quarter // BLOCK
    return pl.multiple_of((((block // each) ^ core) * each + block % each) * BLOCK, BLOCK)


def softmax(scores):
    e = jnp.exp(scores - jnp.max(scores, axis=-1, keepdims=True))
    return (e * (1.0 / jnp.sum(e, axis=-1, keepdims=True))).astype(BF)


def self_forward_kernel(size, half, moves, lengths_ref, *refs):
    pieces = refs[:4]
    gain_ref, w_ref, bias_ref = refs[4:7]
    norm_ref, qkv_ref, context_ref, probs_ref, own_ref, near_ref, far_ref = refs[7:14]
    x, kv = refs[14:]
    heads = bias_ref.shape[0]
    width = heads * size
    quarter = own_ref.shape[0]
    core, chip = core_and_chip()
    ends = running(lengths_ref, lengths_ref.shape[1])
    blocks = 2 * quarter // BLOCK
    gain = gain_ref[...]
    pick_half(half, pieces, x)
    own_ref[...] = x[:quarter, :]
    moves.need(w_ref)

    if half:
        for k in range(4):

            @pl.when((core == 1 - k % 2) & ((chip == 0) == (k < 2)))
            def _(k=k):
                norm_ref[:BLOCK, :] = pieces[k][quarter - BLOCK :, :]

        before = rms_rows(norm_ref[:BLOCK, :].astype(F32), gain)
        kv[:BLOCK, :] = dot(before, w_ref[:, width : 3 * width], NN).astype(BF)
    else:
        kv[:BLOCK, :] = jnp.zeros((BLOCK, 2 * width), BF)

    def project(b, carry):
        at = pl.multiple_of(slot_of(b, core, quarter), BLOCK)
        norm = rms_rows(x[pl.ds(at, BLOCK), :].astype(F32), gain)
        norm_ref[pl.ds(at, BLOCK), :] = norm
        qkv = dot(norm, w_ref[:, : 3 * width], NN).astype(BF)
        qkv_ref[pl.ds(at, BLOCK), :] = qkv
        kv[pl.ds(pl.multiple_of((b + 1) * BLOCK, BLOCK), BLOCK), :] = qkv[:, width:]
        return carry

    lax.fori_loop(0, blocks, project, 0)
    moves.ready(norm_ref, qkv_ref)
    moves.need(bias_ref)

    def block(b, carry):
        own = slot_of(b, core, quarter)
        at = pl.multiple_of(b * BLOCK, BLOCK)
        base = (half * blocks + b) * BLOCK
        query = base + lax.broadcasted_iota(jnp.int32, (BLOCK, 1), 0)
        start = jnp.zeros((BLOCK, 1), jnp.int32)
        for end in ends:
            start = jnp.where(query >= end, end, start)
        key = base - BLOCK + lax.broadcasted_iota(jnp.int32, (BLOCK, 2 * BLOCK), 1)
        allowed = (key >= start) & (key <= query)
        outs = []
        for h in range(heads):
            q = qkv_ref[pl.ds(own, BLOCK), h * size : (h + 1) * size]
            k = kv[pl.ds(at, 2 * BLOCK), h * size : (h + 1) * size]
            v = kv[pl.ds(at, 2 * BLOCK), width + h * size : width + (h + 1) * size]
            probs = softmax(jnp.where(allowed, dot(q, k, NT) + bias_ref[h], NEG))
            probs_ref[b, h] = probs
            outs.append(dot(probs, v, NN).astype(BF))
        context_ref[pl.ds(own, BLOCK), :] = jnp.concatenate(outs, 1)
        return carry

    lax.fori_loop(0, blocks, block, 0)
    moves.ready(context_ref, probs_ref)
    out_weight = w_ref[:, 3 * width : 4 * width]
    far_ref[...] = dot(context_ref[quarter:, :], out_weight, NT).astype(BF)
    near_ref[...] = dot(context_ref[:quarter, :], out_weight, NT).astype(BF)


def self_backward_kernel(size, half, moves, *refs):
    own_ref, other_ref, w_ref, qkv_ref, probs_ref, edge_in = refs[:6]
    out_ref, acc_ref = refs[6:8]
    branch_ref = refs[-4]
    kv, key_acc, grad = refs[-3:]
    heads = acc_ref.shape[0]
    width = heads * size
    quarter = own_ref.shape[0]
    core, chip = core_and_chip()
    blocks = 2 * quarter // BLOCK
    moves.send(own_ref, branch_ref.at[:quarter])
    moves.send(other_ref, branch_ref.at[quarter:])
    key_acc[...] = jnp.zeros_like(key_acc)
    acc_ref[...] = jnp.zeros_like(acc_ref)
    moves.need(w_ref)
    out_weight = w_ref[:, 3 * width : 4 * width]
    grad[:quarter, :] = dot(own_ref[...], out_weight, NN).astype(BF)
    grad[quarter:, :] = dot(other_ref[...], out_weight, NN).astype(BF)
    moves.need(edge_in, qkv_ref)
    if half:
        kv[:BLOCK, :] = edge_in[pl.ds(slot_of(blocks - 1, core, quarter), BLOCK), width:]
    else:
        kv[:BLOCK, :] = jnp.zeros((BLOCK, 2 * width), BF)
        key_acc[:, blocks * BLOCK :] = edge_in[...]
    for b in range(blocks):
        kv[(b + 1) * BLOCK : (b + 2) * BLOCK, :] = qkv_ref[
            pl.ds(slot_of(b, core, quarter), BLOCK), width:
        ]
    moves.need(probs_ref)

    def block(b, carry):
        own = slot_of(b, core, quarter)
        at = pl.multiple_of(b * BLOCK, BLOCK)
        grads_q, grads_k, grads_v = [], [], []
        for h in range(heads):
            q = qkv_ref[pl.ds(own, BLOCK), h * size : (h + 1) * size]
            k = kv[pl.ds(at, 2 * BLOCK), h * size : (h + 1) * size]
            v = kv[pl.ds(at, 2 * BLOCK), width + h * size : width + (h + 1) * size]
            c = grad[pl.ds(own, BLOCK), h * size : (h + 1) * size]
            probs = probs_ref[b, h]
            wide = probs.astype(F32)
            grad_probs = dot(c, v, NT)
            inner = jnp.sum(grad_probs * wide, axis=-1, keepdims=True)
            grad_scores = wide * (grad_probs - inner)
            acc_ref[h] += grad_scores
            short = grad_scores.astype(BF)
            grads_q.append(dot(short, k, NN).astype(BF))
            grads_k.append(dot(q.T, short, NN))
            grads_v.append(dot(c.T, probs, NN))
        out_ref[pl.ds(own, BLOCK), :width] = jnp.concatenate(grads_q, 1)
        key_acc[:, pl.ds(at, 2 * BLOCK)] += jnp.concatenate(grads_k + grads_v, 0)
        return carry

    lax.fori_loop(0, blocks, block, 0)
    for b in range(blocks):
        out_ref[pl.ds(slot_of(b, core, quarter), BLOCK), width:] = key_acc[
            :, (b + 1) * BLOCK : (b + 2) * BLOCK
        ].T.astype(BF)
    if half:
        refs[8][...] = key_acc[:, :BLOCK]


def cross_keys_kernel(width, moves, *refs):
    pieces, w_ref = refs[:4], refs[4]
    kv_ref, enc_ref = refs[5:]
    quarter = pieces[0].shape[1]
    me = lax.axis_index("heads")
    weight = w_ref[:, width : 3 * width]
    for k in range(4):
        at = pl.ds(pl.multiple_of((me ^ k) * quarter, quarter), quarter)
        moves.send(pieces[k].at[0], enc_ref.at[at])
        kv_ref[at, :] = dot(pieces[k][0], weight, NN).astype(BF)


def cross_window(block, dec_ends, enc_ends, enc_length, window):
    first = jnp.int32(0)
    for c in range(len(dec_ends) - 1):
        first = jnp.where(block * BLOCK >= dec_ends[c], enc_ends[c], first)
    return pl.multiple_of(
        jnp.minimum(first // BLOCK * BLOCK, enc_length - window), BLOCK
    )


def cross_forward_kernel(size, half, moves, dec_ref, enc_ref, own_ref, other_ref, w_ref, kv_ref, *refs):
    query_ref, context_ref, near_ref, far_ref = refs[:4]
    all_probs, norm_ref = refs[4:-1], refs[-1]
    heads = refs[4].shape[1]
    width = heads * size
    quarter = own_ref.shape[0]
    core, chip = core_and_chip()
    first = half * (2 * quarter // BLOCK)
    enc_length = kv_ref.shape[0]
    comments = dec_ref.shape[1]
    dec_ends = running(dec_ref, comments)
    enc_ends = running(enc_ref, comments)
    moves.send(own_ref, norm_ref.at[:quarter])
    moves.send(other_ref, norm_ref.at[quarter:])
    moves.need(w_ref)
    query_ref[:quarter, :] = dot(own_ref[...], w_ref[:, :width], NN).astype(BF)
    query_ref[quarter:, :] = dot(other_ref[...], w_ref[:, :width], NN).astype(BF)
    moves.ready(query_ref)
    moves.need(kv_ref)
    done = 0
    for probs_ref in all_probs:
        window = probs_ref.shape[3]

        def block(b, carry, window=window, probs_ref=probs_ref, done=done):
            own = slot_of(b, core, quarter)
            base = (first + b) * BLOCK
            start = (
                cross_window(first + b, dec_ends, enc_ends, enc_length, window)
                if window < enc_length
                else 0
            )
            query = base + lax.broadcasted_iota(jnp.int32, (BLOCK, 1), 0)
            low = jnp.zeros((BLOCK, 1), jnp.int32)
            high = jnp.full((BLOCK, 1), enc_ends[0], jnp.int32)
            for c in range(comments):
                later = query >= dec_ends[c]
                last = c == comments - 1
                low = jnp.where(later, 0 if last else enc_ends[c], low)
                high = jnp.where(later, enc_length if last else enc_ends[c + 1], high)
            key = start + lax.broadcasted_iota(jnp.int32, (BLOCK, window), 1)
            allowed = (key >= low) & (key < high)
            contexts = []
            for h in range(heads):
                q = query_ref[pl.ds(own, BLOCK), h * size : (h + 1) * size]
                k = kv_ref[pl.ds(start, window), h * size : (h + 1) * size]
                v = kv_ref[pl.ds(start, window), width + h * size : width + (h + 1) * size]
                probs = softmax(jnp.where(allowed, dot(q, k, NT), NEG))
                probs_ref[b - done, h] = probs
                contexts.append(dot(probs, v, NN).astype(BF))
            context_ref[pl.ds(own, BLOCK), :] = jnp.concatenate(contexts, 1)
            return carry

        lax.fori_loop(done, done + probs_ref.shape[0], block, 0)
        done += probs_ref.shape[0]
        moves.ready(probs_ref)
    moves.ready(context_ref)
    out_weight = w_ref[:, 3 * width :]
    far_ref[...] = dot(context_ref[quarter:, :], out_weight, NT).astype(BF)
    near_ref[...] = dot(context_ref[:quarter, :], out_weight, NT).astype(BF)


def cross_backward_kernel(size, half, kinds, more, moves, dec_ref, enc_ref, *refs):
    own_ref, other_ref, w_ref, query_ref, kv_ref = refs[:5]
    probs_refs = refs[5 : 5 + kinds]
    so_far = refs[5 + kinds : 5 + kinds + more]
    grad_q_ref, grad_kv_ref, near_ref, far_ref, branch_ref, key_acc, grad = refs[5 + kinds + more :]
    heads = probs_refs[0].shape[1]
    width = heads * size
    quarter = own_ref.shape[0]
    core, chip = core_and_chip()
    first = half * (2 * quarter // BLOCK)
    enc_length = kv_ref.shape[0]
    comments = dec_ref.shape[1]
    dec_ends = running(dec_ref, comments)
    enc_ends = running(enc_ref, comments)
    moves.send(own_ref, branch_ref.at[:quarter])
    moves.send(other_ref, branch_ref.at[quarter:])
    key_acc[...] = so_far[0][...] if more else jnp.zeros_like(key_acc)
    moves.need(w_ref)
    out_weight = w_ref[:, 3 * width :]
    grad[:quarter, :] = dot(own_ref[...], out_weight, NN).astype(BF)
    grad[quarter:, :] = dot(other_ref[...], out_weight, NN).astype(BF)
    moves.need(query_ref, kv_ref)
    done = 0
    for probs_ref in probs_refs:
        moves.need(probs_ref)
        window = probs_ref.shape[3]

        def block(b, carry, window=window, probs_ref=probs_ref, done=done):
            own = slot_of(b, core, quarter)
            start = (
                cross_window(first + b, dec_ends, enc_ends, enc_length, window)
                if window < enc_length
                else 0
            )
            grads_q, grads_k, grads_v = [], [], []
            for h in range(heads):
                q = query_ref[pl.ds(own, BLOCK), h * size : (h + 1) * size]
                k = kv_ref[pl.ds(start, window), h * size : (h + 1) * size]
                v = kv_ref[pl.ds(start, window), width + h * size : width + (h + 1) * size]
                c = grad[pl.ds(own, BLOCK), h * size : (h + 1) * size]
                probs = probs_ref[b - done, h]
                wide = probs.astype(F32)
                grad_probs = dot(c, v, NT)
                inner = jnp.sum(grad_probs * wide, axis=-1, keepdims=True)
                short = (wide * (grad_probs - inner)).astype(BF)
                grads_q.append(dot(short, k, NN).astype(BF))
                grads_k.append(dot(q.T, short, NN))
                grads_v.append(dot(c.T, probs, NN))
            grad_q_ref[pl.ds(own, BLOCK), :] = jnp.concatenate(grads_q, 1)
            key_acc[:, pl.ds(start, window)] += jnp.concatenate(grads_k + grads_v, 0)
            return carry

        lax.fori_loop(done, done + probs_ref.shape[0], block, 0)
        done += probs_ref.shape[0]
    grad_kv_ref[...] = (key_acc[...].T if more else key_acc[...]).astype(grad_kv_ref.dtype)
    weight = w_ref[:, :width]
    far_ref[...] = dot(grad_q_ref[quarter:, :], weight, NT).astype(BF)
    near_ref[...] = dot(grad_q_ref[:quarter, :], weight, NT).astype(BF)


def ffn_kernel(half, moves, own_ref, other_ref, *refs):
    pieces, w_ref = refs[:4], refs[4]
    cot_ref, hidden_ref, active_ref, own_cot_ref, near_ref, far_ref, norms_ref, norms = refs[5:]
    quarter = own_ref.shape[0]
    units = hidden_ref.shape[1]
    part = 256 if units % 256 == 0 else units
    moves.send(own_ref, norms_ref.at[:quarter])
    moves.send(other_ref, norms_ref.at[quarter:])
    pick_half(half, [part.at[1] for part in pieces], cot_ref)
    own_cot_ref[...] = cot_ref[:quarter, :]
    moves.ready(cot_ref)
    moves.need(w_ref)
    norms[:quarter, :] = own_ref[...]
    norms[quarter:, :] = other_ref[...]

    def rows(t, carry):
        at = pl.ds(pl.multiple_of(t * BLOCK, BLOCK), BLOCK)
        norm = norms[at, :]
        cot = cot_ref[at, :]
        for f in range(0, units, part):
            active = dot(norm, w_ref[:, f : f + part], NN)
            grad = dot(cot, w_ref[:, units + f : units + f + part], NN)
            share = 0.5 + 0.5 * lax.erf(active * np.float32(np.sqrt(0.5)))
            slope = share + active * (
                jnp.exp(-0.5 * active * active) * np.float32(1.0 / np.sqrt(2.0 * np.pi))
            )
            hidden_ref[at, f : f + part] = (active * share).astype(BF)
            active_ref[at, f : f + part] = (grad * slope).astype(BF)
        return carry

    lax.fori_loop(0, 2 * quarter // BLOCK, rows, 0)
    moves.ready(hidden_ref, active_ref)
    weight = w_ref[:, :units]
    far_ref[...] = dot(active_ref[quarter:, :], weight, NT).astype(BF)
    near_ref[...] = dot(active_ref[:quarter, :], weight, NT).astype(BF)


def scatter_kernel(first, moves, one_ref, two_ref, w_ref, far_far, far_near, near_far, near_near, picked):
    unused, chip = core_and_chip()
    quarter = far_far.shape[0]
    weight = w_ref[:, first : first + one_ref.shape[1]]
    for index in range(2):

        @pl.when(chip == index)
        def _(index=index):
            picked[0] = (two_ref, one_ref)[index][...]
            picked[1] = (one_ref, two_ref)[index][...]

    far_far[...] = dot(picked[0, quarter:, :], weight, NT).astype(BF)
    near_far[...] = dot(picked[1, quarter:, :], weight, NT).astype(BF)
    far_near[...] = dot(picked[0, :quarter, :], weight, NT).astype(BF)
    near_near[...] = dot(picked[1, :quarter, :], weight, NT).astype(BF)


def scatter_keys_kernel(width, moves, grad_ref, w_ref, *outs):
    quarter = outs[0].shape[0]
    me = lax.axis_index("heads")
    weight = w_ref[:, width : 3 * width]
    for k in range(4):
        at = pl.ds(pl.multiple_of((me ^ k) * quarter, quarter), quarter)
        outs[k][...] = dot(grad_ref[at, :], weight, NT).astype(outs[k].dtype)


def norm_forward_kernel(moves, one_ref, two_ref, base_ref, gain_ref, sum_ref, norm_ref):
    rows = base_ref.shape[0]
    step = min(64, rows)

    def some(t, carry):
        at = pl.ds(pl.multiple_of(t * step, step), step)
        total = base_ref[at, :].astype(F32) + one_ref[at, :].astype(F32) + two_ref[at, :].astype(F32)
        sum_ref[at, :] = total
        norm_ref[at, :] = rms_rows(total, gain_ref[...])
        return carry

    lax.fori_loop(0, rows // step, some, 0)


def norm_backward_kernel(parts, moves, *refs):
    values_ref, base_ref, gain_ref = refs[parts : parts + 3]
    grad_ref, *branch_ref = refs[parts + 3 :]
    rows = values_ref.shape[0]
    step = min(64, rows)

    def some(t, carry):
        at = pl.ds(pl.multiple_of(t * step, step), step)
        grad = refs[0][at, :].astype(F32)
        for part in refs[1:parts]:
            grad = grad + part[at, :].astype(F32)
        values = values_ref[at, :].astype(F32)
        factor = lax.rsqrt(jnp.mean(values * values, axis=-1, keepdims=True) + EPS)
        scaled = gain_ref[...] * grad
        mean = jnp.mean(scaled * values, axis=-1, keepdims=True)
        total = (
            base_ref[at, :].astype(F32)
            + factor * scaled
            - values * (factor * factor * factor * mean)
        )
        grad_ref[at, :] = total
        if branch_ref:
            branch_ref[0][at, :] = total.astype(BF)
        return carry

    lax.fori_loop(0, rows // step, some, 0)


def weights_kernel(segments, moves, *refs):
    keep_ref, away_ref, whole = refs[-3:]
    features = whole.shape[0]
    group = keep_ref.shape[1]
    lower = lax.axis_index("rows") % 2
    step = 384 if features % 384 == 0 else BLOCK
    to = 0
    for pairs in segments:
        for left, right in pairs:
            moves.need(refs[left], refs[right])
        lanes = refs[pairs[0][1]].shape[1]

        def rows(j, carry, pairs=pairs, to=to, lanes=lanes):
            at = pl.ds(pl.multiple_of(j * step, step), step)
            total = sum(dot(refs[left][:, at], refs[right][...], TN) for left, right in pairs)
            whole[at, to : to + lanes] = total.astype(BF)
            return carry

        lax.fori_loop(0, features // step, rows, 0)
        to += lanes
    for r in range(features // group):
        block = slice(r * group, (r + 1) * group)

        @pl.when(lower == r % 2)
        def _(r=r, block=block):
            keep_ref[r // 2] = whole[block, :]

        @pl.when(lower != r % 2)
        def _(r=r, block=block):
            away_ref[r // 2] = whole[block, :]


def weight_blocks(segments, lanes, features, key):
    operands, index = [], {}

    def number(operand):
        key = id(operand.array if isinstance(operand, Far) else operand)
        if key not in index:
            index[key] = len(operands)
            operands.append(operand)
        return index[key]

    numbered = [[(number(l), number(r)) for l, r in pairs] for pairs in segments]
    count = lax.axis_size("rows")
    return call(
        functools.partial(weights_kernel, numbered),
        "weights",
        operands,
        [((count // 2, features // count, lanes), BF)] * 2,
        [pltpu.VMEM((features, lanes), BF)],
        us=4.0,
        key=key,
        lazy=True,
        fetch=True,
    )


def shards(
    inputs,
    encoded,
    cotangent,
    dec_lengths,
    enc_lengths,
    self_query,
    self_key,
    self_value,
    self_output,
    cross_query,
    cross_key,
    cross_value,
    cross_output,
    inner_weight,
    outer_weight,
    bias_table,
    gain_first,
    gain_second,
    gain_third,
):
    groups = lax.axis_size("heads")
    devices = groups * lax.axis_size("rows")
    me = lax.axis_index("heads")
    chip = me // 2
    heads = bias_table.shape[1]
    buckets = bias_table.shape[0]
    width = self_query.shape[1]
    size = width // heads
    quarter = inputs.shape[1]
    half = 2 * quarter
    enc_quarter = encoded.shape[1]
    enc_length = enc_quarter * groups
    features = inputs.shape[2]
    units = inner_weight.shape[1]
    comments = dec_lengths.shape[1]
    starts = bucket_starts(buckets, MAX_DISTANCE)
    blocks = half // BLOCK
    window = 4 * MOST
    order = (1, 0)
    plain = [min(max(LEAST * comments // BLOCK - i * blocks, 0), blocks) for i in range(2)]
    piece = (quarter, features)

    inputs, encoded, cotangent = inputs[0], encoded[0], cotangent[0]

    gains = jnp.concatenate([gain_first, gain_second, gain_third])
    each = gain_first.shape[0]
    spread = jnp.broadcast_to(gains[None], (devices, 3 * each))
    spread = lax.all_to_all(spread, ("rows", "heads"), 0, 0, tiled=True).astype(F32)
    gain_one, gain_two, gain_three = (
        spread[:, i * each : (i + 1) * each].reshape(1, features) for i in range(3)
    )

    far = lambda shape: (shape, BF, "far")
    bias = call(
        functools.partial(bias_kernel, starts),
        "bias",
        [bias_table.astype(F32)],
        [((heads, BLOCK, 2 * BLOCK), F32, "far")],
        us=2.0,
        smem=1,
    )[0]

    weights_one = gather_rows_first(
        jnp.concatenate([self_query, self_key, self_value, self_output.T], 1)
    )
    inputs_pieces = gather_heads(inputs)
    pieces_one = gather_rows_second(
        weights_one[:1] + [after(part, inputs_pieces[2]) for part in weights_one[1:]]
    )
    parts_two = [
        after(part, *weights_one)
        for part in (cross_query, cross_key, cross_value, cross_output)
    ]
    weights_one = lay_rows(pieces_one, spread, bias)
    weights_two = gather_rows_upper(jnp.concatenate(parts_two[:3] + [parts_two[3].T], 1))
    parts_three = [after(part, weights_two) for part in (inner_weight, outer_weight)]
    weights_three = gather_rows_upper(jnp.concatenate([parts_three[0], parts_three[1].T], 1))
    weights_two = gather_rows_lower(weights_two)
    weights_three = gather_rows_lower(weights_three)
    both_pieces = gather_heads(after(jnp.stack([encoded, cotangent]), inputs_pieces[2]))

    def chip_sum(near, far):
        return (near.astype(F32) + send(far, "heads", 1).astype(F32)).astype(BF)

    def forward_norm(one, base, gain, gate):
        total, norm = call(
            norm_forward_kernel,
            "norm_forward",
            [one, send(one, "heads", 2), base, after(gain, *gate)],
            [(piece, F32, "far"), (piece, BF)],
            us=1.0,
        )
        return Far(total), (norm, send(norm, "heads", 1))

    def backward_norm(parts, values, base, gain, branch=True):
        return call(
            functools.partial(norm_backward_kernel, len(parts)),
            "norm_backward",
            [*parts, values, base, gain],
            [(piece, F32)] + [(piece, BF)] * branch,
            us=1.5,
            key="norm_backward" if branch else "input_norm",
        )

    def backward_pair(one, values, base, gain, gate):
        grad, branch = backward_norm(
            [one, send(one, "heads", 2)], values, base, after(gain, *gate)
        )
        return grad, (branch, send(branch, "heads", 1))

    def own_of(pair):
        return jnp.where(chip == 0, *(x.array if isinstance(x, Far) else x for x in pair))

    def scatter_halves(pair, weight, first, key):
        far_far, far_near, near_far, near_near = call(
            functools.partial(scatter_kernel, first),
            "scatter",
            [pair[0], pair[1], Far(weight)],
            [(piece, BF)] * 4,
            [pltpu.VMEM((2, half, (pair[0].array if isinstance(pair[0], Far) else pair[0]).shape[1]), BF)],
            us=2.0,
            key=key,
        )
        across = send(chip_sum(far_near, far_far), "heads", 2)
        return [near_near, send(near_far, "heads", 1), across]

    parts = ((piece, BF), (piece, BF))
    none = [None, None]
    norms_two, norms_three, branches_two, branches_one = (list(none) for unused in range(4))
    norm_one, qkv_one, context_one, probs_one = list(none), list(none), list(none), list(none)
    after_self, norm_two = list(none), list(none)
    query_two, context_two, probs_two = list(none), list(none), list(none)
    second, norm_three = list(none), list(none)
    cot_half, hidden, active = list(none), list(none), list(none)
    grad_second, branch_two = list(none), list(none)
    grad_query_two, grad_after_self, branch_one = list(none), list(none), list(none)
    grad_qkv_one, bias_acc = list(none), list(none)

    def self_forward(i, gate):
        *saved, own, near, away = call(
            functools.partial(self_forward_kernel, size, i),
            "self_forward",
            [dec_lengths, *inputs_pieces, after(gain_one, *gate), Far(weights_one), Far(bias)],
            [
                far((half, features)),
                far((half, 3 * width)),
                far((half, width)),
                far((blocks, heads, BLOCK, 2 * BLOCK)),
                (piece, BF),
                *parts,
            ],
            [
                pltpu.VMEM((half, features), BF),
                pltpu.VMEM((half + BLOCK, 2 * width), BF),
            ],
            us=2.0,
            smem=1,
            lazy=True,
        )
        norm_one[i], qkv_one[i], context_one[i], probs_one[i] = map(Far, saved)

        def finish(one, gate):
            after_self[i], norm_two[i] = forward_norm(one, own, gain_two, gate)
            return norm_two[i][0]

        return near, away, finish

    def cross_forward(i, gate):
        kinds = []
        if plain[i]:
            kinds.append(far((plain[i], heads, BLOCK, window)))
        if plain[i] < blocks:
            kinds.append(far((blocks - plain[i], heads, BLOCK, enc_length)))
        query, context, near, away, *saved = call(
            functools.partial(cross_forward_kernel, size, i),
            "cross_forward",
            [
                dec_lengths,
                enc_lengths,
                *norm_two[i],
                Far(weights_two),
                Far(after(keys["kv"], *gate)),
            ],
            [far((half, width)), far((half, width)), *parts, *kinds, far((half, features))],
            us=4.0,
            smem=2,
            raw=2,
            lazy=True,
        )
        query_two[i], context_two[i] = Far(query), Far(context)
        *probs_two[i], norms_two[i] = map(Far, saved)

        def finish(one, gate):
            second[i], norm_three[i] = forward_norm(one, after_self[i], gain_three, gate)
            return norm_three[i][0]

        return near, away, finish

    def feed_forward(i, gate):
        *saved, own, near, away, norms = call(
            functools.partial(ffn_kernel, i),
            "ffn",
            [*norm_three[i], *both_pieces, Far(after(weights_three, *gate))],
            [
                far((half, features)),
                far((half, units)),
                far((half, units)),
                (piece, BF),
                *parts,
                far((half, features)),
            ],
            [pltpu.VMEM((half, features), BF)],
            us=5.0,
            raw=2,
            lazy=True,
        )
        cot_half[i], hidden[i], active[i] = map(Far, saved)
        norms_three[i] = Far(norms)

        def finish(one, gate):
            grad_second[i], branch_two[i] = backward_pair(
                one, second[i], own, gain_three, gate
            )
            return branch_two[i][0]

        return near, away, finish

    def cross_backward(i, gate):
        last = i == order[-1]
        so_far = keys["grad"]
        grad_query_two[i], grad_kv, near, away, branch = call(
            functools.partial(
                cross_backward_kernel, size, i, len(probs_two[i]), len(so_far)
            ),
            "cross_backward",
            [
                dec_lengths,
                enc_lengths,
                *branch_two[i],
                weights_two,
                query_two[i],
                Far(after(keys["kv"], *gate)),
                *probs_two[i],
                *so_far,
            ],
            [
                ((half, width), BF),
                ((enc_length, 2 * width), BF) if last else ((2 * width, enc_length), F32),
                *parts,
                far((half, features)),
            ],
            [
                pltpu.VMEM((2 * width, enc_length), F32),
                pltpu.VMEM((half, width), BF),
            ],
            us=8.0,
            smem=2,
            raw=2,
            lazy=True,
            fetch=True,
        )
        keys["grad"] = [grad_kv]
        branches_two[i] = Far(branch)

        def finish(one, gate):
            grad_after_self[i], branch_one[i] = backward_pair(
                one, after_self[i], grad_second[i], gain_two, gate
            )
            return branch_one[i][0]

        return near, away, finish

    def self_backward(i, gate):
        first = Far(after(qkv_one[i].array, *gate))
        grad_qkv_one[i], acc, *edge, branch = call(
            functools.partial(self_backward_kernel, size, i),
            "self_backward",
            [
                *branch_one[i],
                weights_one,
                first,
                probs_one[i],
                qkv_one[0] if i else keys["edge"],
            ],
            [
                ((half, 3 * width), BF),
                ((heads, BLOCK, 2 * BLOCK), F32, "far"),
                *[((2 * width, BLOCK), F32)] * i,
                far((half, features)),
            ],
            [
                pltpu.VMEM((half + BLOCK, 2 * width), BF),
                pltpu.VMEM((2 * width, half + BLOCK), F32),
                pltpu.VMEM((half, width), BF),
            ],
            us=2.0,
            raw=2,
            lazy=True,
            fetch=True,
        )
        bias_acc[i], branches_one[i] = Far(acc), Far(branch)
        if edge:
            keys["edge"] = edge[0]
        return [grad_qkv_one[i]]

    def halves(left, right):
        return [(left[i], right[i]) for i in order]

    def make_keys(gate):
        keys["kv"], enc = call(
            functools.partial(cross_keys_kernel, width),
            "cross_keys",
            [*both_pieces, Far(after(weights_two, *gate))],
            [far((enc_length, 2 * width)), far((enc_length, features))],
            us=2.5,
            raw=4,
        )
        keys["enc"] = Far(enc)
        return keys["kv"]

    def ffn_weights(gate):
        held = {i: Far(after(hidden[i].array, *gate)) for i in order}
        blocks = weight_blocks(
            [halves(norms_three, active), halves(cot_half, held)], 2 * units, features, "ffn_weights"
        )
        keys["ffn"] = blocks
        return blocks[0]

    def layer_parts(gate):
        held = [hidden[0], Far(after(hidden[1].array, *gate))]
        layer = scatter_halves(held, weights_three, units, "layer_scatter")
        grads["layer"] = own_of(second) + sum(part.astype(F32) for part in layer)
        cross = scatter_rows_lower(after(keys["cross"][0], layer[0]), keys["cross"][1])
        grads["both"] = scatter_rows_upper(jnp.concatenate([grads["ffn"], cross], 2))
        return key_parts([layer[0]])

    def cross_weights(gate):
        blocks = weight_blocks(
            [
                halves(norms_two, grad_query_two),
                [(keys["enc"], after(keys["grad"][0], *gate))],
                halves(branches_two, context_two),
            ],
            4 * width,
            features,
            "cross_weights",
        )
        grads["ffn"] = scatter_rows_lower(after(keys["ffn"][0], blocks[0]), keys["ffn"][1])
        keys["cross"] = blocks
        return blocks[0]

    def key_parts(gate):
        key_parts = call(
            functools.partial(scatter_keys_kernel, width),
            "scatter_keys",
            [after(keys["grad"][0], *gate), Far(weights_two)],
            [(piece, BF)] * 4,
            us=2.0,
        )
        across = send(chip_sum(key_parts[2], key_parts[3]), "heads", 2)
        grads["encoded"] = (
            key_parts[0].astype(F32)
            + send(key_parts[1], "heads", 1).astype(F32)
            + across.astype(F32)
        )
        return key_parts[0]

    keys = {"grad": [], "edge": []}
    grads = {}
    filler = {2: make_keys, 6: ffn_weights, 8: cross_weights, 9: layer_parts}
    stages = [self_forward, cross_forward, feed_forward, cross_backward, self_backward]
    gate, pending, step = [], None, 0
    for stage in stages:
        for i in order:
            result = stage(i, gate)
            gate = [result[0]]
            step += 1
            if step in filler:
                gate = [filler[step](gate)]
            if pending:
                gate = [pending[0](pending[1], gate)]
                pending = None
            if stage is self_backward:
                continue
            near, away, finish = result
            one = chip_sum(after(near, *gate), away)
            gate = [one]
            pending = (finish, one)
    input_parts = scatter_halves(grad_qkv_one, weights_one, 0, "input_scatter")
    self_blocks = weight_blocks(
        [
            halves(norm_one, [after(grad_qkv_one[0], input_parts[0]), grad_qkv_one[1]]),
            halves(branches_one, context_one),
        ],
        4 * width,
        features,
        "self_weights",
    )
    self_half = scatter_rows_lower(*self_blocks)
    self_got = scatter_rows_upper(after(self_half, grads["both"]))
    (input_grad,) = backward_norm(
        input_parts,
        inputs,
        own_of(grad_after_self),
        gain_one,
        branch=False,
    )
    both_grad, self_grad = sum_rows(grads["both"]), sum_rows(self_got)
    ffn_grad, cross_grad = both_grad[:, : 2 * units], both_grad[:, 2 * units :]

    bias_sums = call(
        bias_grad_kernel,
        "bias_grad",
        [jnp.array(starts + [1 << 20], jnp.int32), Far(after(bias_acc[0].array, self_half)), bias_acc[1]],
        [((heads, buckets, 2 * BLOCK), F32)],
        us=2.0,
        smem=1,
    )[0]
    bias_grad = jnp.sum(bias_sums, axis=-1)
    bits = 1
    while bits < lax.axis_size("rows"):
        bias_grad = bias_grad + send(bias_grad, "rows", bits)
        bits *= 2

    def along(weights, gradient):
        return jnp.sum(
            jnp.concatenate([w.astype(F32) for w in weights], 1) * gradient, axis=1
        )

    gain_grads = jnp.stack(
        [
            along([self_query, self_key, self_value], self_grad[:, : 3 * width]),
            along([cross_query], cross_grad[:, :width]),
            along([inner_weight], ffn_grad[:, :units]),
        ]
    )
    for bits in (1, 2):
        gain_grads = gain_grads + send(gain_grads, "heads", bits)
    gain_grads = lax.dynamic_slice_in_dim(gain_grads, me * each, each, 1) / jnp.stack(
        [gain_first, gain_second, gain_third]
    ).astype(F32)

    return (
        grads["layer"].astype(BF)[None],
        input_grad[None],
        grads["encoded"][None],
        self_grad[:, :width],
        self_grad[:, width : 2 * width],
        self_grad[:, 2 * width : 3 * width],
        self_grad[:, 3 * width :].T,
        cross_grad[:, :width],
        cross_grad[:, width : 2 * width],
        cross_grad[:, 2 * width : 3 * width],
        cross_grad[:, 3 * width :].T,
        ffn_grad[:, :units],
        ffn_grad[:, units:].T,
        bias_grad.T,
        gain_grads[0],
        gain_grads[1],
        gain_grads[2],
    )


def solution(mesh):
    positions = P("rows", "heads", None)
    columns = P("rows", "heads")
    lines = P("heads", "rows")
    gains = P(("rows", "heads"))
    return jax.shard_map(
        shards,
        mesh=mesh,
        in_specs=(
            positions,
            positions,
            positions,
            P("rows", None),
            P("rows", None),
            columns,
            columns,
            columns,
            lines,
            columns,
            columns,
            columns,
            lines,
            columns,
            lines,
            P(None, "heads"),
            gains,
            gains,
            gains,
        ),
        out_specs=(
            positions,
            positions,
            positions,
            columns,
            columns,
            columns,
            lines,
            columns,
            columns,
            columns,
            lines,
            columns,
            lines,
            P(None, "heads"),
            gains,
            gains,
            gains,
        ),
        check_vma=False,
    )
```

```python
import functools

import jax
import jax.numpy as jnp
import numpy as np
from jax import lax
from jax.experimental import pallas as pl
from jax.experimental.pallas import tpu as pltpu
from jax.sharding import PartitionSpec as P

MAX_DISTANCE = 128
EPS = 1e-06
NEG = -1000000000.0
LEAST = 96
MOST = 128
BLOCK = 128
SUM_ROWS = 16
BF = jnp.bfloat16
F32 = jnp.float32
VMEM = pl.BlockSpec(memory_space=pltpu.VMEM)
SMEM = pl.BlockSpec(memory_space=pltpu.SMEM)


def bucket_starts(bucket_count, max_reach):
    exact_span = bucket_count // 2
    starts = list(range(exact_span + 1))
    for target in range(exact_span + 1, bucket_count):
        distance = exact_span
        while (
            distance < max_reach
            and exact_span
            + int(
                np.log(distance / exact_span)
                / np.log(max_reach / exact_span)
                * (bucket_count - exact_span)
            )
            < target
        ):
            distance += 1
        starts.append(distance)
    return starts


COST = {'place': 1.5, 'pair': 1.5, 'bias': 2.0, 'self_forward': 2.0, 'norm_forward': 1.0, 'cross_keys': 2.5, 'cross_forward': 4.0, 'ffn': 5.0, 'cross_backward': 1.0, 'self_backward': 2.0, 'norm_backward': 1.5, 'input_norm': 1.5, 'ffn_weights': 4.0, 'cross_weights': 0.04, 'self_weights': 4.0, 'layer_scatter': 2.0, 'input_scatter': 2.0, 'scatter_keys': 2.0, 'bias_grad': 1.0}


class Far:
    def __init__(self, array):
        self.array = array


class Moves:
    def __init__(self, sems):
        self.sems, self.used = sems, 0
        self.coming, self.going, self.started = [], [], []

    def copy(self, source, target):
        made = pltpu.make_async_copy(source, target, self.sems.at[self.used])
        self.used += 1
        made.start()
        return made

    def need(self, *refs):
        for ref in refs:
            for k, (held, made) in enumerate(self.coming):
                if held is ref:
                    made.wait()
                    del self.coming[k]
                    break

    def need_all(self):
        self.need(*[held for held, made in self.coming])

    def send(self, source, target):
        self.started.append(self.copy(source, target))

    def ready(self, *refs):
        for ref in refs:
            for k, (held, target) in enumerate(self.going):
                if held is ref:
                    self.send(held, target)
                    del self.going[k]
                    break

    def finish(self):
        self.need_all()
        self.ready(*[held for held, target in self.going])
        for made in self.started:
            made.wait()


HBM = pl.BlockSpec(memory_space=pltpu.HBM)


def call(body, name, args, outs, scratch=(), us=2.0, smem=0, raw=0, moved=0, lazy=False, fetch=False, key=None):
    far_in = [fetch and isinstance(x, Far) for x in args]
    arrays = [
        pltpu.with_memory_space_constraint(x.array, pltpu.HBM)
        if f
        else x.array
        if isinstance(x, Far)
        else x
        for x, f in zip(args, far_in)
    ]
    far_out = [len(o) > 2 for o in outs]
    last = len(outs) - (raw > 0)
    held = [pltpu.VMEM(x.shape, x.dtype) for x, f in zip(arrays, far_in) if f]
    held += [pltpu.VMEM(o[0], o[1]) for o, f in zip(outs[:last], far_out) if f]
    copies = len(held) + raw + moved
    if copies:
        held.append(pltpu.SemaphoreType.DMA((copies,)))

    def kernel(*refs):
        ins, results = refs[: len(args)], refs[len(args) : len(args) + len(outs)]
        own = refs[len(args) + len(outs) : len(args) + len(outs) + len(scratch)]
        spare = list(refs[len(args) + len(outs) + len(scratch) :])
        moves = Moves(spare.pop() if copies else None)
        given = []
        for ref, f in zip(ins, far_in):
            if f:
                here = spare.pop(0)
                moves.coming.append((here, moves.copy(ref, here)))
                ref = here
            given.append(ref)
        for k, ref in enumerate(results):
            if far_out[k] and k < last:
                here = spare.pop(0)
                moves.going.append((here, ref))
                ref = here
            given.append(ref)
        if not lazy:
            moves.need_all()
        body(moves, *given, *own)
        moves.finish()

    return pl.pallas_call(
        kernel,
        out_shape=[
            (pltpu.HBM if f else jax.ShapeDtypeStruct)(o[0], o[1])
            for o, f in zip(outs, far_out)
        ],
        in_specs=[SMEM] * smem + [HBM if f else VMEM for f in far_in[smem:]],
        out_specs=[HBM if f else VMEM for f in far_out],
        scratch_shapes=list(scratch) + held,
        compiler_params=pltpu.CompilerParams(vmem_limit_bytes=16 << 20),
        name=name,
        cost_estimate=pl.CostEstimate(
            flops=int(COST.get(key or name, us) * 1e9),
            bytes_accessed=int(COST.get(key or name, us) * 3e6),
            transcendentals=0,
        ),
    )(*arrays)


def send(part, axis, bits):
    count = lax.axis_size(axis)
    return lax.ppermute(part, axis, [(i, i ^ bits) for i in range(count)])


def after(value, *others):
    return lax.optimization_barrier((value,) + others)[0]


def gather_heads(part):
    across = send(part, "heads", 2)
    return [part, send(part, "heads", 1), across, send(across, "heads", 1)]


def place_kernel(count, moves, *refs):
    me = lax.axis_index("rows")
    for t in range(count):
        moves.send(refs[t], refs[count].at[me ^ t])


def pair_kernel(moves, near, other, out):
    lower = lax.axis_index("rows") % 2
    moves.send(near, out.at[:, lower])
    moves.send(other, out.at[:, 1 - lower])


def gather_rows_first(part):
    return [part] + [
        send(part, "rows", 2 * upper) for upper in range(1, lax.axis_size("rows") // 2)
    ]


def gather_rows_second(firsts):
    pieces = []
    for near in firsts:
        pieces += [near, send(near, "rows", 1)]
    return pieces


def lay_rows(pieces, *others):
    count = len(pieces)
    shape = (count,) + pieces[0].shape
    pieces = [after(pieces[0], *others)] + pieces[1:]
    placed = call(
        functools.partial(place_kernel, count), "place", pieces, [(shape, BF)], us=1.5, moved=count
    )[0]
    return placed.reshape(-1, shape[2])


def upper_groups():
    count = lax.axis_size("rows")
    return [list(range(lower, count, 2)) for lower in range(2)]


def gather_rows_upper(part):
    count = lax.axis_size("rows") // 2
    spread = jnp.broadcast_to(part[None], (count,) + part.shape)
    return lax.all_to_all(
        spread, "rows", 0, 0, tiled=True, axis_index_groups=upper_groups()
    )


def gather_rows_lower(near):
    count, rows, lanes = near.shape
    placed = call(
        pair_kernel,
        "pair",
        [near, send(near, "rows", 1)],
        [((count, 2, rows, lanes), BF)],
        us=1.5,
        moved=2,
    )[0]
    return placed.reshape(-1, lanes)


def scatter_rows_lower(keep, away):
    return (keep.astype(F32) + send(away, "rows", 1).astype(F32)).astype(BF)


def scatter_rows_upper(blocks):
    return lax.all_to_all(blocks, "rows", 0, 0, tiled=True, axis_index_groups=upper_groups())


def sum_rows(got):
    return jnp.sum(got.astype(F32), axis=0)


def dot(a, b, dims):
    return lax.dot_general(a, b, (dims, ((), ())), preferred_element_type=F32)


NT = ((1,), (1,))
NN = ((1,), (0,))
TN = ((0,), (0,))


def core_and_chip():
    me = lax.axis_index("heads")
    return me % 2, me // 2


def rms_rows(values, gain):
    factor = lax.rsqrt(jnp.mean(values * values, axis=-1, keepdims=True) + EPS)
    return (values * factor * gain).astype(BF)


def pick_half(half, pieces, out):
    unused, chip = core_and_chip()
    quarter = pieces[0].shape[0]
    for near in (True, False):

        @pl.when((chip == half) == near)
        def _(near=near):
            for s in range(2):
                out[s * quarter : (s + 1) * quarter, :] = pieces[s + (0 if near else 2)][...]


def distances(first, rows):
    query = lax.broadcasted_iota(jnp.int32, (rows, 2 * BLOCK), 0) + (first + BLOCK)
    return query - lax.broadcasted_iota(jnp.int32, (rows, 2 * BLOCK), 1)


def bias_kernel(starts, moves, table_ref, out_ref):
    heads = out_ref.shape[0]
    step = 32

    def rows(t, carry):
        first = pl.multiple_of(t * step, step)
        reach = distances(first, step)
        values = [jnp.full((step, 2 * BLOCK), table_ref[0, h], F32) for h in range(heads)]
        for b in range(1, len(starts)):
            beyond = reach >= starts[b]
            values = [jnp.where(beyond, table_ref[b, h], values[h]) for h in range(heads)]
        for h in range(heads):
            out_ref[h, pl.ds(first, step), :] = values[h]
        return carry

    lax.fori_loop(0, BLOCK // step, rows, 0)


def bias_grad_kernel(starts, moves, one_ref, two_ref, out_ref):
    reach = distances(0, BLOCK)
    for h in range(one_ref.shape[0]):
        acc = one_ref[h] + two_ref[h]
        for b in range(len(starts)):
            inside = reach < starts[1] if b == 0 else reach >= starts[b]
            if 0 < b < len(starts) - 1:
                inside = inside & (reach < starts[b + 1])
            out_ref[h, b : b + 1, :] = jnp.sum(jnp.where(inside, acc, 0.0), axis=0, keepdims=True)


def running(lengths_ref, count):
    total = lengths_ref[0, 0]
    ends = [total]
    for c in range(1, count):
        total = total + lengths_ref[0, c]
        ends.append(total)
    return ends


def slot_of(block, core, quarter):
    each = quarter // BLOCK
    return pl.multiple_of((((block // each) ^ core) * each + block % each) * BLOCK, BLOCK)


def softmax(scores):
    e = jnp.exp(scores - jnp.max(scores, axis=-1, keepdims=True))
    return (e * (1.0 / jnp.sum(e, axis=-1, keepdims=True))).astype(BF)


def self_forward_kernel(size, half, moves, lengths_ref, *refs):
    pieces = refs[:4]
    gain_ref, w_ref, bias_ref = refs[4:7]
    norm_ref, qkv_ref, context_ref, probs_ref, own_ref, near_ref, far_ref = refs[7:14]
    x, kv = refs[14:]
    heads = bias_ref.shape[0]
    width = heads * size
    quarter = own_ref.shape[0]
    core, chip = core_and_chip()
    ends = running(lengths_ref, lengths_ref.shape[1])
    blocks = 2 * quarter // BLOCK
    gain = gain_ref[...]
    moves.need(*pieces)
    pick_half(half, pieces, x)
    own_ref[...] = x[:quarter, :]
    moves.need(w_ref)

    if half:
        for k in range(4):

            @pl.when((core == 1 - k % 2) & ((chip == 0) == (k < 2)))
            def _(k=k):
                norm_ref[:BLOCK, :] = pieces[k][quarter - BLOCK :, :]

        before = rms_rows(norm_ref[:BLOCK, :].astype(F32), gain)
        kv[:BLOCK, :] = dot(before, w_ref[:, width : 3 * width], NN).astype(BF)
    else:
        kv[:BLOCK, :] = jnp.zeros((BLOCK, 2 * width), BF)

    def project(b, carry):
        at = pl.multiple_of(slot_of(b, core, quarter), BLOCK)
        norm = rms_rows(x[pl.ds(at, BLOCK), :].astype(F32), gain)
        norm_ref[pl.ds(at, BLOCK), :] = norm
        qkv = dot(norm, w_ref[:, : 3 * width], NN).astype(BF)
        qkv_ref[pl.ds(at, BLOCK), :] = qkv
        kv[pl.ds(pl.multiple_of((b + 1) * BLOCK, BLOCK), BLOCK), :] = qkv[:, width:]
        return carry

    lax.fori_loop(0, blocks, project, 0)
    moves.ready(norm_ref, qkv_ref)
    moves.need(bias_ref)

    def block(b, carry):
        own = slot_of(b, core, quarter)
        at = pl.multiple_of(b * BLOCK, BLOCK)
        base = (half * blocks + b) * BLOCK
        query = base + lax.broadcasted_iota(jnp.int32, (BLOCK, 1), 0)
        start = jnp.zeros((BLOCK, 1), jnp.int32)
        for end in ends:
            start = jnp.where(query >= end, end, start)
        key = base - BLOCK + lax.broadcasted_iota(jnp.int32, (BLOCK, 2 * BLOCK), 1)
        allowed = (key >= start) & (key <= query)
        outs = []
        for h in range(heads):
            q = qkv_ref[pl.ds(own, BLOCK), h * size : (h + 1) * size]
            k = kv[pl.ds(at, 2 * BLOCK), h * size : (h + 1) * size]
            v = kv[pl.ds(at, 2 * BLOCK), width + h * size : width + (h + 1) * size]
            probs = softmax(jnp.where(allowed, dot(q, k, NT) + bias_ref[h], NEG))
            probs_ref[b, h] = probs
            outs.append(dot(probs, v, NN).astype(BF))
        context_ref[pl.ds(own, BLOCK), :] = jnp.concatenate(outs, 1)
        return carry

    lax.fori_loop(0, blocks, block, 0)
    moves.ready(context_ref, probs_ref)
    out_weight = w_ref[:, 3 * width : 4 * width]
    far_ref[...] = dot(context_ref[quarter:, :], out_weight, NT).astype(BF)
    near_ref[...] = dot(context_ref[:quarter, :], out_weight, NT).astype(BF)


def self_backward_kernel(size, half, moves, *refs):
    own_ref, other_ref, w_ref, qkv_ref, probs_ref, edge_in = refs[:6]
    out_ref, acc_ref = refs[6:8]
    branch_ref = refs[-4]
    kv, key_acc, grad = refs[-3:]
    heads = acc_ref.shape[0]
    width = heads * size
    quarter = own_ref.shape[0]
    core, chip = core_and_chip()
    blocks = 2 * quarter // BLOCK
    moves.send(own_ref, branch_ref.at[:quarter])
    moves.send(other_ref, branch_ref.at[quarter:])
    key_acc[...] = jnp.zeros_like(key_acc)
    acc_ref[...] = jnp.zeros_like(acc_ref)
    moves.need(w_ref)
    out_weight = w_ref[:, 3 * width : 4 * width]
    grad[:quarter, :] = dot(own_ref[...], out_weight, NN).astype(BF)
    grad[quarter:, :] = dot(other_ref[...], out_weight, NN).astype(BF)
    moves.need(edge_in, qkv_ref)
    if half:
        kv[:BLOCK, :] = edge_in[pl.ds(slot_of(blocks - 1, core, quarter), BLOCK), width:]
    else:
        kv[:BLOCK, :] = jnp.zeros((BLOCK, 2 * width), BF)
        key_acc[:, blocks * BLOCK :] = edge_in[...]
    for b in range(blocks):
        kv[(b + 1) * BLOCK : (b + 2) * BLOCK, :] = qkv_ref[
            pl.ds(slot_of(b, core, quarter), BLOCK), width:
        ]
    moves.need(probs_ref)

    def block(b, carry):
        own = slot_of(b, core, quarter)
        at = pl.multiple_of(b * BLOCK, BLOCK)
        grads_q, grads_k, grads_v = [], [], []
        for h in range(heads):
            q = qkv_ref[pl.ds(own, BLOCK), h * size : (h + 1) * size]
            k = kv[pl.ds(at, 2 * BLOCK), h * size : (h + 1) * size]
            v = kv[pl.ds(at, 2 * BLOCK), width + h * size : width + (h + 1) * size]
            c = grad[pl.ds(own, BLOCK), h * size : (h + 1) * size]
            probs = probs_ref[b, h]
            wide = probs.astype(F32)
            grad_probs = dot(c, v, NT)
            inner = jnp.sum(grad_probs * wide, axis=-1, keepdims=True)
            grad_scores = wide * (grad_probs - inner)
            acc_ref[h] += grad_scores
            short = grad_scores.astype(BF)
            grads_q.append(dot(short, k, NN).astype(BF))
            grads_k.append(dot(q.T, short, NN))
            grads_v.append(dot(c.T, probs, NN))
        out_ref[pl.ds(own, BLOCK), :width] = jnp.concatenate(grads_q, 1)
        key_acc[:, pl.ds(at, 2 * BLOCK)] += jnp.concatenate(grads_k + grads_v, 0)
        return carry

    lax.fori_loop(0, blocks, block, 0)
    for b in range(blocks):
        out_ref[pl.ds(slot_of(b, core, quarter), BLOCK), width:] = key_acc[
            :, (b + 1) * BLOCK : (b + 2) * BLOCK
        ].T.astype(BF)
    if half:
        refs[8][...] = key_acc[:, :BLOCK]


def cross_keys_kernel(width, moves, *refs):
    pieces, w_ref = refs[:4], refs[4]
    kv_ref, enc_ref = refs[5:]
    quarter = pieces[0].shape[1]
    me = lax.axis_index("heads")
    weight = w_ref[:, width : 3 * width]
    for k in range(4):
        at = pl.ds(pl.multiple_of((me ^ k) * quarter, quarter), quarter)
        moves.send(pieces[k].at[0], enc_ref.at[at])
        kv_ref[at, :] = dot(pieces[k][0], weight, NN).astype(BF)


def cross_window(block, dec_ends, enc_ends, enc_length, window):
    first = jnp.int32(0)
    for c in range(len(dec_ends) - 1):
        first = jnp.where(block * BLOCK >= dec_ends[c], enc_ends[c], first)
    return pl.multiple_of(
        jnp.minimum(first // BLOCK * BLOCK, enc_length - window), BLOCK
    )


def cross_forward_kernel(size, half, moves, dec_ref, enc_ref, own_ref, other_ref, w_ref, kv_ref, *refs):
    query_ref, context_ref, near_ref, far_ref = refs[:4]
    all_probs, norm_ref = refs[4:-1], refs[-1]
    heads = refs[4].shape[1]
    width = heads * size
    quarter = own_ref.shape[0]
    core, chip = core_and_chip()
    first = half * (2 * quarter // BLOCK)
    enc_length = kv_ref.shape[0]
    comments = dec_ref.shape[1]
    dec_ends = running(dec_ref, comments)
    enc_ends = running(enc_ref, comments)
    moves.send(own_ref, norm_ref.at[:quarter])
    moves.send(other_ref, norm_ref.at[quarter:])
    moves.need(w_ref)
    query_ref[:quarter, :] = dot(own_ref[...], w_ref[:, :width], NN).astype(BF)
    query_ref[quarter:, :] = dot(other_ref[...], w_ref[:, :width], NN).astype(BF)
    moves.ready(query_ref)
    moves.need(kv_ref)
    done = 0
    for probs_ref in all_probs:
        window = probs_ref.shape[3]

        def block(b, carry, window=window, probs_ref=probs_ref, done=done):
            own = slot_of(b, core, quarter)
            base = (first + b) * BLOCK
            start = (
                cross_window(first + b, dec_ends, enc_ends, enc_length, window)
                if window < enc_length
                else 0
            )
            query = base + lax.broadcasted_iota(jnp.int32, (BLOCK, 1), 0)
            low = jnp.zeros((BLOCK, 1), jnp.int32)
            high = jnp.full((BLOCK, 1), enc_ends[0], jnp.int32)
            for c in range(comments):
                later = query >= dec_ends[c]
                last = c == comments - 1
                low = jnp.where(later, 0 if last else enc_ends[c], low)
                high = jnp.where(later, enc_length if last else enc_ends[c + 1], high)
            key = start + lax.broadcasted_iota(jnp.int32, (BLOCK, window), 1)
            allowed = (key >= low) & (key < high)
            contexts = []
            for h in range(heads):
                q = query_ref[pl.ds(own, BLOCK), h * size : (h + 1) * size]
                k = kv_ref[pl.ds(start, window), h * size : (h + 1) * size]
                v = kv_ref[pl.ds(start, window), width + h * size : width + (h + 1) * size]
                probs = softmax(jnp.where(allowed, dot(q, k, NT), NEG))
                probs_ref[b - done, h] = probs
                contexts.append(dot(probs, v, NN).astype(BF))
            context_ref[pl.ds(own, BLOCK), :] = jnp.concatenate(contexts, 1)
            return carry

        lax.fori_loop(done, done + probs_ref.shape[0], block, 0)
        done += probs_ref.shape[0]
        moves.ready(probs_ref)
    moves.ready(context_ref)
    out_weight = w_ref[:, 3 * width :]
    far_ref[...] = dot(context_ref[quarter:, :], out_weight, NT).astype(BF)
    near_ref[...] = dot(context_ref[:quarter, :], out_weight, NT).astype(BF)


def cross_backward_kernel(size, half, kinds, more, moves, dec_ref, enc_ref, *refs):
    own_ref, other_ref, w_ref, query_ref, kv_ref = refs[:5]
    probs_refs = refs[5 : 5 + kinds]
    so_far = refs[5 + kinds : 5 + kinds + more]
    grad_q_ref, grad_kv_ref, near_ref, far_ref, branch_ref, key_acc, grad = refs[5 + kinds + more :]
    heads = probs_refs[0].shape[1]
    width = heads * size
    quarter = own_ref.shape[0]
    core, chip = core_and_chip()
    first = half * (2 * quarter // BLOCK)
    enc_length = kv_ref.shape[0]
    comments = dec_ref.shape[1]
    dec_ends = running(dec_ref, comments)
    enc_ends = running(enc_ref, comments)
    moves.send(own_ref, branch_ref.at[:quarter])
    moves.send(other_ref, branch_ref.at[quarter:])
    key_acc[...] = so_far[0][...] if more else jnp.zeros_like(key_acc)
    moves.need(w_ref)
    out_weight = w_ref[:, 3 * width :]
    grad[:quarter, :] = dot(own_ref[...], out_weight, NN).astype(BF)
    grad[quarter:, :] = dot(other_ref[...], out_weight, NN).astype(BF)
    moves.need(query_ref, kv_ref)
    done = 0
    for probs_ref in probs_refs:
        moves.need(probs_ref)
        window = probs_ref.shape[3]

        def block(b, carry, window=window, probs_ref=probs_ref, done=done):
            own = slot_of(b, core, quarter)
            start = (
                cross_window(first + b, dec_ends, enc_ends, enc_length, window)
                if window < enc_length
                else 0
            )
            grads_q, grads_k, grads_v = [], [], []
            for h in range(heads):
                q = query_ref[pl.ds(own, BLOCK), h * size : (h + 1) * size]
                k = kv_ref[pl.ds(start, window), h * size : (h + 1) * size]
                v = kv_ref[pl.ds(start, window), width + h * size : width + (h + 1) * size]
                c = grad[pl.ds(own, BLOCK), h * size : (h + 1) * size]
                probs = probs_ref[b - done, h]
                wide = probs.astype(F32)
                grad_probs = dot(c, v, NT)
                inner = jnp.sum(grad_probs * wide, axis=-1, keepdims=True)
                short = (wide * (grad_probs - inner)).astype(BF)
                grads_q.append(dot(short, k, NN).astype(BF))
                grads_k.append(dot(q.T, short, NN))
                grads_v.append(dot(c.T, probs, NN))
            grad_q_ref[pl.ds(own, BLOCK), :] = jnp.concatenate(grads_q, 1)
            key_acc[:, pl.ds(start, window)] += jnp.concatenate(grads_k + grads_v, 0)
            return carry

        lax.fori_loop(done, done + probs_ref.shape[0], block, 0)
        done += probs_ref.shape[0]
    grad_kv_ref[...] = (key_acc[...].T if more else key_acc[...]).astype(grad_kv_ref.dtype)
    weight = w_ref[:, :width]
    far_ref[...] = dot(grad_q_ref[quarter:, :], weight, NT).astype(BF)
    near_ref[...] = dot(grad_q_ref[:quarter, :], weight, NT).astype(BF)


def ffn_kernel(half, moves, own_ref, other_ref, *refs):
    pieces, w_ref = refs[:4], refs[4]
    cot_ref, hidden_ref, active_ref, own_cot_ref, near_ref, far_ref, norms_ref, norms = refs[5:]
    quarter = own_ref.shape[0]
    units = hidden_ref.shape[1]
    part = 256 if units % 256 == 0 else units
    moves.send(own_ref, norms_ref.at[:quarter])
    moves.send(other_ref, norms_ref.at[quarter:])
    pick_half(half, [part.at[1] for part in pieces], cot_ref)
    own_cot_ref[...] = cot_ref[:quarter, :]
    moves.ready(cot_ref)
    moves.need(w_ref)
    norms[:quarter, :] = own_ref[...]
    norms[quarter:, :] = other_ref[...]

    def rows(t, carry):
        at = pl.ds(pl.multiple_of(t * BLOCK, BLOCK), BLOCK)
        norm = norms[at, :]
        cot = cot_ref[at, :]
        for f in range(0, units, part):
            active = dot(norm, w_ref[:, f : f + part], NN)
            grad = dot(cot, w_ref[:, units + f : units + f + part], NN)
            share = 0.5 + 0.5 * lax.erf(active * np.float32(np.sqrt(0.5)))
            slope = share + active * (
                jnp.exp(-0.5 * active * active) * np.float32(1.0 / np.sqrt(2.0 * np.pi))
            )
            hidden_ref[at, f : f + part] = (active * share).astype(BF)
            active_ref[at, f : f + part] = (grad * slope).astype(BF)
        return carry

    lax.fori_loop(0, 2 * quarter // BLOCK, rows, 0)
    moves.ready(hidden_ref, active_ref)
    weight = w_ref[:, :units]
    far_ref[...] = dot(active_ref[quarter:, :], weight, NT).astype(BF)
    near_ref[...] = dot(active_ref[:quarter, :], weight, NT).astype(BF)


def scatter_kernel(first, moves, one_ref, two_ref, w_ref, far_far, far_near, near_far, near_near, picked):
    unused, chip = core_and_chip()
    quarter = far_far.shape[0]
    weight = w_ref[:, first : first + one_ref.shape[1]]
    for index in range(2):

        @pl.when(chip == index)
        def _(index=index):
            picked[0] = (two_ref, one_ref)[index][...]
            picked[1] = (one_ref, two_ref)[index][...]

    far_far[...] = dot(picked[0, quarter:, :], weight, NT).astype(BF)
    near_far[...] = dot(picked[1, quarter:, :], weight, NT).astype(BF)
    far_near[...] = dot(picked[0, :quarter, :], weight, NT).astype(BF)
    near_near[...] = dot(picked[1, :quarter, :], weight, NT).astype(BF)


def scatter_keys_kernel(width, moves, grad_ref, w_ref, *outs):
    quarter = outs[0].shape[0]
    me = lax.axis_index("heads")
    weight = w_ref[:, width : 3 * width]
    for k in range(4):
        at = pl.ds(pl.multiple_of((me ^ k) * quarter, quarter), quarter)
        outs[k][...] = dot(grad_ref[at, :], weight, NT).astype(outs[k].dtype)


def norm_forward_kernel(moves, one_ref, two_ref, base_ref, gain_ref, sum_ref, norm_ref):
    rows = base_ref.shape[0]
    step = min(64, rows)

    def some(t, carry):
        at = pl.ds(pl.multiple_of(t * step, step), step)
        total = base_ref[at, :].astype(F32) + one_ref[at, :].astype(F32) + two_ref[at, :].astype(F32)
        sum_ref[at, :] = total
        norm_ref[at, :] = rms_rows(total, gain_ref[...])
        return carry

    lax.fori_loop(0, rows // step, some, 0)


def norm_backward_kernel(parts, moves, *refs):
    values_ref, base_ref, gain_ref = refs[parts : parts + 3]
    grad_ref, *branch_ref = refs[parts + 3 :]
    rows = values_ref.shape[0]
    step = min(64, rows)

    def some(t, carry):
        at = pl.ds(pl.multiple_of(t * step, step), step)
        grad = refs[0][at, :].astype(F32)
        for part in refs[1:parts]:
            grad = grad + part[at, :].astype(F32)
        values = values_ref[at, :].astype(F32)
        factor = lax.rsqrt(jnp.mean(values * values, axis=-1, keepdims=True) + EPS)
        scaled = gain_ref[...] * grad
        mean = jnp.mean(scaled * values, axis=-1, keepdims=True)
        total = (
            base_ref[at, :].astype(F32)
            + factor * scaled
            - values * (factor * factor * factor * mean)
        )
        grad_ref[at, :] = total
        if branch_ref:
            branch_ref[0][at, :] = total.astype(BF)
        return carry

    lax.fori_loop(0, rows // step, some, 0)


def weights_kernel(segments, sums, moves, *refs):
    keep_ref, away_ref, whole = refs[-3:]
    features = whole.shape[0]
    ahead = SUM_ROWS if sums else 0
    group = keep_ref.shape[1] - ahead
    lower = lax.axis_index("rows") % 2
    if sums:
        ones = jnp.ones((8, refs[0].shape[2]), F32)
        lines = [
            lax.dot_general(ones, refs[0][h], (NT, ((), ())), precision=lax.Precision.HIGHEST)
            for h in range(refs[0].shape[0])
        ]
        line = jnp.concatenate(lines + lines, 1)[:, : lines[0].shape[1] * len(lines)].astype(BF)
        line = jnp.concatenate([line] * (SUM_ROWS // 8), 0)
        for out in (keep_ref, away_ref):
            for k in range(out.shape[0]):
                out[k, :SUM_ROWS, :] = jnp.zeros((SUM_ROWS, out.shape[2]), BF)
                out[k, :SUM_ROWS, : line.shape[1]] = line
    step = 384 if features % 384 == 0 else BLOCK
    to = 0
    for pairs in segments:
        for left, right in pairs:
            moves.need(refs[left], refs[right])
        lanes = refs[pairs[0][1]].shape[1]

        def rows(j, carry, pairs=pairs, to=to, lanes=lanes):
            at = pl.ds(pl.multiple_of(j * step, step), step)
            total = sum(dot(refs[left][:, at], refs[right][...], TN) for left, right in pairs)
            whole[at, to : to + lanes] = total.astype(BF)
            return carry

        lax.fori_loop(0, features // step, rows, 0)
        to += lanes
    for r in range(features // group):
        block = slice(r * group, (r + 1) * group)

        @pl.when(lower == r % 2)
        def _(r=r, block=block):
            keep_ref[r // 2, ahead:, :] = whole[block, :]

        @pl.when(lower != r % 2)
        def _(r=r, block=block):
            away_ref[r // 2, ahead:, :] = whole[block, :]


def weight_blocks(segments, lanes, features, key, sums=None):
    operands, index = [] if sums is None else [sums], {}

    def number(operand):
        key = id(operand.array if isinstance(operand, Far) else operand)
        if key not in index:
            index[key] = len(operands)
            operands.append(operand)
        return index[key]

    numbered = [[(number(l), number(r)) for l, r in pairs] for pairs in segments]
    count = lax.axis_size("rows")
    return call(
        functools.partial(weights_kernel, numbered, sums is not None),
        "weights",
        operands,
        [((count // 2, features // count + SUM_ROWS * (sums is not None), lanes), BF)] * 2,
        [pltpu.VMEM((features, lanes), BF)],
        us=4.0,
        key=key,
        lazy=True,
        fetch=True,
    )


def shards(
    inputs,
    encoded,
    cotangent,
    dec_lengths,
    enc_lengths,
    self_query,
    self_key,
    self_value,
    self_output,
    cross_query,
    cross_key,
    cross_value,
    cross_output,
    inner_weight,
    outer_weight,
    bias_table,
    gain_first,
    gain_second,
    gain_third,
):
    groups = lax.axis_size("heads")
    devices = groups * lax.axis_size("rows")
    me = lax.axis_index("heads")
    chip = me // 2
    heads = bias_table.shape[1]
    buckets = bias_table.shape[0]
    width = self_query.shape[1]
    size = width // heads
    quarter = inputs.shape[1]
    half = 2 * quarter
    enc_quarter = encoded.shape[1]
    enc_length = enc_quarter * groups
    features = inputs.shape[2]
    units = inner_weight.shape[1]
    comments = dec_lengths.shape[1]
    starts = bucket_starts(buckets, MAX_DISTANCE)
    blocks = half // BLOCK
    window = 4 * MOST
    order = (1, 0)
    plain = [min(max(LEAST * comments // BLOCK - i * blocks, 0), blocks) for i in range(2)]
    piece = (quarter, features)

    inputs, encoded, cotangent = inputs[0], encoded[0], cotangent[0]

    gains = jnp.concatenate([gain_first, gain_second, gain_third])
    each = gain_first.shape[0]
    spread = jnp.broadcast_to(gains[None], (devices, 3 * each))
    spread = lax.all_to_all(spread, ("rows", "heads"), 0, 0, tiled=True).astype(F32)
    gain_one, gain_two, gain_three = (
        spread[:, i * each : (i + 1) * each].reshape(1, features) for i in range(3)
    )

    far = lambda shape: (shape, BF, "far")
    bias = call(
        functools.partial(bias_kernel, starts),
        "bias",
        [bias_table.astype(F32)],
        [((heads, BLOCK, 2 * BLOCK), F32, "far")],
        us=2.0,
        smem=1,
    )[0]

    weights_one = gather_rows_first(
        jnp.concatenate([self_query, self_key, self_value, self_output.T], 1)
    )
    inputs_pieces = gather_heads(inputs)
    pieces_one = gather_rows_second(
        weights_one[:1] + [after(part) for part in weights_one[1:]]
    )
    parts_two = [
        after(part, pieces_one[5])
        for part in (cross_query, cross_key, cross_value, cross_output)
    ]
    weights_one = lay_rows(pieces_one, spread, bias)
    weights_two = gather_rows_upper(jnp.concatenate(parts_two[:3] + [parts_two[3].T], 1))
    parts_three = [after(part, weights_two) for part in (inner_weight, outer_weight)]
    weights_three = gather_rows_upper(jnp.concatenate([parts_three[0], parts_three[1].T], 1))
    weights_two = gather_rows_lower(weights_two)
    weights_three = gather_rows_lower(weights_three)
    both_pieces = gather_heads(after(jnp.stack([encoded, cotangent]), inputs_pieces[2]))

    def chip_sum(near, far):
        return (near.astype(F32) + send(far, "heads", 1).astype(F32)).astype(BF)

    def forward_norm(one, base, gain, gate):
        total, norm = call(
            norm_forward_kernel,
            "norm_forward",
            [one, send(one, "heads", 2), base, after(gain, *gate)],
            [(piece, F32, "far"), (piece, BF)],
            us=1.0,
        )
        return Far(total), (norm, send(norm, "heads", 1))

    def backward_norm(parts, values, base, gain, branch=True):
        return call(
            functools.partial(norm_backward_kernel, len(parts)),
            "norm_backward",
            [*parts, values, base, gain],
            [(piece, F32)] + [(piece, BF)] * branch,
            us=1.5,
            key="norm_backward" if branch else "input_norm",
        )

    def backward_pair(one, values, base, gain, gate):
        grad, branch = backward_norm(
            [one, send(one, "heads", 2)], values, base, after(gain, *gate)
        )
        return grad, (branch, send(branch, "heads", 1))

    def own_of(pair):
        return jnp.where(chip == 0, *(x.array if isinstance(x, Far) else x for x in pair))

    def scatter_halves(pair, weight, first, key):
        far_far, far_near, near_far, near_near = call(
            functools.partial(scatter_kernel, first),
            "scatter",
            [pair[0], pair[1], Far(weight)],
            [(piece, BF)] * 4,
            [pltpu.VMEM((2, half, (pair[0].array if isinstance(pair[0], Far) else pair[0]).shape[1]), BF)],
            us=2.0,
            key=key,
        )
        across = send(chip_sum(far_near, far_far), "heads", 2)
        return [near_near, send(near_far, "heads", 1), across]

    parts = ((piece, BF), (piece, BF))
    none = [None, None]
    norms_two, norms_three, branches_two, branches_one = (list(none) for unused in range(4))
    norm_one, qkv_one, context_one, probs_one = list(none), list(none), list(none), list(none)
    after_self, norm_two = list(none), list(none)
    query_two, context_two, probs_two = list(none), list(none), list(none)
    second, norm_three = list(none), list(none)
    cot_half, hidden, active = list(none), list(none), list(none)
    grad_second, branch_two = list(none), list(none)
    grad_query_two, grad_after_self, branch_one = list(none), list(none), list(none)
    grad_qkv_one, bias_acc = list(none), list(none)

    def self_forward(i, gate):
        *saved, own, near, away = call(
            functools.partial(self_forward_kernel, size, i),
            "self_forward",
            [dec_lengths, *map(Far, inputs_pieces), after(gain_one, *gate), Far(weights_one), Far(bias)],
            [
                far((half, features)),
                far((half, 3 * width)),
                far((half, width)),
                far((blocks, heads, BLOCK, 2 * BLOCK)),
                (piece, BF),
                *parts,
            ],
            [
                pltpu.VMEM((half, features), BF),
                pltpu.VMEM((half + BLOCK, 2 * width), BF),
            ],
            us=2.0,
            smem=1,
            lazy=True,
            fetch=True,
        )
        norm_one[i], qkv_one[i], context_one[i], probs_one[i] = map(Far, saved)

        def finish(one, gate):
            after_self[i], norm_two[i] = forward_norm(one, own, gain_two, gate)
            return norm_two[i][0]

        return near, away, finish

    def cross_forward(i, gate):
        kinds = []
        if plain[i]:
            kinds.append(far((plain[i], heads, BLOCK, window)))
        if plain[i] < blocks:
            kinds.append(far((blocks - plain[i], heads, BLOCK, enc_length)))
        query, context, near, away, *saved = call(
            functools.partial(cross_forward_kernel, size, i),
            "cross_forward",
            [
                dec_lengths,
                enc_lengths,
                *norm_two[i],
                Far(weights_two),
                Far(after(keys["kv"], *gate)),
            ],
            [far((half, width)), far((half, width)), *parts, *kinds, far((half, features))],
            us=4.0,
            smem=2,
            raw=2,
            lazy=True,
        )
        query_two[i], context_two[i] = Far(query), Far(context)
        *probs_two[i], norms_two[i] = map(Far, saved)

        def finish(one, gate):
            second[i], norm_three[i] = forward_norm(one, after_self[i], gain_three, gate)
            return norm_three[i][0]

        return near, away, finish

    def feed_forward(i, gate):
        *saved, own, near, away, norms = call(
            functools.partial(ffn_kernel, i),
            "ffn",
            [*norm_three[i], *both_pieces, Far(after(weights_three, *gate))],
            [
                far((half, features)),
                far((half, units)),
                far((half, units)),
                (piece, BF),
                *parts,
                far((half, features)),
            ],
            [pltpu.VMEM((half, features), BF)],
            us=5.0,
            raw=2,
            lazy=True,
        )
        cot_half[i], hidden[i], active[i] = map(Far, saved)
        norms_three[i] = Far(norms)

        def finish(one, gate):
            grad_second[i], branch_two[i] = backward_pair(
                one, second[i], own, gain_three, gate
            )
            return branch_two[i][0]

        return near, away, finish

    def cross_backward(i, gate):
        last = i == order[-1]
        so_far = keys["grad"]
        grad_query_two[i], grad_kv, near, away, branch = call(
            functools.partial(
                cross_backward_kernel, size, i, len(probs_two[i]), len(so_far)
            ),
            "cross_backward",
            [
                dec_lengths,
                enc_lengths,
                *branch_two[i],
                weights_two,
                query_two[i],
                Far(after(keys["kv"], *gate)),
                *probs_two[i],
                *so_far,
            ],
            [
                ((half, width), BF),
                ((enc_length, 2 * width), BF) if last else ((2 * width, enc_length), F32),
                *parts,
                far((half, features)),
            ],
            [
                pltpu.VMEM((2 * width, enc_length), F32),
                pltpu.VMEM((half, width), BF),
            ],
            us=8.0,
            smem=2,
            raw=2,
            lazy=True,
            fetch=True,
        )
        keys["grad"] = [grad_kv]
        branches_two[i] = Far(branch)

        def finish(one, gate):
            grad_after_self[i], branch_one[i] = backward_pair(
                one, after_self[i], grad_second[i], gain_two, gate
            )
            return branch_one[i][0]

        return near, away, finish

    def self_backward(i, gate):
        first = Far(after(qkv_one[i].array, *gate))
        grad_qkv_one[i], acc, *edge, branch = call(
            functools.partial(self_backward_kernel, size, i),
            "self_backward",
            [
                *branch_one[i],
                weights_one,
                first,
                probs_one[i],
                qkv_one[0] if i else keys["edge"],
            ],
            [
                ((half, 3 * width), BF),
                ((heads, BLOCK, 2 * BLOCK), F32, "far"),
                *[((2 * width, BLOCK), F32)] * i,
                far((half, features)),
            ],
            [
                pltpu.VMEM((half + BLOCK, 2 * width), BF),
                pltpu.VMEM((2 * width, half + BLOCK), F32),
                pltpu.VMEM((half, width), BF),
            ],
            us=2.0,
            raw=2,
            lazy=True,
            fetch=True,
        )
        bias_acc[i], branches_one[i] = Far(acc), Far(branch)
        if edge:
            keys["edge"] = edge[0]
        return [grad_qkv_one[i]]

    def halves(left, right):
        return [(left[i], right[i]) for i in order]

    def make_keys(gate):
        keys["kv"], enc = call(
            functools.partial(cross_keys_kernel, width),
            "cross_keys",
            [*both_pieces, Far(after(weights_two, *gate))],
            [far((enc_length, 2 * width)), far((enc_length, features))],
            us=2.5,
            raw=4,
        )
        keys["enc"] = Far(enc)
        return keys["kv"]

    def ffn_weights(gate):
        held = {i: Far(after(hidden[i].array, *gate)) for i in order}
        blocks = weight_blocks(
            [halves(norms_three, active), halves(cot_half, held)], 2 * units, features, "ffn_weights"
        )
        keys["ffn"] = blocks
        return blocks[0]

    def layer_parts(gate):
        held = [hidden[0], Far(after(hidden[1].array, *gate))]
        layer = scatter_halves(held, weights_three, units, "layer_scatter")
        grads["layer"] = own_of(second) + sum(part.astype(F32) for part in layer)
        cross = scatter_rows_lower(after(keys["cross"][0], layer[0]), keys["cross"][1])
        grads["both"] = scatter_rows_upper(jnp.concatenate([grads["ffn"], cross], 2))
        return key_parts([layer[0]])

    def cross_weights(gate):
        grads["ffn"] = scatter_rows_lower(after(keys["ffn"][0], *gate), keys["ffn"][1])
        gate = gate + [grads["ffn"]]
        blocks = weight_blocks(
            [
                halves(norms_two, grad_query_two),
                [(keys["enc"], after(keys["grad"][0], *gate))],
                halves(branches_two, context_two),
            ],
            4 * width,
            features,
            "cross_weights",
        )
        keys["cross"] = blocks
        return blocks[0]

    def key_parts(gate):
        key_parts = call(
            functools.partial(scatter_keys_kernel, width),
            "scatter_keys",
            [after(keys["grad"][0], *gate), Far(weights_two)],
            [(piece, BF)] * 4,
            us=2.0,
        )
        across = send(chip_sum(key_parts[2], key_parts[3]), "heads", 2)
        grads["encoded"] = (
            key_parts[0].astype(F32)
            + send(key_parts[1], "heads", 1).astype(F32)
            + across.astype(F32)
        )
        return key_parts[0]

    keys = {"grad": [], "edge": []}
    grads = {}
    filler = {2: make_keys, 6: ffn_weights, 8: cross_weights, 9: layer_parts}
    stages = [self_forward, cross_forward, feed_forward, cross_backward, self_backward]
    gate, pending, step = [], None, 0
    for stage in stages:
        for i in order:
            result = stage(i, gate)
            gate = [result[0]]
            step += 1
            if step in filler:
                gate = [filler[step](gate)]
            if pending:
                gate = [pending[0](pending[1], gate)]
                pending = None
            if stage is self_backward:
                continue
            near, away, finish = result
            one = chip_sum(after(near, *gate), away)
            gate = [one]
            pending = (finish, one)
    input_parts = scatter_halves(grad_qkv_one, weights_one, 0, "input_scatter")
    bias_sums = call(
        functools.partial(bias_grad_kernel, starts),
        "bias_grad",
        [bias_acc[0], bias_acc[1]],
        [((heads, buckets, 2 * BLOCK), F32)],
        us=1.0,
    )[0]
    self_blocks = weight_blocks(
        [
            halves(norm_one, [after(grad_qkv_one[0], input_parts[0]), grad_qkv_one[1]]),
            halves(branches_one, context_one),
        ],
        4 * width,
        features,
        "self_weights",
        bias_sums,
    )
    (input_grad,) = backward_norm(
        input_parts,
        inputs,
        own_of(grad_after_self),
        gain_one,
        branch=False,
    )
    self_half = scatter_rows_lower(after(self_blocks[0], input_grad), self_blocks[1])
    self_got = scatter_rows_upper(after(self_half, grads["both"]))
    both_grad, self_grad = sum_rows(grads["both"]), sum_rows(self_got)
    bias_grad = self_grad[0, : heads * buckets].reshape(heads, buckets)
    self_grad = self_grad[SUM_ROWS:]
    ffn_grad, cross_grad = both_grad[:, : 2 * units], both_grad[:, 2 * units :]

    def along(weights, gradient):
        return jnp.sum(
            jnp.concatenate([w.astype(F32) for w in weights], 1) * gradient, axis=1
        )

    gain_grads = jnp.stack(
        [
            along([self_query, self_key, self_value], self_grad[:, : 3 * width]),
            along([cross_query], cross_grad[:, :width]),
            along([inner_weight], ffn_grad[:, :units]),
        ]
    )
    for bits in (1, 2):
        gain_grads = gain_grads + send(gain_grads, "heads", bits)
    gain_grads = lax.dynamic_slice_in_dim(gain_grads, me * each, each, 1) / jnp.stack(
        [gain_first, gain_second, gain_third]
    ).astype(F32)

    return (
        grads["layer"].astype(BF)[None],
        input_grad[None],
        grads["encoded"][None],
        self_grad[:, :width],
        self_grad[:, width : 2 * width],
        self_grad[:, 2 * width : 3 * width],
        self_grad[:, 3 * width :].T,
        cross_grad[:, :width],
        cross_grad[:, width : 2 * width],
        cross_grad[:, 2 * width : 3 * width],
        cross_grad[:, 3 * width :].T,
        ffn_grad[:, :units],
        ffn_grad[:, units:].T,
        bias_grad.T,
        gain_grads[0],
        gain_grads[1],
        gain_grads[2],
    )


def solution(mesh):
    positions = P("rows", "heads", None)
    columns = P("rows", "heads")
    lines = P("heads", "rows")
    gains = P(("rows", "heads"))
    return jax.shard_map(
        shards,
        mesh=mesh,
        in_specs=(
            positions,
            positions,
            positions,
            P("rows", None),
            P("rows", None),
            columns,
            columns,
            columns,
            lines,
            columns,
            columns,
            columns,
            lines,
            columns,
            lines,
            P(None, "heads"),
            gains,
            gains,
            gains,
        ),
        out_specs=(
            positions,
            positions,
            positions,
            columns,
            columns,
            columns,
            lines,
            columns,
            columns,
            columns,
            lines,
            columns,
            lines,
            P(None, "heads"),
            gains,
            gains,
            gains,
        ),
        check_vma=False,
    )
```

```python
import functools

import jax
import jax.numpy as jnp
import numpy as np
from jax import lax
from jax.experimental import pallas as pl
from jax.experimental.pallas import tpu as pltpu
from jax.sharding import PartitionSpec as P

MAX_DISTANCE = 128
EPS = 1e-06
NEG = -1000000000.0
LEAST = 96
MOST = 128
BLOCK = 128
SUM_ROWS = 16
BF = jnp.bfloat16
F32 = jnp.float32
VMEM = pl.BlockSpec(memory_space=pltpu.VMEM)
SMEM = pl.BlockSpec(memory_space=pltpu.SMEM)


def bucket_starts(bucket_count, max_reach):
    exact_span = bucket_count // 2
    starts = list(range(exact_span + 1))
    for target in range(exact_span + 1, bucket_count):
        distance = exact_span
        while (
            distance < max_reach
            and exact_span
            + int(
                np.log(distance / exact_span)
                / np.log(max_reach / exact_span)
                * (bucket_count - exact_span)
            )
            < target
        ):
            distance += 1
        starts.append(distance)
    return starts


COST = {'place': 1.5, 'pair': 1.5, 'bias': 2.0, 'self_forward': 2.0, 'norm_forward': 1.0, 'cross_keys': 2.5, 'cross_forward': 4.0, 'ffn': 5.0, 'cross_backward': 1.0, 'self_backward': 2.0, 'norm_backward': 1.5, 'input_norm': 1.5, 'ffn_weights': 4.0, 'cross_weights': 0.04, 'self_weights': 4.0, 'layer_scatter': 2.0, 'input_scatter': 2.0, 'scatter_keys': 2.0, 'bias_grad': 1.0}


class Far:
    def __init__(self, array):
        self.array = array


class Moves:
    def __init__(self, sems):
        self.sems, self.used = sems, 0
        self.coming, self.going, self.started = [], [], []

    def copy(self, source, target):
        made = pltpu.make_async_copy(source, target, self.sems.at[self.used])
        self.used += 1
        made.start()
        return made

    def need(self, *refs):
        for ref in refs:
            for k, (held, made) in enumerate(self.coming):
                if held is ref:
                    made.wait()
                    del self.coming[k]
                    break

    def need_all(self):
        self.need(*[held for held, made in self.coming])

    def send(self, source, target):
        self.started.append(self.copy(source, target))

    def ready(self, *refs):
        for ref in refs:
            for k, (held, target) in enumerate(self.going):
                if held is ref:
                    self.send(held, target)
                    del self.going[k]
                    break

    def finish(self):
        self.need_all()
        self.ready(*[held for held, target in self.going])
        for made in self.started:
            made.wait()


HBM = pl.BlockSpec(memory_space=pltpu.HBM)


def call(body, name, args, outs, scratch=(), us=2.0, smem=0, raw=0, moved=0, lazy=False, fetch=False, key=None):
    far_in = [fetch and isinstance(x, Far) for x in args]
    arrays = [
        pltpu.with_memory_space_constraint(x.array, pltpu.HBM)
        if f
        else x.array
        if isinstance(x, Far)
        else x
        for x, f in zip(args, far_in)
    ]
    far_out = [len(o) > 2 for o in outs]
    last = len(outs) - (raw > 0)
    held = [pltpu.VMEM(x.shape, x.dtype) for x, f in zip(arrays, far_in) if f]
    held += [pltpu.VMEM(o[0], o[1]) for o, f in zip(outs[:last], far_out) if f]
    copies = len(held) + raw + moved
    if copies:
        held.append(pltpu.SemaphoreType.DMA((copies,)))

    def kernel(*refs):
        ins, results = refs[: len(args)], refs[len(args) : len(args) + len(outs)]
        own = refs[len(args) + len(outs) : len(args) + len(outs) + len(scratch)]
        spare = list(refs[len(args) + len(outs) + len(scratch) :])
        moves = Moves(spare.pop() if copies else None)
        given = []
        for ref, f in zip(ins, far_in):
            if f:
                here = spare.pop(0)
                moves.coming.append((here, moves.copy(ref, here)))
                ref = here
            given.append(ref)
        for k, ref in enumerate(results):
            if far_out[k] and k < last:
                here = spare.pop(0)
                moves.going.append((here, ref))
                ref = here
            given.append(ref)
        if not lazy:
            moves.need_all()
        body(moves, *given, *own)
        moves.finish()

    return pl.pallas_call(
        kernel,
        out_shape=[
            (pltpu.HBM if f else jax.ShapeDtypeStruct)(o[0], o[1])
            for o, f in zip(outs, far_out)
        ],
        in_specs=[SMEM] * smem + [HBM if f else VMEM for f in far_in[smem:]],
        out_specs=[HBM if f else VMEM for f in far_out],
        scratch_shapes=list(scratch) + held,
        compiler_params=pltpu.CompilerParams(vmem_limit_bytes=16 << 20),
        name=name,
        cost_estimate=pl.CostEstimate(
            flops=int(COST.get(key or name, us) * 1e9),
            bytes_accessed=int(COST.get(key or name, us) * 3e6),
            transcendentals=0,
        ),
    )(*arrays)


def send(part, axis, bits):
    count = lax.axis_size(axis)
    return lax.ppermute(part, axis, [(i, i ^ bits) for i in range(count)])


def after(value, *others):
    return lax.optimization_barrier((value,) + others)[0]


def gather_heads(part):
    across = send(part, "heads", 2)
    return [part, send(part, "heads", 1), across, send(across, "heads", 1)]


def place_kernel(count, moves, *refs):
    me = lax.axis_index("rows")
    for t in range(count):
        moves.send(refs[t], refs[count].at[me ^ t])


def pair_kernel(moves, near, other, out):
    lower = lax.axis_index("rows") % 2
    moves.send(near, out.at[:, lower])
    moves.send(other, out.at[:, 1 - lower])


def gather_rows_first(part):
    return [part] + [
        send(part, "rows", 2 * upper) for upper in range(1, lax.axis_size("rows") // 2)
    ]


def gather_rows_second(firsts):
    pieces = []
    for near in firsts:
        pieces += [near, send(near, "rows", 1)]
    return pieces


def lay_rows(pieces, *others):
    count = len(pieces)
    shape = (count,) + pieces[0].shape
    pieces = [after(pieces[0], *others)] + pieces[1:]
    placed = call(
        functools.partial(place_kernel, count), "place", pieces, [(shape, BF)], us=1.5, moved=count
    )[0]
    return placed.reshape(-1, shape[2])


def upper_groups():
    count = lax.axis_size("rows")
    return [list(range(lower, count, 2)) for lower in range(2)]


def gather_rows_upper(part):
    count = lax.axis_size("rows") // 2
    spread = jnp.broadcast_to(part[None], (count,) + part.shape)
    return lax.all_to_all(
        spread, "rows", 0, 0, tiled=True, axis_index_groups=upper_groups()
    )


def gather_rows_lower(near):
    count, rows, lanes = near.shape
    placed = call(
        pair_kernel,
        "pair",
        [near, send(near, "rows", 1)],
        [((count, 2, rows, lanes), BF)],
        us=1.5,
        moved=2,
    )[0]
    return placed.reshape(-1, lanes)


def scatter_rows_lower(keep, away):
    return (keep.astype(F32) + send(away, "rows", 1).astype(F32)).astype(BF)


def scatter_rows_upper(blocks):
    return lax.all_to_all(blocks, "rows", 0, 0, tiled=True, axis_index_groups=upper_groups())


def sum_rows(got):
    return jnp.sum(got.astype(F32), axis=0)


def dot(a, b, dims):
    return lax.dot_general(a, b, (dims, ((), ())), preferred_element_type=F32)


NT = ((1,), (1,))
NN = ((1,), (0,))
TN = ((0,), (0,))


def core_and_chip():
    me = lax.axis_index("heads")
    return me % 2, me // 2


def rms_rows(values, gain):
    factor = lax.rsqrt(jnp.mean(values * values, axis=-1, keepdims=True) + EPS)
    return (values * factor * gain).astype(BF)


def pick_half(half, pieces, out):
    unused, chip = core_and_chip()
    quarter = pieces[0].shape[0]
    for near in (True, False):

        @pl.when((chip == half) == near)
        def _(near=near):
            for s in range(2):
                out[s * quarter : (s + 1) * quarter, :] = pieces[s + (0 if near else 2)][...]


def distances(first, rows):
    query = lax.broadcasted_iota(jnp.int32, (rows, 2 * BLOCK), 0) + (first + BLOCK)
    return query - lax.broadcasted_iota(jnp.int32, (rows, 2 * BLOCK), 1)


def bias_kernel(starts, moves, table_ref, out_ref):
    heads = out_ref.shape[0]
    step = 32

    def rows(t, carry):
        first = pl.multiple_of(t * step, step)
        reach = distances(first, step)
        values = [jnp.full((step, 2 * BLOCK), table_ref[0, h], F32) for h in range(heads)]
        for b in range(1, len(starts)):
            beyond = reach >= starts[b]
            values = [jnp.where(beyond, table_ref[b, h], values[h]) for h in range(heads)]
        for h in range(heads):
            out_ref[h, pl.ds(first, step), :] = values[h]
        return carry

    lax.fori_loop(0, BLOCK // step, rows, 0)


def bias_grad_kernel(starts, moves, one_ref, two_ref, out_ref):
    reach = distances(0, BLOCK)
    for h in range(one_ref.shape[0]):
        acc = one_ref[h] + two_ref[h]
        for b in range(len(starts)):
            inside = reach < starts[1] if b == 0 else reach >= starts[b]
            if 0 < b < len(starts) - 1:
                inside = inside & (reach < starts[b + 1])
            out_ref[h, b : b + 1, :] = jnp.sum(jnp.where(inside, acc, 0.0), axis=0, keepdims=True)


def running(lengths_ref, count):
    total = lengths_ref[0, 0]
    ends = [total]
    for c in range(1, count):
        total = total + lengths_ref[0, c]
        ends.append(total)
    return ends


def slot_of(block, core, quarter):
    each = quarter // BLOCK
    return pl.multiple_of((((block // each) ^ core) * each + block % each) * BLOCK, BLOCK)


def softmax(scores):
    e = jnp.exp(scores - jnp.max(scores, axis=-1, keepdims=True))
    return (e * (1.0 / jnp.sum(e, axis=-1, keepdims=True))).astype(BF)


def self_forward_kernel(size, half, moves, lengths_ref, *refs):
    pieces = refs[:4]
    gain_ref, w_ref, bias_ref = refs[4:7]
    norm_ref, qkv_ref, context_ref, probs_ref, own_ref, near_ref, far_ref = refs[7:14]
    x, kv = refs[14:]
    heads = bias_ref.shape[0]
    width = heads * size
    quarter = own_ref.shape[0]
    core, chip = core_and_chip()
    ends = running(lengths_ref, lengths_ref.shape[1])
    blocks = 2 * quarter // BLOCK
    gain = gain_ref[...]
    moves.need(*pieces)
    pick_half(half, pieces, x)
    own_ref[...] = x[:quarter, :]
    moves.need(w_ref)

    if half:
        for k in range(4):

            @pl.when((core == 1 - k % 2) & ((chip == 0) == (k < 2)))
            def _(k=k):
                norm_ref[:BLOCK, :] = pieces[k][quarter - BLOCK :, :]

        before = rms_rows(norm_ref[:BLOCK, :].astype(F32), gain)
        kv[:BLOCK, :] = dot(before, w_ref[:, width : 3 * width], NN).astype(BF)
    else:
        kv[:BLOCK, :] = jnp.zeros((BLOCK, 2 * width), BF)

    def project(b, carry):
        at = pl.multiple_of(slot_of(b, core, quarter), BLOCK)
        norm = rms_rows(x[pl.ds(at, BLOCK), :].astype(F32), gain)
        norm_ref[pl.ds(at, BLOCK), :] = norm
        qkv = dot(norm, w_ref[:, : 3 * width], NN).astype(BF)
        qkv_ref[pl.ds(at, BLOCK), :] = qkv
        kv[pl.ds(pl.multiple_of((b + 1) * BLOCK, BLOCK), BLOCK), :] = qkv[:, width:]
        return carry

    lax.fori_loop(0, blocks, project, 0)
    moves.ready(norm_ref, qkv_ref)
    moves.need(bias_ref)

    def block(b, carry):
        own = slot_of(b, core, quarter)
        at = pl.multiple_of(b * BLOCK, BLOCK)
        base = (half * blocks + b) * BLOCK
        query = base + lax.broadcasted_iota(jnp.int32, (BLOCK, 1), 0)
        start = jnp.zeros((BLOCK, 1), jnp.int32)
        for end in ends:
            start = jnp.where(query >= end, end, start)
        key = base - BLOCK + lax.broadcasted_iota(jnp.int32, (BLOCK, 2 * BLOCK), 1)
        allowed = (key >= start) & (key <= query)
        outs = []
        for h in range(heads):
            q = qkv_ref[pl.ds(own, BLOCK), h * size : (h + 1) * size]
            k = kv[pl.ds(at, 2 * BLOCK), h * size : (h + 1) * size]
            v = kv[pl.ds(at, 2 * BLOCK), width + h * size : width + (h + 1) * size]
            probs = softmax(jnp.where(allowed, dot(q, k, NT) + bias_ref[h], NEG))
            probs_ref[b, h] = probs
            outs.append(dot(probs, v, NN).astype(BF))
        context_ref[pl.ds(own, BLOCK), :] = jnp.concatenate(outs, 1)
        return carry

    lax.fori_loop(0, blocks, block, 0)
    moves.ready(context_ref, probs_ref)
    out_weight = w_ref[:, 3 * width : 4 * width]
    far_ref[...] = dot(context_ref[quarter:, :], out_weight, NT).astype(BF)
    near_ref[...] = dot(context_ref[:quarter, :], out_weight, NT).astype(BF)


def self_backward_kernel(size, half, moves, *refs):
    own_ref, other_ref, w_ref, qkv_ref, probs_ref, edge_in = refs[:6]
    out_ref, acc_ref = refs[6:8]
    branch_ref = refs[-4]
    kv, key_acc, grad = refs[-3:]
    heads = acc_ref.shape[0]
    width = heads * size
    quarter = own_ref.shape[0]
    core, chip = core_and_chip()
    blocks = 2 * quarter // BLOCK
    moves.send(own_ref, branch_ref.at[:quarter])
    moves.send(other_ref, branch_ref.at[quarter:])
    key_acc[...] = jnp.zeros_like(key_acc)
    acc_ref[...] = jnp.zeros_like(acc_ref)
    moves.need(w_ref)
    out_weight = w_ref[:, 3 * width : 4 * width]
    grad[:quarter, :] = dot(own_ref[...], out_weight, NN).astype(BF)
    grad[quarter:, :] = dot(other_ref[...], out_weight, NN).astype(BF)
    moves.need(edge_in, qkv_ref)
    if half:
        kv[:BLOCK, :] = edge_in[pl.ds(slot_of(blocks - 1, core, quarter), BLOCK), width:]
    else:
        kv[:BLOCK, :] = jnp.zeros((BLOCK, 2 * width), BF)
        key_acc[:, blocks * BLOCK :] = edge_in[...]
    for b in range(blocks):
        kv[(b + 1) * BLOCK : (b + 2) * BLOCK, :] = qkv_ref[
            pl.ds(slot_of(b, core, quarter), BLOCK), width:
        ]
    moves.need(probs_ref)

    def block(b, carry):
        own = slot_of(b, core, quarter)
        at = pl.multiple_of(b * BLOCK, BLOCK)
        grads_q, grads_k, grads_v = [], [], []
        for h in range(heads):
            q = qkv_ref[pl.ds(own, BLOCK), h * size : (h + 1) * size]
            k = kv[pl.ds(at, 2 * BLOCK), h * size : (h + 1) * size]
            v = kv[pl.ds(at, 2 * BLOCK), width + h * size : width + (h + 1) * size]
            c = grad[pl.ds(own, BLOCK), h * size : (h + 1) * size]
            probs = probs_ref[b, h]
            wide = probs.astype(F32)
            grad_probs = dot(c, v, NT)
            inner = jnp.sum(grad_probs * wide, axis=-1, keepdims=True)
            grad_scores = wide * (grad_probs - inner)
            acc_ref[h] += grad_scores
            short = grad_scores.astype(BF)
            grads_q.append(dot(short, k, NN).astype(BF))
            grads_k.append(dot(q.T, short, NN))
            grads_v.append(dot(c.T, probs, NN))
        out_ref[pl.ds(own, BLOCK), :width] = jnp.concatenate(grads_q, 1)
        key_acc[:, pl.ds(at, 2 * BLOCK)] += jnp.concatenate(grads_k + grads_v, 0)
        return carry

    lax.fori_loop(0, blocks, block, 0)
    for b in range(blocks):
        out_ref[pl.ds(slot_of(b, core, quarter), BLOCK), width:] = key_acc[
            :, (b + 1) * BLOCK : (b + 2) * BLOCK
        ].T.astype(BF)
    if half:
        refs[8][...] = key_acc[:, :BLOCK]


def cross_keys_kernel(width, moves, *refs):
    pieces, w_ref = refs[:4], refs[4]
    kv_ref, enc_ref = refs[5:]
    quarter = pieces[0].shape[1]
    me = lax.axis_index("heads")
    weight = w_ref[:, width : 3 * width]
    for k in range(4):
        at = pl.ds(pl.multiple_of((me ^ k) * quarter, quarter), quarter)
        moves.send(pieces[k].at[0], enc_ref.at[at])
        kv_ref[at, :] = dot(pieces[k][0], weight, NN).astype(BF)


def cross_window(block, dec_ends, enc_ends, enc_length, window):
    first = jnp.int32(0)
    for c in range(len(dec_ends) - 1):
        first = jnp.where(block * BLOCK >= dec_ends[c], enc_ends[c], first)
    return pl.multiple_of(
        jnp.minimum(first // BLOCK * BLOCK, enc_length - window), BLOCK
    )


def cross_forward_kernel(size, half, moves, dec_ref, enc_ref, own_ref, other_ref, w_ref, kv_ref, *refs):
    query_ref, context_ref, near_ref, far_ref = refs[:4]
    all_probs, norm_ref = refs[4:-1], refs[-1]
    heads = refs[4].shape[1]
    width = heads * size
    quarter = own_ref.shape[0]
    core, chip = core_and_chip()
    first = half * (2 * quarter // BLOCK)
    enc_length = kv_ref.shape[0]
    comments = dec_ref.shape[1]
    dec_ends = running(dec_ref, comments)
    enc_ends = running(enc_ref, comments)
    moves.send(own_ref, norm_ref.at[:quarter])
    moves.send(other_ref, norm_ref.at[quarter:])
    moves.need(w_ref)
    query_ref[:quarter, :] = dot(own_ref[...], w_ref[:, :width], NN).astype(BF)
    query_ref[quarter:, :] = dot(other_ref[...], w_ref[:, :width], NN).astype(BF)
    moves.ready(query_ref)
    moves.need(kv_ref)
    done = 0
    for probs_ref in all_probs:
        window = probs_ref.shape[3]

        def block(b, carry, window=window, probs_ref=probs_ref, done=done):
            own = slot_of(b, core, quarter)
            base = (first + b) * BLOCK
            start = (
                cross_window(first + b, dec_ends, enc_ends, enc_length, window)
                if window < enc_length
                else 0
            )
            query = base + lax.broadcasted_iota(jnp.int32, (BLOCK, 1), 0)
            low = jnp.zeros((BLOCK, 1), jnp.int32)
            high = jnp.full((BLOCK, 1), enc_ends[0], jnp.int32)
            for c in range(comments):
                later = query >= dec_ends[c]
                last = c == comments - 1
                low = jnp.where(later, 0 if last else enc_ends[c], low)
                high = jnp.where(later, enc_length if last else enc_ends[c + 1], high)
            key = start + lax.broadcasted_iota(jnp.int32, (BLOCK, window), 1)
            allowed = (key >= low) & (key < high)
            contexts = []
            for h in range(heads):
                q = query_ref[pl.ds(own, BLOCK), h * size : (h + 1) * size]
                k = kv_ref[pl.ds(start, window), h * size : (h + 1) * size]
                v = kv_ref[pl.ds(start, window), width + h * size : width + (h + 1) * size]
                probs = softmax(jnp.where(allowed, dot(q, k, NT), NEG))
                probs_ref[b - done, h] = probs
                contexts.append(dot(probs, v, NN).astype(BF))
            context_ref[pl.ds(own, BLOCK), :] = jnp.concatenate(contexts, 1)
            return carry

        lax.fori_loop(done, done + probs_ref.shape[0], block, 0)
        done += probs_ref.shape[0]
        moves.ready(probs_ref)
    moves.ready(context_ref)
    out_weight = w_ref[:, 3 * width :]
    far_ref[...] = dot(context_ref[quarter:, :], out_weight, NT).astype(BF)
    near_ref[...] = dot(context_ref[:quarter, :], out_weight, NT).astype(BF)


def cross_backward_kernel(size, half, kinds, more, moves, dec_ref, enc_ref, *refs):
    own_ref, other_ref, w_ref, query_ref, kv_ref = refs[:5]
    probs_refs = refs[5 : 5 + kinds]
    so_far = refs[5 + kinds : 5 + kinds + more]
    grad_q_ref, grad_kv_ref, near_ref, far_ref, branch_ref, key_acc, grad = refs[5 + kinds + more :]
    heads = probs_refs[0].shape[1]
    width = heads * size
    quarter = own_ref.shape[0]
    core, chip = core_and_chip()
    first = half * (2 * quarter // BLOCK)
    enc_length = kv_ref.shape[0]
    comments = dec_ref.shape[1]
    dec_ends = running(dec_ref, comments)
    enc_ends = running(enc_ref, comments)
    moves.send(own_ref, branch_ref.at[:quarter])
    moves.send(other_ref, branch_ref.at[quarter:])
    key_acc[...] = so_far[0][...] if more else jnp.zeros_like(key_acc)
    moves.need(w_ref)
    out_weight = w_ref[:, 3 * width :]
    grad[:quarter, :] = dot(own_ref[...], out_weight, NN).astype(BF)
    grad[quarter:, :] = dot(other_ref[...], out_weight, NN).astype(BF)
    moves.need(query_ref, kv_ref)
    done = 0
    for probs_ref in probs_refs:
        moves.need(probs_ref)
        window = probs_ref.shape[3]

        def block(b, carry, window=window, probs_ref=probs_ref, done=done):
            own = slot_of(b, core, quarter)
            start = (
                cross_window(first + b, dec_ends, enc_ends, enc_length, window)
                if window < enc_length
                else 0
            )
            grads_q, grads_k, grads_v = [], [], []
            for h in range(heads):
                q = query_ref[pl.ds(own, BLOCK), h * size : (h + 1) * size]
                k = kv_ref[pl.ds(start, window), h * size : (h + 1) * size]
                v = kv_ref[pl.ds(start, window), width + h * size : width + (h + 1) * size]
                c = grad[pl.ds(own, BLOCK), h * size : (h + 1) * size]
                probs = probs_ref[b - done, h]
                wide = probs.astype(F32)
                grad_probs = dot(c, v, NT)
                inner = jnp.sum(grad_probs * wide, axis=-1, keepdims=True)
                short = (wide * (grad_probs - inner)).astype(BF)
                grads_q.append(dot(short, k, NN).astype(BF))
                grads_k.append(dot(q.T, short, NN))
                grads_v.append(dot(c.T, probs, NN))
            grad_q_ref[pl.ds(own, BLOCK), :] = jnp.concatenate(grads_q, 1)
            key_acc[:, pl.ds(start, window)] += jnp.concatenate(grads_k + grads_v, 0)
            return carry

        lax.fori_loop(done, done + probs_ref.shape[0], block, 0)
        done += probs_ref.shape[0]
    grad_kv_ref[...] = (key_acc[...].T if more else key_acc[...]).astype(grad_kv_ref.dtype)
    weight = w_ref[:, :width]
    far_ref[...] = dot(grad_q_ref[quarter:, :], weight, NT).astype(BF)
    near_ref[...] = dot(grad_q_ref[:quarter, :], weight, NT).astype(BF)


def ffn_kernel(half, moves, own_ref, other_ref, *refs):
    pieces, w_ref = refs[:4], refs[4]
    cot_ref, hidden_ref, active_ref, own_cot_ref, near_ref, far_ref, norms_ref, norms = refs[5:]
    quarter = own_ref.shape[0]
    units = hidden_ref.shape[1]
    part = 256 if units % 256 == 0 else units
    moves.send(own_ref, norms_ref.at[:quarter])
    moves.send(other_ref, norms_ref.at[quarter:])
    pick_half(half, [part.at[1] for part in pieces], cot_ref)
    own_cot_ref[...] = cot_ref[:quarter, :]
    moves.ready(cot_ref)
    moves.need(w_ref)
    norms[:quarter, :] = own_ref[...]
    norms[quarter:, :] = other_ref[...]

    def rows(t, carry):
        at = pl.ds(pl.multiple_of(t * BLOCK, BLOCK), BLOCK)
        norm = norms[at, :]
        cot = cot_ref[at, :]
        for f in range(0, units, part):
            active = dot(norm, w_ref[:, f : f + part], NN)
            grad = dot(cot, w_ref[:, units + f : units + f + part], NN)
            share = 0.5 + 0.5 * lax.erf(active * np.float32(np.sqrt(0.5)))
            slope = share + active * (
                jnp.exp(-0.5 * active * active) * np.float32(1.0 / np.sqrt(2.0 * np.pi))
            )
            hidden_ref[at, f : f + part] = (active * share).astype(BF)
            active_ref[at, f : f + part] = (grad * slope).astype(BF)
        return carry

    lax.fori_loop(0, 2 * quarter // BLOCK, rows, 0)
    moves.ready(hidden_ref, active_ref)
    weight = w_ref[:, :units]
    far_ref[...] = dot(active_ref[quarter:, :], weight, NT).astype(BF)
    near_ref[...] = dot(active_ref[:quarter, :], weight, NT).astype(BF)


def scatter_kernel(first, moves, one_ref, two_ref, w_ref, far_far, far_near, near_far, near_near, picked):
    unused, chip = core_and_chip()
    quarter = far_far.shape[0]
    weight = w_ref[:, first : first + one_ref.shape[1]]
    for index in range(2):

        @pl.when(chip == index)
        def _(index=index):
            picked[0] = (two_ref, one_ref)[index][...]
            picked[1] = (one_ref, two_ref)[index][...]

    far_far[...] = dot(picked[0, quarter:, :], weight, NT).astype(BF)
    near_far[...] = dot(picked[1, quarter:, :], weight, NT).astype(BF)
    far_near[...] = dot(picked[0, :quarter, :], weight, NT).astype(BF)
    near_near[...] = dot(picked[1, :quarter, :], weight, NT).astype(BF)


def scatter_keys_kernel(width, moves, grad_ref, w_ref, *outs):
    quarter = outs[0].shape[0]
    me = lax.axis_index("heads")
    weight = w_ref[:, width : 3 * width]
    for k in range(4):
        at = pl.ds(pl.multiple_of((me ^ k) * quarter, quarter), quarter)
        outs[k][...] = dot(grad_ref[at, :], weight, NT).astype(outs[k].dtype)


def norm_forward_kernel(moves, one_ref, two_ref, base_ref, gain_ref, sum_ref, norm_ref):
    rows = base_ref.shape[0]
    step = min(64, rows)

    def some(t, carry):
        at = pl.ds(pl.multiple_of(t * step, step), step)
        total = base_ref[at, :].astype(F32) + one_ref[at, :].astype(F32) + two_ref[at, :].astype(F32)
        sum_ref[at, :] = total
        norm_ref[at, :] = rms_rows(total, gain_ref[...])
        return carry

    lax.fori_loop(0, rows // step, some, 0)


def norm_backward_kernel(parts, moves, *refs):
    values_ref, base_ref, gain_ref = refs[parts : parts + 3]
    grad_ref, *branch_ref = refs[parts + 3 :]
    rows = values_ref.shape[0]
    step = min(64, rows)

    def some(t, carry):
        at = pl.ds(pl.multiple_of(t * step, step), step)
        grad = refs[0][at, :].astype(F32)
        for part in refs[1:parts]:
            grad = grad + part[at, :].astype(F32)
        values = values_ref[at, :].astype(F32)
        factor = lax.rsqrt(jnp.mean(values * values, axis=-1, keepdims=True) + EPS)
        scaled = gain_ref[...] * grad
        mean = jnp.mean(scaled * values, axis=-1, keepdims=True)
        total = (
            base_ref[at, :].astype(F32)
            + factor * scaled
            - values * (factor * factor * factor * mean)
        )
        grad_ref[at, :] = total
        if branch_ref:
            branch_ref[0][at, :] = total.astype(BF)
        return carry

    lax.fori_loop(0, rows // step, some, 0)


def weights_kernel(segments, sums, moves, *refs):
    keep_ref, away_ref, whole = refs[-3:]
    features = whole.shape[0]
    ahead = SUM_ROWS if sums else 0
    group = keep_ref.shape[1] - ahead
    lower = lax.axis_index("rows") % 2
    if sums:
        ones = jnp.ones((8, refs[0].shape[2]), F32)
        lines = [
            lax.dot_general(ones, refs[0][h], (NT, ((), ())), precision=lax.Precision.HIGHEST)
            for h in range(refs[0].shape[0])
        ]
        line = jnp.concatenate(lines + lines, 1)[:, : lines[0].shape[1] * len(lines)].astype(BF)
        line = jnp.concatenate([line] * (SUM_ROWS // 8), 0)
        for out in (keep_ref, away_ref):
            for k in range(out.shape[0]):
                out[k, :SUM_ROWS, :] = jnp.zeros((SUM_ROWS, out.shape[2]), BF)
                out[k, :SUM_ROWS, : line.shape[1]] = line
    step = 384 if features % 384 == 0 else BLOCK
    to = 0
    for pairs in segments:
        for left, right in pairs:
            moves.need(refs[left], refs[right])
        lanes = refs[pairs[0][1]].shape[1]

        def rows(j, carry, pairs=pairs, to=to, lanes=lanes):
            at = pl.ds(pl.multiple_of(j * step, step), step)
            total = sum(dot(refs[left][:, at], refs[right][...], TN) for left, right in pairs)
            whole[at, to : to + lanes] = total.astype(BF)
            return carry

        lax.fori_loop(0, features // step, rows, 0)
        to += lanes
    for r in range(features // group):
        block = slice(r * group, (r + 1) * group)

        @pl.when(lower == r % 2)
        def _(r=r, block=block):
            keep_ref[r // 2, ahead:, :] = whole[block, :]

        @pl.when(lower != r % 2)
        def _(r=r, block=block):
            away_ref[r // 2, ahead:, :] = whole[block, :]


def weight_blocks(segments, lanes, features, key, sums=None):
    operands, index = [] if sums is None else [sums], {}

    def number(operand):
        key = id(operand.array if isinstance(operand, Far) else operand)
        if key not in index:
            index[key] = len(operands)
            operands.append(operand)
        return index[key]

    numbered = [[(number(l), number(r)) for l, r in pairs] for pairs in segments]
    count = lax.axis_size("rows")
    return call(
        functools.partial(weights_kernel, numbered, sums is not None),
        "weights",
        operands,
        [((count // 2, features // count + SUM_ROWS * (sums is not None), lanes), BF)] * 2,
        [pltpu.VMEM((features, lanes), BF)],
        us=4.0,
        key=key,
        lazy=True,
        fetch=True,
    )


def shards(
    inputs,
    encoded,
    cotangent,
    dec_lengths,
    enc_lengths,
    self_query,
    self_key,
    self_value,
    self_output,
    cross_query,
    cross_key,
    cross_value,
    cross_output,
    inner_weight,
    outer_weight,
    bias_table,
    gain_first,
    gain_second,
    gain_third,
):
    groups = lax.axis_size("heads")
    devices = groups * lax.axis_size("rows")
    me = lax.axis_index("heads")
    chip = me // 2
    heads = bias_table.shape[1]
    buckets = bias_table.shape[0]
    width = self_query.shape[1]
    size = width // heads
    quarter = inputs.shape[1]
    half = 2 * quarter
    enc_quarter = encoded.shape[1]
    enc_length = enc_quarter * groups
    features = inputs.shape[2]
    units = inner_weight.shape[1]
    comments = dec_lengths.shape[1]
    starts = bucket_starts(buckets, MAX_DISTANCE)
    blocks = half // BLOCK
    window = 4 * MOST
    order = (1, 0)
    plain = [min(max(LEAST * comments // BLOCK - i * blocks, 0), blocks) for i in range(2)]
    piece = (quarter, features)

    inputs, encoded, cotangent = inputs[0], encoded[0], cotangent[0]

    gains = jnp.concatenate([gain_first, gain_second, gain_third])
    each = gain_first.shape[0]
    spread = jnp.broadcast_to(gains[None], (devices, 3 * each))
    spread = lax.all_to_all(spread, ("rows", "heads"), 0, 0, tiled=True).astype(F32)
    gain_one, gain_two, gain_three = (
        spread[:, i * each : (i + 1) * each].reshape(1, features) for i in range(3)
    )

    far = lambda shape: (shape, BF, "far")
    bias = call(
        functools.partial(bias_kernel, starts),
        "bias",
        [bias_table.astype(F32)],
        [((heads, BLOCK, 2 * BLOCK), F32, "far")],
        us=2.0,
        smem=1,
    )[0]

    weights_one = gather_rows_first(
        jnp.concatenate([self_query, self_key, self_value, self_output.T], 1)
    )
    inputs_pieces = gather_heads(inputs)
    pieces_one = gather_rows_second(
        weights_one[:1] + [after(part) for part in weights_one[1:]]
    )
    parts_two = [
        after(part, pieces_one[5])
        for part in (cross_query, cross_key, cross_value, cross_output)
    ]
    weights_one = lay_rows(pieces_one, spread, bias)
    weights_two = gather_rows_upper(jnp.concatenate(parts_two[:3] + [parts_two[3].T], 1))
    parts_three = [after(part, weights_two) for part in (inner_weight, outer_weight)]
    weights_three = gather_rows_upper(jnp.concatenate([parts_three[0], parts_three[1].T], 1))
    weights_two = gather_rows_lower(weights_two)
    weights_three = gather_rows_lower(weights_three)
    both_pieces = gather_heads(after(jnp.stack([encoded, cotangent]), inputs_pieces[2]))

    def chip_sum(near, far):
        return (near.astype(F32) + send(far, "heads", 1).astype(F32)).astype(BF)

    def forward_norm(one, base, gain, gate):
        total, norm = call(
            norm_forward_kernel,
            "norm_forward",
            [one, send(one, "heads", 2), base, after(gain, *gate)],
            [(piece, F32), (piece, BF)],
            us=1.0,
        )
        return Far(total), (norm, send(norm, "heads", 1))

    def backward_norm(parts, values, base, gain, branch=True):
        return call(
            functools.partial(norm_backward_kernel, len(parts)),
            "norm_backward",
            [*parts, values, base, gain],
            [(piece, F32)] + [(piece, BF)] * branch,
            us=1.5,
            key="norm_backward" if branch else "input_norm",
        )

    def backward_pair(one, values, base, gain, gate):
        grad, branch = backward_norm(
            [one, send(one, "heads", 2)], values, base, after(gain, *gate)
        )
        return grad, (branch, send(branch, "heads", 1))

    def own_of(pair):
        return jnp.where(chip == 0, *(x.array if isinstance(x, Far) else x for x in pair))

    def scatter_halves(pair, weight, first, key):
        far_far, far_near, near_far, near_near = call(
            functools.partial(scatter_kernel, first),
            "scatter",
            [pair[0], pair[1], Far(weight)],
            [(piece, BF)] * 4,
            [pltpu.VMEM((2, half, (pair[0].array if isinstance(pair[0], Far) else pair[0]).shape[1]), BF)],
            us=2.0,
            key=key,
        )
        across = send(chip_sum(far_near, far_far), "heads", 2)
        return [near_near, send(near_far, "heads", 1), across]

    parts = ((piece, BF), (piece, BF))
    none = [None, None]
    norms_two, norms_three, branches_two, branches_one = (list(none) for unused in range(4))
    norm_one, qkv_one, context_one, probs_one = list(none), list(none), list(none), list(none)
    after_self, norm_two = list(none), list(none)
    query_two, context_two, probs_two = list(none), list(none), list(none)
    second, norm_three = list(none), list(none)
    cot_half, hidden, active = list(none), list(none), list(none)
    grad_second, branch_two = list(none), list(none)
    grad_query_two, grad_after_self, branch_one = list(none), list(none), list(none)
    grad_qkv_one, bias_acc = list(none), list(none)

    def self_forward(i, gate):
        *saved, own, near, away = call(
            functools.partial(self_forward_kernel, size, i),
            "self_forward",
            [dec_lengths, *map(Far, inputs_pieces), after(gain_one, *gate), Far(weights_one), Far(bias)],
            [
                far((half, features)),
                far((half, 3 * width)),
                far((half, width)),
                far((blocks, heads, BLOCK, 2 * BLOCK)),
                (piece, BF),
                *parts,
            ],
            [
                pltpu.VMEM((half, features), BF),
                pltpu.VMEM((half + BLOCK, 2 * width), BF),
            ],
            us=2.0,
            smem=1,
            lazy=True,
            fetch=True,
        )
        norm_one[i], qkv_one[i], context_one[i], probs_one[i] = map(Far, saved)

        def finish(one, gate):
            after_self[i], norm_two[i] = forward_norm(one, own, gain_two, gate)
            return norm_two[i][0]

        return near, away, finish

    def cross_forward(i, gate):
        kinds = []
        if plain[i]:
            kinds.append(far((plain[i], heads, BLOCK, window)))
        if plain[i] < blocks:
            kinds.append(far((blocks - plain[i], heads, BLOCK, enc_length)))
        query, context, near, away, *saved = call(
            functools.partial(cross_forward_kernel, size, i),
            "cross_forward",
            [
                dec_lengths,
                enc_lengths,
                *norm_two[i],
                Far(weights_two),
                Far(after(keys["kv"], *gate)),
            ],
            [far((half, width)), far((half, width)), *parts, *kinds, far((half, features))],
            us=4.0,
            smem=2,
            raw=2,
            lazy=True,
        )
        query_two[i], context_two[i] = Far(query), Far(context)
        *probs_two[i], norms_two[i] = map(Far, saved)

        def finish(one, gate):
            second[i], norm_three[i] = forward_norm(one, after_self[i], gain_three, gate)
            return norm_three[i][0]

        return near, away, finish

    def feed_forward(i, gate):
        *saved, own, near, away, norms = call(
            functools.partial(ffn_kernel, i),
            "ffn",
            [*norm_three[i], *both_pieces, Far(after(weights_three, *gate))],
            [
                far((half, features)),
                far((half, units)),
                far((half, units)),
                (piece, BF),
                *parts,
                far((half, features)),
            ],
            [pltpu.VMEM((half, features), BF)],
            us=5.0,
            raw=2,
            lazy=True,
        )
        cot_half[i], hidden[i], active[i] = map(Far, saved)
        norms_three[i] = Far(norms)

        def finish(one, gate):
            grad_second[i], branch_two[i] = backward_pair(
                one, second[i], own, gain_three, gate
            )
            return branch_two[i][0]

        return near, away, finish

    def cross_backward(i, gate):
        last = i == order[-1]
        so_far = keys["grad"]
        grad_query_two[i], grad_kv, near, away, branch = call(
            functools.partial(
                cross_backward_kernel, size, i, len(probs_two[i]), len(so_far)
            ),
            "cross_backward",
            [
                dec_lengths,
                enc_lengths,
                *branch_two[i],
                weights_two,
                query_two[i],
                Far(after(keys["kv"], *gate)),
                *probs_two[i],
                *so_far,
            ],
            [
                ((half, width), BF),
                ((enc_length, 2 * width), BF) if last else ((2 * width, enc_length), F32),
                *parts,
                far((half, features)),
            ],
            [
                pltpu.VMEM((2 * width, enc_length), F32),
                pltpu.VMEM((half, width), BF),
            ],
            us=8.0,
            smem=2,
            raw=2,
            lazy=True,
            fetch=True,
        )
        keys["grad"] = [grad_kv]
        branches_two[i] = Far(branch)

        def finish(one, gate):
            grad_after_self[i], branch_one[i] = backward_pair(
                one, after_self[i], grad_second[i], gain_two, gate
            )
            return branch_one[i][0]

        return near, away, finish

    def self_backward(i, gate):
        first = Far(after(qkv_one[i].array, *gate))
        grad_qkv_one[i], acc, *edge, branch = call(
            functools.partial(self_backward_kernel, size, i),
            "self_backward",
            [
                *branch_one[i],
                weights_one,
                first,
                probs_one[i],
                qkv_one[0] if i else keys["edge"],
            ],
            [
                ((half, 3 * width), BF),
                ((heads, BLOCK, 2 * BLOCK), F32, "far"),
                *[((2 * width, BLOCK), F32)] * i,
                far((half, features)),
            ],
            [
                pltpu.VMEM((half + BLOCK, 2 * width), BF),
                pltpu.VMEM((2 * width, half + BLOCK), F32),
                pltpu.VMEM((half, width), BF),
            ],
            us=2.0,
            raw=2,
            lazy=True,
            fetch=True,
        )
        bias_acc[i], branches_one[i] = Far(acc), Far(branch)
        if edge:
            keys["edge"] = edge[0]
        return [grad_qkv_one[i]]

    def halves(left, right):
        return [(left[i], right[i]) for i in order]

    def make_keys(gate):
        keys["kv"], enc = call(
            functools.partial(cross_keys_kernel, width),
            "cross_keys",
            [*both_pieces, Far(after(weights_two, *gate))],
            [far((enc_length, 2 * width)), far((enc_length, features))],
            us=2.5,
            raw=4,
        )
        keys["enc"] = Far(enc)
        return keys["kv"]

    def ffn_weights(gate):
        held = {i: Far(after(hidden[i].array, *gate)) for i in order}
        blocks = weight_blocks(
            [halves(norms_three, active), halves(cot_half, held)], 2 * units, features, "ffn_weights"
        )
        keys["ffn"] = blocks
        return blocks[0]

    def layer_parts(gate):
        held = [hidden[0], Far(after(hidden[1].array, *gate))]
        layer = scatter_halves(held, weights_three, units, "layer_scatter")
        grads["layer"] = own_of(second) + sum(part.astype(F32) for part in layer)
        cross = scatter_rows_lower(after(keys["cross"][0], layer[0]), keys["cross"][1])
        grads["both"] = scatter_rows_upper(jnp.concatenate([grads["ffn"], cross], 2))
        return key_parts([layer[0]])

    def cross_weights(gate):
        grads["ffn"] = scatter_rows_lower(after(keys["ffn"][0], *gate), keys["ffn"][1])
        gate = gate + [grads["ffn"]]
        blocks = weight_blocks(
            [
                halves(norms_two, grad_query_two),
                [(keys["enc"], after(keys["grad"][0], *gate))],
                halves(branches_two, context_two),
            ],
            4 * width,
            features,
            "cross_weights",
        )
        keys["cross"] = blocks
        return blocks[0]

    def key_parts(gate):
        key_parts = call(
            functools.partial(scatter_keys_kernel, width),
            "scatter_keys",
            [after(keys["grad"][0], *gate), Far(weights_two)],
            [(piece, BF)] * 4,
            us=2.0,
        )
        across = send(chip_sum(key_parts[2], key_parts[3]), "heads", 2)
        grads["encoded"] = (
            key_parts[0].astype(F32)
            + send(key_parts[1], "heads", 1).astype(F32)
            + across.astype(F32)
        )
        return key_parts[0]

    keys = {"grad": [], "edge": []}
    grads = {}
    filler = {2: make_keys, 6: ffn_weights, 8: cross_weights, 9: layer_parts}
    stages = [self_forward, cross_forward, feed_forward, cross_backward, self_backward]
    gate, pending, step = [], None, 0
    for stage in stages:
        for i in order:
            result = stage(i, gate)
            gate = [result[0]]
            step += 1
            if step in filler:
                gate = [filler[step](gate)]
            if pending:
                gate = [pending[0](pending[1], gate)]
                pending = None
            if stage is self_backward:
                continue
            near, away, finish = result
            one = chip_sum(after(near, *gate), away)
            gate = [one]
            pending = (finish, one)
    input_parts = scatter_halves(grad_qkv_one, weights_one, 0, "input_scatter")
    bias_sums = call(
        functools.partial(bias_grad_kernel, starts),
        "bias_grad",
        [bias_acc[0], bias_acc[1]],
        [((heads, buckets, 2 * BLOCK), F32)],
        us=1.0,
    )[0]
    self_blocks = weight_blocks(
        [
            halves(norm_one, [after(grad_qkv_one[0], input_parts[0]), grad_qkv_one[1]]),
            halves(branches_one, context_one),
        ],
        4 * width,
        features,
        "self_weights",
        bias_sums,
    )
    (input_grad,) = backward_norm(
        input_parts,
        inputs,
        own_of(grad_after_self),
        gain_one,
        branch=False,
    )
    self_half = scatter_rows_lower(after(self_blocks[0], input_grad), self_blocks[1])
    self_got = scatter_rows_upper(after(self_half, grads["both"]))
    both_grad, self_grad = sum_rows(grads["both"]), sum_rows(self_got)
    bias_grad = self_grad[0, : heads * buckets].reshape(heads, buckets)
    self_grad = self_grad[SUM_ROWS:]
    ffn_grad, cross_grad = both_grad[:, : 2 * units], both_grad[:, 2 * units :]

    def along(weights, gradient):
        return jnp.sum(
            jnp.concatenate([w.astype(F32) for w in weights], 1) * gradient, axis=1
        )

    gain_grads = jnp.stack(
        [
            along([self_query, self_key, self_value], self_grad[:, : 3 * width]),
            along([cross_query], cross_grad[:, :width]),
            along([inner_weight], ffn_grad[:, :units]),
        ]
    )
    for bits in (1, 2):
        gain_grads = gain_grads + send(gain_grads, "heads", bits)
    gain_grads = lax.dynamic_slice_in_dim(gain_grads, me * each, each, 1) / jnp.stack(
        [gain_first, gain_second, gain_third]
    ).astype(F32)

    return (
        grads["layer"].astype(BF)[None],
        input_grad[None],
        grads["encoded"][None],
        self_grad[:, :width],
        self_grad[:, width : 2 * width],
        self_grad[:, 2 * width : 3 * width],
        self_grad[:, 3 * width :].T,
        cross_grad[:, :width],
        cross_grad[:, width : 2 * width],
        cross_grad[:, 2 * width : 3 * width],
        cross_grad[:, 3 * width :].T,
        ffn_grad[:, :units],
        ffn_grad[:, units:].T,
        bias_grad.T,
        gain_grads[0],
        gain_grads[1],
        gain_grads[2],
    )


def solution(mesh):
    positions = P("rows", "heads", None)
    columns = P("rows", "heads")
    lines = P("heads", "rows")
    gains = P(("rows", "heads"))
    return jax.shard_map(
        shards,
        mesh=mesh,
        in_specs=(
            positions,
            positions,
            positions,
            P("rows", None),
            P("rows", None),
            columns,
            columns,
            columns,
            lines,
            columns,
            columns,
            columns,
            lines,
            columns,
            lines,
            P(None, "heads"),
            gains,
            gains,
            gains,
        ),
        out_specs=(
            positions,
            positions,
            positions,
            columns,
            columns,
            columns,
            lines,
            columns,
            columns,
            columns,
            lines,
            columns,
            lines,
            P(None, "heads"),
            gains,
            gains,
            gains,
        ),
        check_vma=False,
    )
```
